128 devices in a mesh: mic: 16 (over z, y), mode: 8 (over x, core).
Axes of the slice: x: 4, y: 4, z: 4, core: 2. Of those that a mesh axis runs over, the one named last changes fastest.
Arguments:
- signal: bfloat16 [16, 4096, 4096], P('mic', 'mode'), may hold values from -6 to 6
- mic_axial: int32 [4096], P('mic'), may hold values from 0 to 63
- mic_azimuth: int32 [4096], P('mic'), may hold values from 0 to 511
- mode_m: int32 [8192], P('mode'), may hold values from -128 to 127
- mode_n: int32 [8192], P('mode'), may hold values from 0 to 31
- freq_bins: int32 [16], replicated, may hold values from 1 to 1023
Outputs:
- amplitude: float32 [16, 2, 16, 8192], P(None, None, None, 'mode')
- power: float32 [16, 8192], P(None, 'mode')
- residual: float32 [16, 2, 16, 4096], P('mode', None, None, 'mic')
The draws below stay inside these ranges and needn't reach their ends.
All inputs are finite; a program needn't handle non-finite values.
Results may differ from the reference program's by a relative error of at most 0.0051.
Values may be sent and summed in bfloat16 or wider, within the bound.
No kernel may reach another device: no remote copies, remote signals or barrier semaphores. Data moves between devices by JAX's collectives and lax.ppermute only.
A program may use at most 64 MiB of HBM per device.

```python
import math
import jax
import jax.numpy as jnp
from jax import lax

SEGLEN = 4096
FREQS = 16
MODES = 8192
ITERS = 2
AZIM = 512
AXIAL = 64
NRAD = 32
MICS = 4096
SEGS = 16


def plant(result, stream_key, smallest, largest):
    place = [jax.random.randint(jax.random.fold_in(stream_key, axis), (), 0, length) for axis, length in enumerate(result.shape)]
    main_axis = result.shape.index(max(result.shape))
    beside = place[:main_axis] + [(place[main_axis] + 1) % result.shape[main_axis]] + place[main_axis + 1:]
    return result.at[tuple(place)].set(smallest).at[tuple(beside)].set(largest)


def block_scale(rng, shape, pieces, low, high):
    def one(axis_at, parts):
        steps = jax.random.uniform(jax.random.fold_in(jax.random.fold_in(rng, 6), axis_at), (parts,), jnp.float32, low / len(pieces), high / len(pieces))
        return jnp.repeat(jnp.exp(steps), shape[axis_at] // parts).reshape((-1,) + (1,) * (len(shape) - axis_at - 1))

    loudness = one(*pieces[0])
    for cut in pieces[1:]:
        loudness = loudness * one(*cut)
    return loudness


def bell_draw(key, dims, spread, bound, pieces=(), kind=jnp.bfloat16):
    factor_of = block_scale(key, dims, pieces, -0.22, 0.18) if pieces else 1.0
    values = jax.random.normal(key, dims, jnp.float32) * spread * factor_of
    return jnp.minimum(jnp.maximum(values, -bound), bound).astype(kind)


def setup_inputs(seed: int = 0) -> dict:
    seeds = jax.random.split(jax.random.key(seed), 7)
    signal = bell_draw(seeds[0], (SEGS, MICS, SEGLEN), 1.0, 6.0, ((0, 16), (1, 8)))
    mic_axial = plant(jax.random.randint(seeds[1], (MICS,), 0, AXIAL), jax.random.fold_in(seeds[1], 1), 0, AXIAL - 1).astype(jnp.int32)
    mic_azimuth = plant(jax.random.randint(seeds[2], (MICS,), 0, AZIM), jax.random.fold_in(seeds[2], 1), 0, AZIM - 1).astype(jnp.int32)
    mode_m = plant(jax.random.randint(seeds[3], (MODES,), -128, 128), jax.random.fold_in(seeds[3], 1), -128, 127).astype(jnp.int32)
    mode_n = plant(jax.random.randint(seeds[4], (MODES,), 0, NRAD), jax.random.fold_in(seeds[4], 1), 0, NRAD - 1).astype(jnp.int32)
    freq_bins = plant(jax.random.randint(seeds[5], (FREQS,), 1, SEGLEN // 4), jax.random.fold_in(seeds[5], 1), 1, (SEGLEN // 4) - 1).astype(jnp.int32)
    return dict(signal=signal, mic_axial=mic_axial, mic_azimuth=mic_azimuth, mode_m=mode_m, mode_n=mode_n, freq_bins=freq_bins)


EPS = 1e-06

def analysis_rows(freq_bins, seglen):
    sample_index = jnp.arange(seglen, dtype=jnp.int32)
    phase_turns = jnp.mod(freq_bins[:, None] * sample_index[None, :], seglen)
    phase_angle = phase_turns.astype(jnp.float32) * (2.0 * math.pi / seglen)
    window = 0.5 - 0.5 * jnp.cos(sample_index.astype(jnp.float32) * (2.0 * math.pi / seglen))
    norm_scale = (3.0 * seglen / 8.0) ** (-0.5)
    cosine = window[None, :] * jnp.cos(phase_angle) * norm_scale
    sine = -window[None, :] * jnp.sin(phase_angle) * norm_scale
    stacked = jnp.stack([cosine, sine], axis=1)
    return stacked.reshape(2 * freq_bins.shape[0], seglen).astype(jnp.bfloat16)

def mode_tile(bin_value, mic_axial, mic_azimuth, mode_m, mode_n, norm_scale):
    period = AZIM * AXIAL
    phase_turns = jnp.mod(mic_azimuth[:, None] * (mode_m * AXIAL)[None, :] + mic_axial[:, None] * (bin_value * (2 * NRAD - mode_n))[None, :], period)
    phase_angle = phase_turns.astype(jnp.float32) * (2.0 * math.pi / period)
    weight = norm_scale / jnp.sqrt(1.0 + mode_n.astype(jnp.float32))
    real_part = (weight[None, :] * jnp.cos(phase_angle)).astype(jnp.bfloat16)
    imag_part = (weight[None, :] * jnp.sin(phase_angle)).astype(jnp.bfloat16)
    return (real_part, imag_part)

def forward_product(real_part, imag_part, vector):
    segs = vector.shape[1]
    stacked = vector.reshape(2 * segs, vector.shape[2]).astype(jnp.bfloat16)
    first = jnp.dot(stacked, real_part.T, preferred_element_type=jnp.float32)
    second = jnp.dot(stacked, imag_part.T, preferred_element_type=jnp.float32)
    return jnp.stack([first[:segs] - second[segs:], first[segs:] + second[:segs]])

def adjoint_product(real_part, imag_part, vector):
    segs = vector.shape[1]
    stacked = vector.reshape(2 * segs, vector.shape[2]).astype(jnp.bfloat16)
    first = jnp.dot(stacked, real_part, preferred_element_type=jnp.float32)
    second = jnp.dot(stacked, imag_part, preferred_element_type=jnp.float32)
    return jnp.stack([first[:segs] + second[segs:], first[segs:] - second[:segs]])

def reference(signal, mic_axial, mic_azimuth, mode_m, mode_n, freq_bins):
    analysis = analysis_rows(freq_bins, SEGLEN)

    def transform(segment):
        return jnp.dot(analysis, segment.T, preferred_element_type=jnp.float32)
    spectra = lax.map(transform, signal)
    rhs = spectra.reshape(SEGS, FREQS, 2, MICS).transpose(1, 2, 0, 3)
    norm_scale = MICS ** (-0.5)

    def solve(item):
        bin_value, right_side = item
        real_part, imag_part = mode_tile(bin_value, mic_axial, mic_azimuth, mode_m, mode_n, norm_scale)
        residual = right_side
        gradient = adjoint_product(real_part, imag_part, residual)
        grad_norm = lax.optimization_barrier(jnp.sum(gradient * gradient, axis=(0, 2)))
        direction = gradient
        amplitude = jnp.zeros_like(direction)
        for sweep in range(ITERS):
            image = forward_product(real_part, imag_part, direction)
            image_norm = lax.optimization_barrier(jnp.sum(image * image, axis=(0, 2)))
            step_size = grad_norm / (image_norm + EPS)
            amplitude = amplitude + step_size[None, :, None] * direction
            residual = residual - step_size[None, :, None] * image
            if sweep + 1 < ITERS:
                gradient = adjoint_product(real_part, imag_part, residual)
                next_norm = lax.optimization_barrier(jnp.sum(gradient * gradient, axis=(0, 2)))
                direction = gradient + (next_norm / (grad_norm + EPS))[None, :, None] * direction
                grad_norm = next_norm
        return (amplitude, residual)
    amplitude, residual = lax.map(solve, (freq_bins, rhs))
    power = lax.optimization_barrier(jnp.mean(lax.optimization_barrier(jnp.sum(amplitude * amplitude, axis=1)), axis=1))
    return (amplitude, power, residual)
```

```python
import math

import jax
import jax.numpy as jnp
from jax import lax
from jax.experimental import pallas as pl
from jax.experimental.pallas import tpu as pltpu
from jax.sharding import PartitionSpec as P

ITERS = 2
AZIM = 512
AXIAL = 64
NRAD = 32
ORDERS = 256
EPS = 1e-06
SIN_COEFS = (1.5707963200919937, -0.6459637612912833, 0.07968992686556589, -0.0046741574942986315, 0.0001516785309118288)
BF16 = jnp.bfloat16
F32 = jnp.float32


def cos_turns(phase, bits):
    half = 1 << (bits - 1)
    quarter = 1 << (bits - 2)
    centred = ((phase + half) & (2 * half - 1)) - half
    y = (quarter - jnp.abs(centred)).astype(F32) * (1.0 / quarter)
    square = y * y
    total = jnp.full_like(y, SIN_COEFS[-1])
    for coef in SIN_COEFS[-2::-1]:
        total = total * square + coef
    return total * y


def sin_turns(phase, bits):
    return cos_turns(phase - (1 << (bits - 2)), bits)


def iota(shape, axis):
    return lax.broadcasted_iota(jnp.int32, shape, axis)


def nt_dot(a, b):
    return lax.dot_general(a, b, (((1,), (1,)), ((), ())), preferred_element_type=F32)


def spectra_kernel(freq_ref, m_lo_ref, m_hi_ref, n_lo_ref, n_hi_ref, signal_ref, out_ref, analysis_ref):
    rows, seglen = analysis_ref.shape
    freqs = rows // 2

    @pl.when(pl.program_id(0) == 0)
    def _():
        row = iota((rows, 128), 0)
        column = jnp.zeros((rows, 128), jnp.int32)
        for f in range(freqs):
            column = jnp.where((row >> 1) == f, freq_ref[f], column)
        quarter = (row & 1) * (seglen // 4)
        bits = seglen.bit_length() - 1
        scale = (3.0 * seglen / 8.0) ** (-0.5)
        for block in range(seglen // 128):
            sample = iota((rows, 128), 1) + block * 128
            wave = cos_turns(column * sample + quarter, bits)
            window = 0.5 - 0.5 * cos_turns(iota((8, 128), 1) + block * 128, bits)[:1]
            analysis_ref[:, block * 128 : (block + 1) * 128] = (window * wave * scale).astype(BF16)

    spectra = nt_dot(analysis_ref[...], signal_ref[...])
    per = rows // out_ref.shape[0]
    for d in range(out_ref.shape[0]):
        out_ref[d, 0:per, :] = spectra[d * per : (d + 1) * per]
    codes = []
    for m_ref, n_ref in ((m_lo_ref, n_lo_ref), (m_hi_ref, n_hi_ref)):
        m = m_ref[...]
        codes.append((jnp.where(m >= 0, m, ORDERS // 2 - 1 - m) * NRAD + n_ref[...]).astype(F32))
    for d in range(out_ref.shape[0]):
        out_ref[d, per : per + 1, :] = codes[0]
        out_ref[d, per + 1 : per + 2, :] = codes[1]
        out_ref[d, per + 2 :, :] = jnp.zeros((out_ref.shape[1] - per - 2, 128), F32)


def spectra_call(freq_bins, mode_m, mode_n, signal, dests):
    mics, seglen = signal.shape
    rows = 2 * freq_bins.shape[0]
    steps = mics // 128
    lo = pl.BlockSpec((1, 128), lambda i: (0, i))
    hi = pl.BlockSpec((1, 128), lambda i: (0, steps + i))
    m_row, n_row = mode_m.reshape(1, -1), mode_n.reshape(1, -1)
    return pl.pallas_call(
        spectra_kernel,
        grid=(steps,),
        in_specs=[
            pl.BlockSpec(memory_space=pltpu.SMEM),
            lo,
            hi,
            lo,
            hi,
            pl.BlockSpec((128, seglen), lambda i: (i, 0)),
        ],
        out_specs=pl.BlockSpec((dests, 8, 128), lambda i: (0, 0, i)),
        out_shape=jax.ShapeDtypeStruct((dests, 8, mics), F32),
        scratch_shapes=[pltpu.VMEM((rows, seglen), BF16)],
        name="spectra",
        cost_estimate=pl.CostEstimate(flops=2 * rows * mics * seglen, bytes_accessed=mics * seglen * 2, transcendentals=0),
    )(freq_bins, m_row, m_row, n_row, n_row, signal)


def basis_kernel(freq_ref, code_ref, azim_ref, radial_ref):
    half = ORDERS // 2
    for b in range(code_ref.shape[0]):
        lanes = code_ref.shape[2]
        at = pl.ds(b * lanes, lanes)
        code = code_ref[b]
        azimuth = code >> 6
        axial = code & 63
        fine_phase = azimuth * (2 * iota((8, lanes), 0) + 1)
        fine_cos, fine_sin = cos_turns(fine_phase, 10), sin_turns(fine_phase, 10)
        coarse_phase = azimuth * (8 * iota((half // 8, lanes), 0))
        coarse_cos, coarse_sin = cos_turns(coarse_phase, 9), sin_turns(coarse_phase, 9)
        cos_rows, sin_rows = [], []
        for a in range(half // 8):
            cc, cs = coarse_cos[a : a + 1], coarse_sin[a : a + 1]
            cos_rows.append(cc * fine_cos - cs * fine_sin)
            sin_rows.append(cs * fine_cos + cc * fine_sin)
        azim_ref[0, 0:half, at] = jnp.concatenate(cos_rows, axis=0).astype(BF16)
        azim_ref[0, half:, at] = jnp.concatenate(sin_rows, axis=0).astype(BF16)
        for fl in range(radial_ref.shape[1]):
            turns = axial * freq_ref[fl]
            phase = turns * (2 * NRAD - iota((NRAD, lanes), 0)) - azimuth * 32
            radial_ref[0, fl, 0, :, at] = cos_turns(phase, 15)
            radial_ref[0, fl, 1, :, at] = sin_turns(phase, 15)


def basis_call(own_bins, codes, chunks):
    blocks, _, lanes = codes.shape
    mics = blocks * lanes
    per = mics // chunks
    own = own_bins.shape[0]
    return pl.pallas_call(
        basis_kernel,
        grid=(chunks,),
        in_specs=[
            pl.BlockSpec(memory_space=pltpu.SMEM),
            pl.BlockSpec((blocks // chunks, 1, lanes), lambda i: (i, 0, 0)),
        ],
        out_specs=[
            pl.BlockSpec((1, ORDERS, per), lambda i: (i, 0, 0)),
            pl.BlockSpec((1, own, 2, NRAD, per), lambda i: (i, 0, 0, 0, 0)),
        ],
        out_shape=[
            jax.ShapeDtypeStruct((chunks, ORDERS, per), BF16),
            jax.ShapeDtypeStruct((chunks, own, 2, NRAD, per), F32),
        ],
        name="basis",
        cost_estimate=pl.CostEstimate(flops=40 * ORDERS * mics, bytes_accessed=6 * ORDERS * mics, transcendentals=0),
    )(own_bins, codes)


def solve_kernel(recv_ref, azim_ref, radial_ref, amp_ref, res_out_ref, onehot_ref, radmask_ref, res_ref, image_ref, acc_ref, rows_ref):
    chunks, _, per = azim_ref.shape
    own = radial_ref.shape[1]
    half = ORDERS // 2
    group = 2 * NRAD
    mics = chunks * per

    acc_ref[0:NRAD, :] = jnp.zeros((NRAD, ORDERS), F32)

    @pl.loop(0, chunks)
    def _(ch):
        for part in range(2):
            code = recv_ref[ch, 2 * own + part : 2 * own + part + 1, :].astype(jnp.int32)
            at = pl.ds(part * per, per)
            onehot_ref[ch, :, at] = jnp.where(iota((ORDERS, per), 0) == (code >> 5), 1.0, 0.0).astype(BF16)
            radmask_ref[ch, :, at] = jnp.where(iota((NRAD, per), 0) == (code & 31), 1.0, 0.0)
        acc_ref[0:NRAD, :] += nt_dot(radmask_ref[ch].astype(BF16), onehot_ref[ch])

    counts = acc_ref[0:NRAD, :]
    n_column = iota((NRAD, ORDERS), 0).astype(F32)
    weight = (mics ** (-0.5)) * lax.rsqrt(1.0 + n_column)
    counts_weight = counts * weight

    def adjoint(update):
        acc_ref[...] = jnp.zeros(acc_ref.shape, F32)

        @pl.loop(0, chunks)
        def _(ch):
            rows = []
            for fl in range(own):
                re = update(ch, 2 * fl)
                im = update(ch, 2 * fl + 1)
                ec, es = radial_ref[ch, fl, 0], radial_ref[ch, fl, 1]
                rows.append((re * ec + im * es).astype(BF16))
                rows.append((im * ec - re * es).astype(BF16))
            acc_ref[...] += nt_dot(jnp.concatenate(rows, axis=0), azim_ref[ch])

        gradients = []
        for fl in range(own):
            re = acc_ref[fl * group : fl * group + NRAD, :]
            im = acc_ref[fl * group + NRAD : (fl + 1) * group, :]
            rc, rs, ic, isn = re[:, :half], re[:, half:], im[:, :half], im[:, half:]
            g_re = jnp.concatenate([rc + isn, rc - isn], axis=1) * weight
            g_im = jnp.concatenate([ic - rs, ic + rs], axis=1) * weight
            gradients.append((g_re, g_im))
        norms = [total(counts * (g[0] * g[0] + g[1] * g[1])) for g in gradients]
        return gradients, norms

    def total(x):
        return jnp.sum(jnp.sum(x, axis=0, keepdims=True), axis=1, keepdims=True)

    def forward(directions):
        stacked = []
        for d_re, d_im in directions:
            x_re, x_im = d_re * counts_weight, d_im * counts_weight
            p_re, m_re, p_im, m_im = x_re[:, :half], x_re[:, half:], x_im[:, :half], x_im[:, half:]
            stacked.append(jnp.concatenate([p_re + m_re, m_im - p_im], axis=1))
            stacked.append(jnp.concatenate([p_im + m_im, p_re - m_re], axis=1))
        rows_ref[...] = jnp.concatenate(stacked, axis=0).astype(BF16)

        def step(ch, norms):
            fields = jnp.dot(rows_ref[...], azim_ref[ch], preferred_element_type=F32)
            out = []
            for fl in range(own):
                t_re = fields[fl * group : fl * group + NRAD]
                t_im = fields[fl * group + NRAD : (fl + 1) * group]
                ec, es = radial_ref[ch, fl, 0], radial_ref[ch, fl, 1]
                i_re = jnp.sum(ec * t_re - es * t_im, axis=0, keepdims=True)
                i_im = jnp.sum(ec * t_im + es * t_re, axis=0, keepdims=True)
                image_ref[ch, 2 * fl : 2 * fl + 1, :] = i_re
                image_ref[ch, 2 * fl + 1 : 2 * fl + 2, :] = i_im
                out.append(norms[fl] + i_re * i_re + i_im * i_im)
            return tuple(out)

        sums = lax.fori_loop(0, chunks, step, tuple(jnp.zeros((1, per), F32) for _ in range(own)))
        return [jnp.sum(s, axis=1, keepdims=True) for s in sums]

    def first(ch, row):
        value = recv_ref[ch, row : row + 1, :]
        res_ref[ch, row : row + 1, :] = value
        return value

    gradients, norms = adjoint(first)
    directions = gradients
    amplitude = None
    for sweep in range(ITERS):
        image_norms = forward(directions)
        steps = [g / (i + EPS) for g, i in zip(norms, image_norms)]
        grown = [(s * d[0], s * d[1]) for s, d in zip(steps, directions)]
        if amplitude is None:
            amplitude = grown
        else:
            amplitude = [(a[0] + g[0], a[1] + g[1]) for a, g in zip(amplitude, grown)]

        def advance(ch, row, steps=steps):
            value = res_ref[ch, row : row + 1, :] - steps[row // 2] * image_ref[ch, row : row + 1, :]
            res_ref[ch, row : row + 1, :] = value
            return value

        if sweep + 1 < ITERS:
            gradients, next_norms = adjoint(advance)
            momenta = [a / (b + EPS) for a, b in zip(next_norms, norms)]
            directions = [(g[0] + q * d[0], g[1] + q * d[1]) for g, q, d in zip(gradients, momenta, directions)]
            norms = next_norms

    blocks, _, width = res_out_ref.shape
    pieces = blocks // chunks
    for ch in range(chunks):
        for row in range(2 * own):
            value = advance(ch, row)
            for piece in range(pieces):
                res_out_ref[ch * pieces + piece, row : row + 1, :] = value[:, piece * width : (piece + 1) * width]

    rows_ref[...] = jnp.concatenate([part for a in amplitude for part in a], axis=0).astype(BF16)
    copies = amp_ref.shape[0]

    @pl.loop(0, chunks)
    def _(ch):
        for part in range(2):
            at = pl.ds(part * per, per)
            picked = jnp.dot(rows_ref[...], onehot_ref[ch, :, at], preferred_element_type=F32)
            mask = radmask_ref[ch, :, at]
            for row in range(2 * own):
                value = jnp.sum(picked[row * NRAD : (row + 1) * NRAD] * mask, axis=0, keepdims=True)
                for q in range(per // 128):
                    kc = part * (per // 128) + q
                    acc_ref[kc * 2 * own + row : kc * 2 * own + row + 1, 0:128] = value[:, q * 128 : (q + 1) * 128]
        packed = acc_ref[0 : amp_ref.shape[2], 0:128].astype(BF16)
        for copy in range(copies):
            amp_ref[copy, ch] = packed


def solve_call(recv, azim, radial, copies, own):
    chunks, _, per = azim.shape
    modes = 2 * per * chunks
    vmem = pl.BlockSpec(memory_space=pltpu.VMEM)
    return pl.pallas_call(
        solve_kernel,
        in_specs=[vmem] * 3,
        out_specs=[vmem] * 2,
        out_shape=[
            jax.ShapeDtypeStruct((copies, chunks, 2 * own * modes // chunks // 128, 128), BF16),
            jax.ShapeDtypeStruct((copies, 2 * own, chunks * per // copies), F32),
        ],
        scratch_shapes=[
            pltpu.VMEM((chunks, ORDERS, 2 * per), BF16),
            pltpu.VMEM((chunks, NRAD, 2 * per), F32),
            pltpu.VMEM((chunks, 2 * own, per), F32),
            pltpu.VMEM((chunks, 2 * own, per), F32),
            pltpu.VMEM((2 * own * NRAD, ORDERS), F32),
            pltpu.VMEM((2 * own * NRAD, ORDERS), BF16),
        ],
        compiler_params=pltpu.CompilerParams(vmem_limit_bytes=40 << 20),
        name="solve",
        cost_estimate=pl.CostEstimate(flops=10 * 256 * 4096 * 128, bytes_accessed=8 << 20, transcendentals=0),
    )(recv, azim, radial)


def expand_kernel(in_ref, amp_ref, pow_ref, wide_ref):
    segs, dests, lines, _ = in_ref.shape
    rows = amp_ref.shape[0] // dests
    wide_ref[...] = in_ref[...].astype(F32).reshape(wide_ref.shape)
    for d in range(dests):
        for kc in range(lines // rows):
            power = []
            for row in range(rows):
                value = wide_ref[pl.ds(d * lines + kc * rows + row, segs, stride=dests * lines), :]
                amp_ref[d * rows + row, :, kc * 128 : (kc + 1) * 128] = value
                power.append(jnp.sum(value * value, axis=0, keepdims=True))
            for fl in range(rows // 2):
                at = d * (rows // 2) + fl
                pow_ref[at : at + 1, kc * 128 : (kc + 1) * 128] = (power[2 * fl] + power[2 * fl + 1]) * (1.0 / segs)


def expand_call(recv, rows, splits):
    segs, dests, lines, _ = recv.shape
    modes = lines // rows * 128
    here = dests // splits
    return pl.pallas_call(
        expand_kernel,
        grid=(splits,),
        in_specs=[pl.BlockSpec((segs, here, lines, 128), lambda i: (0, i, 0, 0))],
        out_specs=[
            pl.BlockSpec((here * rows, segs, modes), lambda i: (i, 0, 0)),
            pl.BlockSpec((here * rows // 2, modes), lambda i: (i, 0)),
        ],
        out_shape=[
            jax.ShapeDtypeStruct((dests * rows, segs, modes), F32),
            jax.ShapeDtypeStruct((dests * rows // 2, modes), F32),
        ],
        scratch_shapes=[pltpu.VMEM((segs * here * lines, 128), F32)],
        name="expand",
        cost_estimate=pl.CostEstimate(flops=1 << 21, bytes_accessed=3 << 20, transcendentals=0),
    )(recv)


def turn_kernel(in_ref, out_ref):
    for row in range(out_ref.shape[0]):
        out_ref[row] = in_ref[:, row, :]


def turn_call(recv):
    segs, rows, width = recv.shape
    vmem = pl.BlockSpec(memory_space=pltpu.VMEM)
    return pl.pallas_call(
        turn_kernel,
        in_specs=[vmem],
        out_specs=vmem,
        out_shape=jax.ShapeDtypeStruct((rows, segs, width), F32),
        name="turn",
        cost_estimate=pl.CostEstimate(flops=0, bytes_accessed=1 << 17, transcendentals=0),
    )(recv)


def on_device(signal, mic_axial, mic_azimuth, mode_m, mode_n, freq_bins):
    segs = lax.axis_size("mic")
    owners = lax.axis_size("mode")
    freqs = freq_bins.shape[0]
    own = freqs // owners
    code = mic_azimuth * AXIAL + mic_axial
    codes = lax.all_to_all(jnp.broadcast_to(code[None, None, :], (segs, 1, code.shape[0])), "mic", 0, 0, tiled=True)
    spectra = spectra_call(freq_bins, mode_m, mode_n, signal[0], owners)
    recv = lax.all_to_all(spectra, "mode", 0, 0, tiled=True)
    own_bins = lax.dynamic_slice_in_dim(freq_bins, lax.axis_index("mode") * own, own, 0)
    azim, radial = basis_call(own_bins, codes, owners)
    amp, res = solve_call(recv, azim, radial, segs, own)
    residual = turn_call(lax.all_to_all(res, "mic", 0, 0, tiled=True))
    shape = amp.shape
    amp = lax.all_to_all(amp.reshape(segs * owners, *shape[2:]), ("mic", "mode"), 0, 0, tiled=True)
    amplitude, power = expand_call(amp.reshape(shape), 2 * own, 2)
    modes = mode_m.shape[0]
    return (
        amplitude.reshape(freqs, 2, segs, modes),
        power,
        residual.reshape(own, 2, segs, residual.shape[2]),
    )


def solution(mesh):
    in_specs = (P("mic", "mode", None), P("mic"), P("mic"), P("mode"), P("mode"), P())
    out_specs = (P(None, None, None, "mode"), P(None, "mode"), P("mode", None, None, "mic"))
    return jax.shard_map(
        on_device, mesh=mesh, in_specs=in_specs, out_specs=out_specs, check_vma=False
    )
```

```python
import jax
import jax.numpy as jnp
from jax import lax
from jax.experimental import pallas as pl
from jax.experimental.pallas import tpu as pltpu
from jax.sharding import PartitionSpec as P

ITERS = 2
AXIAL = 64
NRAD = 32
ORDERS = 256
HALF = ORDERS // 2
EPS = 1e-06
SIN_COEFS = (1.5707963200919937, -0.6459637612912833, 0.07968992686556589, -0.0046741574942986315, 0.0001516785309118288)
BF16 = jnp.bfloat16
F32 = jnp.float32
VMEM = pl.BlockSpec(memory_space=pltpu.VMEM)
SMEM = pl.BlockSpec(memory_space=pltpu.SMEM)


def cos_turns(turns):
    z = 1.0 - 4.0 * jnp.abs(turns - jnp.round(turns))
    square = z * z
    total = SIN_COEFS[-1] * square + SIN_COEFS[-2]
    for coef in SIN_COEFS[-3::-1]:
        total = total * square + coef
    return total * z


def sin_turns(turns):
    return cos_turns(turns - 0.25)


def turn_by(re, im, step_re, step_im):
    return re * step_re - im * step_im, re * step_im + im * step_re


def iota(shape, axis):
    return lax.broadcasted_iota(jnp.int32, shape, axis)


def nt_dot(a, b):
    return lax.dot_general(a, b, (((1,), (1,)), ((), ())), preferred_element_type=F32)


def groups(x):
    return x.reshape(x.shape[0] // 8, 8, x.shape[1])


def periodic(x):
    x = x + pltpu.roll(x, 4, 0)
    return x + pltpu.roll(x, 2, 0)


def analysis_kernel(freq_ref, out_ref):
    rows, seglen = out_ref.shape
    freqs = rows // 2
    row = iota((freqs, 128), 0)
    freq = jnp.zeros((freqs, 128), jnp.int32)
    for f in range(freqs):
        freq = jnp.where(row == f, freq_ref[f], freq)
    freq = freq.astype(F32)
    lane = iota((freqs, 128), 1).astype(F32)
    start = freq * lane * (1.0 / seglen)
    step = freq * (128.0 / seglen)
    re, im = cos_turns(start), -sin_turns(start)
    step_re, step_im = cos_turns(step), -sin_turns(step)
    scale = (3.0 * seglen / 8.0) ** (-0.5)
    for block in range(seglen // 128):
        sample = iota((8, 128), 1).astype(F32) + block * 128.0
        window = (0.5 - 0.5 * cos_turns(sample * (1.0 / seglen)))[None] * scale
        at = slice(block * 128, (block + 1) * 128)
        out_ref[0:freqs, at] = (groups(re) * window).reshape(freqs, 128).astype(BF16)
        out_ref[freqs:, at] = (groups(im) * window).reshape(freqs, 128).astype(BF16)
        re, im = turn_by(re, im, step_re, step_im)


def analysis_call(freq_bins, seglen):
    return pl.pallas_call(
        analysis_kernel,
        in_specs=[SMEM],
        out_specs=VMEM,
        out_shape=jax.ShapeDtypeStruct((2 * freq_bins.shape[0], seglen), BF16),
        name="analysis",
        cost_estimate=pl.CostEstimate(flops=1 << 21, bytes_accessed=1 << 18, transcendentals=0),
    )(freq_bins)


def spectra_kernel(analysis_ref, m_lo_ref, m_hi_ref, n_lo_ref, n_hi_ref, first_ref, second_ref, signal_ref, out_ref):
    dests = out_ref.shape[0]
    freqs = analysis_ref.shape[0] // 2
    own = freqs // dests
    step = pl.program_id(0)
    spectra = nt_dot(analysis_ref[...], signal_ref[...])
    codes = []
    for m_ref, n_ref in ((m_lo_ref, n_lo_ref), (m_hi_ref, n_hi_ref)):
        m = m_ref[...]
        codes.append((jnp.where(m >= 0, m, HALF - 1 - m) * NRAD + n_ref[...]).astype(F32))
    straight = (lax.axis_index("mic") < dests) == (step < pl.num_programs(0) // 2)
    codes.append(jnp.where(straight, first_ref[...], second_ref[...]).astype(F32))
    codes.append(jnp.zeros_like(codes[0]))
    tail = jnp.concatenate(codes, axis=0)
    for d in range(dests):
        out_ref[d, 0:own, :] = spectra[d * own : (d + 1) * own]
        out_ref[d, own : 2 * own, :] = spectra[freqs + d * own : freqs + (d + 1) * own]
        out_ref[d, 2 * own :, :] = tail


def spectra_call(analysis, mode_m, mode_n, first, second, signal, dests):
    mics, seglen = signal.shape
    rows = analysis.shape[0]
    steps = mics // 128
    lo = pl.BlockSpec((1, 128), lambda i: (0, i))
    hi = pl.BlockSpec((1, 128), lambda i: (0, steps + i))
    code = pl.BlockSpec((1, 128), lambda i: (0, i % (steps // 2)))
    m_row, n_row = mode_m.reshape(1, -1), mode_n.reshape(1, -1)
    return pl.pallas_call(
        spectra_kernel,
        grid=(steps,),
        in_specs=[VMEM, lo, hi, lo, hi, code, code, pl.BlockSpec((128, seglen), lambda i: (i, 0))],
        out_specs=pl.BlockSpec((dests, 8, 128), lambda i: (0, 0, i)),
        out_shape=jax.ShapeDtypeStruct((dests, 8, mics), F32),
        name="spectra",
        cost_estimate=pl.CostEstimate(flops=2 * rows * mics * seglen, bytes_accessed=mics * seglen * 2, transcendentals=0),
    )(analysis, m_row, m_row, n_row, n_row, first.reshape(1, -1), second.reshape(1, -1), signal)


def solve_kernel(
    freq_ref, recv_ref, out_ref, azim_ref, rad_ref, res_ref, image_ref, field_ref, onehot_ref, radhot_ref, dir_ref, grown_ref, rows_ref
):
    chunks, _, per = recv_ref.shape
    mics = chunks * per
    stack = 2 * NRAD
    base = 2 * lax.axis_index("mode")
    odd = (iota((8, per), 0) & 1) == 1
    freq = jnp.where(odd, freq_ref[base + 1], freq_ref[base]).astype(F32)
    row = iota((8, per), 0).astype(F32)
    radial = (iota((8, per), 0) >> 1).astype(F32)

    @pl.loop(0, chunks)
    def _(ch):
        at = pl.ds(pl.multiple_of(ch * per, per), per)
        code = jnp.broadcast_to(recv_ref[ch, 6:7, :], (8, per))
        azimuth = jnp.floor(code * (1.0 / AXIAL))
        axial = code - azimuth * AXIAL
        turns = azimuth * (row + 0.5) * (1.0 / 512)
        re, im = cos_turns(turns), sin_turns(turns)
        turns = azimuth * (8.0 / 512)
        step_re, step_im = cos_turns(turns), sin_turns(turns)
        next_re, next_im = turn_by(re, im, step_re, step_im)
        step_re, step_im = turn_by(step_re, step_im, step_re, step_im)
        re = jnp.stack([re, next_re])
        im = jnp.stack([im, next_im])
        for a in range(HALF // 16):
            azim_ref[16 * a : 16 * a + 16, at] = re.reshape(16, per).astype(BF16)
            azim_ref[HALF + 16 * a : HALF + 16 * a + 16, at] = im.reshape(16, per).astype(BF16)
            if a + 1 < HALF // 16:
                re, im = turn_by(re, im, step_re[None], step_im[None])
        turns = (axial * freq * (2.0 * NRAD - radial) - azimuth * 32.0) * (1.0 / 32768)
        re, im = cos_turns(turns), sin_turns(turns)
        turns = axial * freq * (-4.0 / 32768)
        step_re, step_im = cos_turns(turns), sin_turns(turns)
        for a in range(stack // 8):
            rad_ref[0, 8 * a : 8 * a + 8, at] = re
            rad_ref[1, 8 * a : 8 * a + 8, at] = im
            if a + 1 < stack // 8:
                re, im = turn_by(re, im, step_re, step_im)
        for c in range(2):
            res_ref[c, :, at] = jnp.where(odd, recv_ref[ch, 2 * c + 1 : 2 * c + 2, :], recv_ref[ch, 2 * c : 2 * c + 1, :])

    order_rows = iota((ORDERS, 128), 0).astype(F32).astype(BF16)
    radial_rows = (iota((stack, 128), 0) >> 1).astype(F32).astype(BF16)
    one, zero = jnp.ones((), BF16), jnp.zeros((), BF16)

    @pl.loop(0, chunks)
    def _(ch):
        for part in range(2):
            code = recv_ref[ch, 4 + part : 5 + part, :]
            order = jnp.floor(code * (1.0 / NRAD))
            radius = (code - order * NRAD).astype(BF16)
            order = order.astype(BF16)
            for q in range(per // 128):
                at = pl.ds(pl.multiple_of(ch * 2 * per + part * per + q * 128, 128), 128)
                lanes = slice(q * 128, (q + 1) * 128)
                onehot_ref[:, at] = jnp.where(order_rows == order[:, lanes], one, zero)
                radhot_ref[:, at] = jnp.where(radial_rows == radius[:, lanes], one, zero)

    counts = nt_dot(radhot_ref[...], onehot_ref[...])
    weight = (mics ** (-0.5)) * lax.rsqrt(1.0 + (iota((stack, ORDERS), 0) >> 1).astype(F32))
    counts_weight = counts * weight

    def scaled(column, x):
        return (column[None] * groups(x)).reshape(x.shape)

    def row_sums(x):
        return periodic(jnp.sum(jnp.sum(groups(x), axis=0), axis=1, keepdims=True))

    def adjoint(advance):
        for ch in range(chunks):
            at = slice(ch * per, (ch + 1) * per)
            re, im = advance(0, at)[None], advance(1, at)[None]
            ec, es = groups(rad_ref[0, :, at]), groups(rad_ref[1, :, at])
            field_ref[0:stack, at] = (re * ec + im * es).reshape(stack, per).astype(BF16)
            field_ref[stack:, at] = (im * ec - re * es).reshape(stack, per).astype(BF16)
        out = nt_dot(field_ref[...], azim_ref[...])
        re, im = out[:stack], out[stack:]
        rc, rs, ic, ics = re[:, :HALF], re[:, HALF:], im[:, :HALF], im[:, HALF:]
        g_re = jnp.concatenate([rc + ics, rc - ics], axis=1) * weight
        g_im = jnp.concatenate([ic - rs, ic + rs], axis=1) * weight
        return g_re, g_im, row_sums(counts * (g_re * g_re + g_im * g_im))

    def forward():
        x_re, x_im = dir_ref[0] * counts_weight, dir_ref[1] * counts_weight
        p_re, m_re, p_im, m_im = x_re[:, :HALF], x_re[:, HALF:], x_im[:, :HALF], x_im[:, HALF:]
        rows_ref[0:stack] = jnp.concatenate([p_re + m_re, m_im - p_im], axis=1).astype(BF16)
        rows_ref[stack:] = jnp.concatenate([p_im + m_im, p_re - m_re], axis=1).astype(BF16)
        norm = jnp.zeros((8, per), F32)
        for ch in range(chunks):
            at = slice(ch * per, (ch + 1) * per)
            out = jnp.dot(rows_ref[...], azim_ref[:, at], preferred_element_type=F32)
            t_re, t_im = out[:stack], out[stack:]
            ec, es = rad_ref[0, :, at], rad_ref[1, :, at]
            i_re = periodic(jnp.sum(groups(ec * t_re - es * t_im), axis=0))
            i_im = periodic(jnp.sum(groups(ec * t_im + es * t_re), axis=0))
            image_ref[0, :, at] = i_re
            image_ref[1, :, at] = i_im
            norm = norm + (i_re * i_re + i_im * i_im)
        return jnp.sum(norm, axis=1, keepdims=True)

    g_re, g_im, norm = adjoint(lambda c, at: res_ref[c, :, at])
    dir_ref[0] = g_re
    dir_ref[1] = g_im
    for sweep in range(ITERS):
        step = norm / (forward() + EPS)

        def advance(c, at, step=step):
            value = res_ref[c, :, at] - step * image_ref[c, :, at]
            res_ref[c, :, at] = value
            return value

        for c in range(2):
            grown = scaled(step, dir_ref[c])
            grown_ref[c] = grown if sweep == 0 else grown_ref[c] + grown
        if sweep + 1 < ITERS:
            g_re, g_im, next_norm = adjoint(advance)
            momentum = next_norm / (norm + EPS)
            dir_ref[0] = g_re + scaled(momentum, dir_ref[0])
            dir_ref[1] = g_im + scaled(momentum, dir_ref[1])
            norm = next_norm

    copies, _, lines, _ = out_ref.shape
    width = mics // copies
    upper = (iota((8, width), 0) & 2) == 0
    first = iota((8, 128), 0) < 4
    for copy in range(copies):
        at = slice(copy * width, (copy + 1) * width)
        value = jnp.where(upper, advance(0, at), advance(1, at))
        packed = jnp.where(first, value[:, :128], value[:, 128:]).astype(BF16)
        for ch in range(chunks):
            out_ref[copy, ch, lines - 8 :, :] = packed

    rows_ref[0:stack] = grown_ref[0].astype(BF16)
    rows_ref[stack:] = grown_ref[1].astype(BF16)
    upper = (iota((8, per), 0) & 2) == 0
    radial_rows = (iota((stack, per), 0) >> 1).astype(F32)
    for ch in range(chunks):
        tiles = []
        for part in range(2):
            code = recv_ref[ch, 4 + part : 5 + part, :]
            radius = code - jnp.floor(code * (1.0 / NRAD)) * NRAD
            begin = ch * 2 * per + part * per
            picked = jnp.dot(rows_ref[...], onehot_ref[:, begin : begin + per], preferred_element_type=F32)
            mask = radial_rows == radius
            re = periodic(jnp.sum(groups(jnp.where(mask, picked[:stack], 0.0)), axis=0))
            im = periodic(jnp.sum(groups(jnp.where(mask, picked[stack:], 0.0)), axis=0))
            value = jnp.where(upper, re, im)
            for q in range(0, per // 128, 2):
                tiles.append(jnp.where(first, value[:, q * 128 : (q + 1) * 128], value[:, (q + 1) * 128 : (q + 2) * 128]))
        packed = jnp.concatenate(tiles, axis=0).astype(BF16)
        for copy in range(copies):
            out_ref[copy, ch, 0 : lines - 8, :] = packed


def solve_call(freq_bins, recv, copies):
    chunks, _, per = recv.shape
    mics, modes, stack = chunks * per, 2 * chunks * per, 2 * NRAD
    return pl.pallas_call(
        solve_kernel,
        in_specs=[SMEM, VMEM],
        out_specs=VMEM,
        out_shape=jax.ShapeDtypeStruct((copies, chunks, 4 * modes // chunks // 128 + 8, 128), BF16),
        scratch_shapes=[
            pltpu.VMEM((ORDERS, mics), BF16),
            pltpu.VMEM((2, stack, mics), F32),
            pltpu.VMEM((2, 8, mics), F32),
            pltpu.VMEM((2, 8, mics), F32),
            pltpu.VMEM((2 * stack, mics), BF16),
            pltpu.VMEM((ORDERS, modes), BF16),
            pltpu.VMEM((stack, modes), BF16),
            pltpu.VMEM((2, stack, ORDERS), F32),
            pltpu.VMEM((2, stack, ORDERS), F32),
            pltpu.VMEM((2 * stack, ORDERS), BF16),
        ],
        compiler_params=pltpu.CompilerParams(vmem_limit_bytes=40 << 20),
        name="solve",
        cost_estimate=pl.CostEstimate(flops=10 * 256 * 4096 * 128, bytes_accessed=8 << 20, transcendentals=0),
    )(freq_bins, recv)


def expand_kernel(in_ref, amp_ref, pow_ref, res_ref, wide_ref):
    segs, _, lines, _ = in_ref.shape
    lines = lines - 8
    rows = 4
    dests = amp_ref.shape[0] // rows
    step = pl.program_id(0)
    for d in range(dests):
        for s in range(segs):
            wide_ref[d, pl.ds(s, lines, stride=segs), :] = in_ref[s, step * dests + d, 0:lines, :].astype(F32)
        for kc in range(lines // rows):
            at = slice(kc * 128, (kc + 1) * 128)
            for fl in range(rows // 2):
                power = jnp.zeros((1, 128), F32)
                for c in range(2):
                    line = kc * rows + 2 * c + fl
                    value = wide_ref[d, line * segs : (line + 1) * segs, :]
                    amp_ref[d * rows + 2 * fl + c, :, at] = value
                    power = power + jnp.sum(value * value, axis=0, keepdims=True)
                pow_ref[2 * d + fl : 2 * d + fl + 1, at] = power * (1.0 / segs)

    @pl.when(step == 0)
    def _():
        owner = lax.axis_index("mode")
        for s in range(segs):
            wide_ref[0, pl.ds(s, 8, stride=segs), :] = in_ref[s, owner, lines:, :].astype(F32)
        for half in range(2):
            for fl in range(2):
                for c in range(2):
                    line = half * rows + 2 * c + fl
                    res_ref[2 * fl + c, :, half * 128 : (half + 1) * 128] = wide_ref[0, line * segs : (line + 1) * segs, :]


def expand_call(recv, splits):
    segs, dests, lines, _ = recv.shape
    lines = lines - 8
    rows = 4
    modes = lines // rows * 128
    here = dests // splits
    return pl.pallas_call(
        expand_kernel,
        grid=(splits,),
        in_specs=[VMEM],
        out_specs=[
            pl.BlockSpec((here * rows, segs, modes), lambda i: (i, 0, 0)),
            pl.BlockSpec((here * rows // 2, modes), lambda i: (i, 0)),
            pl.BlockSpec((rows, segs, 256), lambda i: (0, 0, 0)),
        ],
        out_shape=[
            jax.ShapeDtypeStruct((dests * rows, segs, modes), F32),
            jax.ShapeDtypeStruct((dests * rows // 2, modes), F32),
            jax.ShapeDtypeStruct((rows, segs, 256), F32),
        ],
        scratch_shapes=[pltpu.VMEM((here, segs * lines, 128), F32)],
        name="expand",
        cost_estimate=pl.CostEstimate(flops=1 << 21, bytes_accessed=3 << 20, transcendentals=0),
    )(recv)


def on_device(signal, mic_axial, mic_azimuth, mode_m, mode_n, freq_bins):
    segs = lax.axis_size("mic")
    owners = lax.axis_size("mode")
    freqs = freq_bins.shape[0]
    own = freqs // owners
    code = mic_azimuth * AXIAL + mic_axial
    pairs = ([], [])
    for block in range(segs):
        for j in range(owners):
            source = block * owners + j
            pairs[0].append((source, (j + owners * (block % 2)) * owners + block // 2))
            pairs[1].append((source, (j + owners * (1 - block % 2)) * owners + block // 2))
    first = lax.ppermute(code, ("mic", "mode"), pairs[0])
    second = lax.ppermute(code, ("mic", "mode"), pairs[1])
    analysis = analysis_call(freq_bins, signal.shape[2])
    spectra = spectra_call(analysis, mode_m, mode_n, first, second, signal[0], owners)
    recv = lax.all_to_all(spectra, "mode", 0, 0, tiled=True)
    slots = solve_call(freq_bins, recv, segs)
    shape = slots.shape
    slots = lax.all_to_all(slots.reshape(segs * owners, *shape[2:]), ("mic", "mode"), 0, 0, tiled=True)
    amplitude, power, residual = expand_call(slots.reshape(shape), 2)
    modes = mode_m.shape[0]
    return (
        amplitude.reshape(freqs, 2, segs, modes),
        power,
        residual.reshape(own, 2, segs, residual.shape[2]),
    )


def solution(mesh):
    in_specs = (P("mic", "mode", None), P("mic"), P("mic"), P("mode"), P("mode"), P())
    out_specs = (P(None, None, None, "mode"), P(None, "mode"), P("mode", None, None, "mic"))
    return jax.shard_map(
        on_device, mesh=mesh, in_specs=in_specs, out_specs=out_specs, check_vma=False
    )
```

```python
import jax
import jax.numpy as jnp
from jax import lax
from jax.experimental import pallas as pl
from jax.experimental.pallas import tpu as pltpu
from jax.sharding import PartitionSpec as P

ITERS = 2
AXIAL = 64
NRAD = 32
ORDERS = 256
HALF = ORDERS // 2
EPS = 1e-06
SIN_COEFS = (1.5707963200919937, -0.6459637612912833, 0.07968992686556589, -0.0046741574942986315, 0.0001516785309118288)
BF16 = jnp.bfloat16
F32 = jnp.float32
VMEM = pl.BlockSpec(memory_space=pltpu.VMEM)
SMEM = pl.BlockSpec(memory_space=pltpu.SMEM)


def cos_turns(turns):
    z = 1.0 - 4.0 * jnp.abs(turns - jnp.round(turns))
    square = z * z
    total = SIN_COEFS[-1] * square + SIN_COEFS[-2]
    for coef in SIN_COEFS[-3::-1]:
        total = total * square + coef
    return total * z


def sin_turns(turns):
    return cos_turns(turns - 0.25)


def turn_by(re, im, step_re, step_im):
    return re * step_re - im * step_im, re * step_im + im * step_re


def iota(shape, axis):
    return lax.broadcasted_iota(jnp.int32, shape, axis)


def nt_dot(a, b):
    return lax.dot_general(a, b, (((1,), (1,)), ((), ())), preferred_element_type=F32)


def groups(x):
    return x.reshape(x.shape[0] // 8, 8, x.shape[1])


def periodic(x):
    x = x + pltpu.roll(x, 4, 0)
    return x + pltpu.roll(x, 2, 0)


def codes_kernel(azimuth_ref, axial_ref, out_ref):
    code = azimuth_ref[...] * AXIAL + axial_ref[...]
    for copy in range(out_ref.shape[0]):
        out_ref[copy] = code


def codes_call(azimuth, axial, copies):
    mics = azimuth.shape[0]
    return pl.pallas_call(
        codes_kernel,
        in_specs=[VMEM] * 2,
        out_specs=VMEM,
        out_shape=jax.ShapeDtypeStruct((copies, 1, mics), jnp.int32),
        name="codes",
        cost_estimate=pl.CostEstimate(flops=1 << 10, bytes_accessed=1 << 14, transcendentals=0),
    )(azimuth.reshape(1, -1), axial.reshape(1, -1))


def spectra_kernel(freq_ref, m_ref, n_ref, signal_hbm, out_ref, analysis_ref, signal_ref, sems):
    pieces = sems.shape[0]
    tall = signal_ref.shape[0] // pieces
    copies = []
    for k in range(pieces):
        part = pl.ds(k * tall, tall)
        copies.append(pltpu.make_async_copy(signal_hbm.at[part], signal_ref.at[part], sems.at[k]))
        copies[-1].start()
    rows, seglen = analysis_ref.shape
    dests = out_ref.shape[0]
    freqs = rows // 2
    own = freqs // dests
    row = iota((freqs, 128), 0)
    freq = jnp.zeros((freqs, 128), jnp.int32)
    for f in range(freqs):
        freq = jnp.where(row == f, freq_ref[f], freq)
    freq = freq.astype(F32)
    lane = iota((freqs, 128), 1).astype(F32)
    start = freq * lane * (1.0 / seglen)
    step = freq * (128.0 / seglen)
    re, im = cos_turns(start), -sin_turns(start)
    step_re, step_im = cos_turns(step), -sin_turns(step)
    scale = (3.0 * seglen / 8.0) ** (-0.5)
    for block in range(seglen // 128):
        sample = iota((8, 128), 1).astype(F32) + block * 128.0
        window = (0.5 - 0.5 * cos_turns(sample * (1.0 / seglen)))[None] * scale
        at = slice(block * 128, (block + 1) * 128)
        analysis_ref[0:freqs, at] = (groups(re) * window).reshape(freqs, 128).astype(BF16)
        analysis_ref[freqs:, at] = (groups(im) * window).reshape(freqs, 128).astype(BF16)
        re, im = turn_by(re, im, step_re, step_im)

    mics = signal_ref.shape[0]
    m = m_ref[...]
    code = (jnp.where(m >= 0, m, HALF - 1 - m) * NRAD + n_ref[...]).astype(F32)
    tail = jnp.concatenate([code[:, :mics], code[:, mics:], jnp.zeros((2, mics), F32)], axis=0)
    for d in range(dests):
        out_ref[d, 2 * own :, :] = tail
    width = 128
    for block in range(mics // width):
        at = slice(block * width, (block + 1) * width)
        for k in range(block * width // tall, (block + 1) * width // tall):
            copies[k].wait()
        spectra = nt_dot(analysis_ref[...], signal_ref[at, :])
        for d in range(dests):
            out_ref[d, 0:own, at] = spectra[d * own : (d + 1) * own]
            out_ref[d, own : 2 * own, at] = spectra[freqs + d * own : freqs + (d + 1) * own]


def spectra_call(freq_bins, mode_m, mode_n, signal, dests):
    mics, seglen = signal.shape
    rows = 2 * freq_bins.shape[0]
    return pl.pallas_call(
        spectra_kernel,
        in_specs=[SMEM, VMEM, VMEM, pl.BlockSpec(memory_space=pltpu.HBM)],
        out_specs=VMEM,
        out_shape=jax.ShapeDtypeStruct((dests, 8, mics), F32),
        scratch_shapes=[
            pltpu.VMEM((rows, seglen), BF16),
            pltpu.VMEM((mics, seglen), BF16),
            pltpu.SemaphoreType.DMA((16,)),
        ],
        name="spectra",
        cost_estimate=pl.CostEstimate(flops=2 * rows * mics * seglen, bytes_accessed=mics * seglen * 2, transcendentals=0),
    )(freq_bins, mode_m.reshape(1, -1), mode_n.reshape(1, -1), signal)


def basis_kernel(freq_ref, code_ref, azim_ref, seed_ref):
    blocks, _, width = code_ref.shape
    chunks, _, per = azim_ref.shape
    base = 2 * lax.axis_index("mode")
    odd = (iota((8, width), 0) & 1) == 1
    freq = jnp.where(odd, freq_ref[base + 1], freq_ref[base]).astype(F32)
    row = iota((8, width), 0).astype(F32)
    radial = (iota((8, width), 0) >> 1).astype(F32)

    @pl.loop(0, chunks)
    def _(ch):
        for piece in range(per // width):
            at = slice(piece * width, (piece + 1) * width)
            code = jnp.broadcast_to(code_ref[ch * (per // width) + piece], (8, width))
            azimuth = (code >> 6).astype(F32)
            axial = (code & (AXIAL - 1)).astype(F32)
            turns = azimuth * (row + 0.5) * (1.0 / 512)
            re, im = cos_turns(turns), sin_turns(turns)
            turns = azimuth * (8.0 / 512)
            step_re, step_im = cos_turns(turns), sin_turns(turns)
            next_re, next_im = turn_by(re, im, step_re, step_im)
            step_re, step_im = turn_by(step_re, step_im, step_re, step_im)
            re = jnp.stack([re, next_re])
            im = jnp.stack([im, next_im])
            for a in range(HALF // 16):
                azim_ref[ch, 16 * a : 16 * a + 16, at] = re.reshape(16, width).astype(BF16)
                azim_ref[ch, HALF + 16 * a : HALF + 16 * a + 16, at] = im.reshape(16, width).astype(BF16)
                if a + 1 < HALF // 16:
                    re, im = turn_by(re, im, step_re[None], step_im[None])
            turns = (axial * freq * (2.0 * NRAD - radial) - azimuth * 32.0) * (1.0 / 32768)
            re, im = cos_turns(turns), sin_turns(turns)
            turns = axial * freq * (-4.0 / 32768)
            step_re, step_im = cos_turns(turns), sin_turns(turns)
            for k, value in enumerate((re, im, step_re, step_im)):
                seed_ref[ch, k, :, at] = value


def basis_call(freq_bins, codes, chunks):
    blocks, _, width = codes.shape
    per = blocks * width // chunks
    return pl.pallas_call(
        basis_kernel,
        in_specs=[SMEM, VMEM],
        out_specs=[VMEM] * 2,
        out_shape=[
            jax.ShapeDtypeStruct((chunks, ORDERS, per), BF16),
            jax.ShapeDtypeStruct((chunks, 4, 8, per), F32),
        ],
        compiler_params=pltpu.CompilerParams(vmem_limit_bytes=12 << 20),
        name="basis",
        cost_estimate=pl.CostEstimate(flops=40 * ORDERS * per * chunks, bytes_accessed=3 << 20, transcendentals=0),
    )(freq_bins, codes)


def solve_kernel(
    recv_ref, azim_ref, seed_ref, out_ref, rad_ref, res_ref, image_ref, field_ref, onehot_ref, dir_ref, grown_ref, rows_ref
):
    chunks, _, per = recv_ref.shape
    mics = chunks * per
    stack = 2 * NRAD
    odd = (iota((8, per), 0) & 1) == 1
    for ch in range(chunks):
        for c in range(2):
            res_ref[ch, c] = jnp.where(odd, recv_ref[ch, 2 * c + 1 : 2 * c + 2, :], recv_ref[ch, 2 * c : 2 * c + 1, :])

        re, im, step_re, step_im = (seed_ref[ch, k] for k in range(4))
        for a in range(stack // 8):
            rad_ref[ch, 0, 8 * a : 8 * a + 8] = re
            rad_ref[ch, 1, 8 * a : 8 * a + 8] = im
            if a + 1 < stack // 8:
                re, im = turn_by(re, im, step_re, step_im)

    order_rows = iota((ORDERS, 128), 0).astype(F32).astype(BF16)
    radial_rows = (iota((stack, 128), 0) >> 1).astype(F32).astype(BF16)
    one, zero = jnp.ones((), BF16), jnp.zeros((), BF16)
    counts = jnp.zeros((stack, ORDERS), F32)

    def modes_of(k):
        return jnp.concatenate([onehot_ref[k, q] for q in range(per // 128)], axis=1)

    for ch in range(chunks):
        for part in range(2):
            code = recv_ref[ch, 4 + part : 5 + part, :]
            order = jnp.floor(code * (1.0 / NRAD))
            radius = (code - order * NRAD).astype(BF16)
            order = order.astype(BF16)
            picks = []
            for q in range(per // 128):
                at = slice(q * 128, (q + 1) * 128)
                onehot_ref[2 * ch + part, q] = jnp.where(order_rows == order[:, at], one, zero)
                picks.append(jnp.where(radial_rows == radius[:, at], one, zero))
            counts = counts + nt_dot(jnp.concatenate(picks, axis=1), modes_of(2 * ch + part))

    weight = (mics ** (-0.5)) * lax.rsqrt(1.0 + (iota((stack, ORDERS), 0) >> 1).astype(F32))
    counts_weight = counts * weight

    def scaled(column, x):
        return (column[None] * groups(x)).reshape(x.shape)

    def row_sums(x):
        return periodic(jnp.sum(jnp.sum(groups(x), axis=0), axis=1, keepdims=True))

    def adjoint(advance):
        out = jnp.zeros((2 * stack, ORDERS), F32)
        for ch in range(chunks):
            re, im = advance(ch, 0)[None], advance(ch, 1)[None]
            ec, es = groups(rad_ref[ch, 0]), groups(rad_ref[ch, 1])
            field_ref[ch, 0:stack] = (re * ec + im * es).reshape(stack, per).astype(BF16)
            field_ref[ch, stack:] = (im * ec - re * es).reshape(stack, per).astype(BF16)
            out = out + nt_dot(field_ref[ch], azim_ref[ch])
        re, im = out[:stack], out[stack:]
        rc, rs, ic, ics = re[:, :HALF], re[:, HALF:], im[:, :HALF], im[:, HALF:]
        g_re = jnp.concatenate([rc + ics, rc - ics], axis=1) * weight
        g_im = jnp.concatenate([ic - rs, ic + rs], axis=1) * weight
        return g_re, g_im, row_sums(counts * (g_re * g_re + g_im * g_im))

    def forward():
        x_re, x_im = dir_ref[0] * counts_weight, dir_ref[1] * counts_weight
        p_re, m_re, p_im, m_im = x_re[:, :HALF], x_re[:, HALF:], x_im[:, :HALF], x_im[:, HALF:]
        rows_ref[0:stack] = jnp.concatenate([p_re + m_re, m_im - p_im], axis=1).astype(BF16)
        rows_ref[stack:] = jnp.concatenate([p_im + m_im, p_re - m_re], axis=1).astype(BF16)
        norm = jnp.zeros((8, per), F32)
        for ch in range(chunks):
            out = jnp.dot(rows_ref[...], azim_ref[ch], preferred_element_type=F32)
            t_re, t_im = out[:stack], out[stack:]
            ec, es = rad_ref[ch, 0], rad_ref[ch, 1]
            i_re = periodic(jnp.sum(groups(ec * t_re - es * t_im), axis=0))
            i_im = periodic(jnp.sum(groups(ec * t_im + es * t_re), axis=0))
            image_ref[ch, 0] = i_re
            image_ref[ch, 1] = i_im
            norm = norm + (i_re * i_re + i_im * i_im)
        return jnp.sum(norm, axis=1, keepdims=True)

    g_re, g_im, norm = adjoint(lambda ch, c: res_ref[ch, c])
    dir_ref[0] = g_re
    dir_ref[1] = g_im
    for sweep in range(ITERS):
        step = norm / (forward() + EPS)

        def advance(ch, c, step=step):
            value = res_ref[ch, c] - step * image_ref[ch, c]
            res_ref[ch, c] = value
            return value

        for c in range(2):
            grown = scaled(step, dir_ref[c])
            grown_ref[c] = grown if sweep == 0 else grown_ref[c] + grown
        if sweep + 1 < ITERS:
            g_re, g_im, next_norm = adjoint(advance)
            momentum = next_norm / (norm + EPS)
            dir_ref[0] = g_re + scaled(momentum, dir_ref[0])
            dir_ref[1] = g_im + scaled(momentum, dir_ref[1])
            norm = next_norm

    copies, _, lines, _ = out_ref.shape
    width = mics // copies
    upper = (iota((8, per), 0) & 2) == 0
    first = iota((8, 128), 0) < 4
    for ch in range(chunks):
        value = jnp.where(upper, advance(ch, 0), advance(ch, 1))
        for piece in range(per // width):
            left, right = value[:, piece * width : piece * width + 128], value[:, piece * width + 128 : (piece + 1) * width]
            packed = jnp.where(first, left, right).astype(BF16)
            for owner in range(chunks):
                out_ref[ch * (per // width) + piece, owner, lines - 8 :, :] = packed

    rows_ref[0:stack] = grown_ref[0].astype(BF16)
    rows_ref[stack:] = grown_ref[1].astype(BF16)
    radial_rows = (iota((stack, per), 0) >> 1).astype(F32)
    for ch in range(chunks):
        tiles = []
        for part in range(2):
            code = recv_ref[ch, 4 + part : 5 + part, :]
            radius = code - jnp.floor(code * (1.0 / NRAD)) * NRAD
            picked = jnp.dot(rows_ref[...], modes_of(2 * ch + part), preferred_element_type=F32)
            mask = radial_rows == radius
            re = periodic(jnp.sum(groups(jnp.where(mask, picked[:stack], 0.0)), axis=0))
            im = periodic(jnp.sum(groups(jnp.where(mask, picked[stack:], 0.0)), axis=0))
            value = jnp.where(upper, re, im)
            for q in range(0, per // 128, 2):
                tiles.append(jnp.where(first, value[:, q * 128 : (q + 1) * 128], value[:, (q + 1) * 128 : (q + 2) * 128]))
        packed = jnp.concatenate(tiles, axis=0).astype(BF16)
        for copy in range(copies):
            out_ref[copy, ch, 0 : lines - 8, :] = packed


def solve_call(recv, azim, seeds, copies):
    chunks, _, per = recv.shape
    modes, stack = 2 * chunks * per, 2 * NRAD
    return pl.pallas_call(
        solve_kernel,
        in_specs=[VMEM] * 3,
        out_specs=VMEM,
        out_shape=jax.ShapeDtypeStruct((copies, chunks, 4 * modes // chunks // 128 + 8, 128), BF16),
        scratch_shapes=[
            pltpu.VMEM((chunks, 2, stack, per), F32),
            pltpu.VMEM((chunks, 2, 8, per), F32),
            pltpu.VMEM((chunks, 2, 8, per), F32),
            pltpu.VMEM((chunks, 2 * stack, per), BF16),
            pltpu.VMEM((2 * chunks, per // 128, ORDERS, 128), BF16),
            pltpu.VMEM((2, stack, ORDERS), F32),
            pltpu.VMEM((2, stack, ORDERS), F32),
            pltpu.VMEM((2 * stack, ORDERS), BF16),
        ],
        compiler_params=pltpu.CompilerParams(vmem_limit_bytes=14 << 20),
        name="solve",
        cost_estimate=pl.CostEstimate(flops=10 * 256 * 4096 * 128, bytes_accessed=8 << 20, transcendentals=0),
    )(recv, azim, seeds)


def expand_kernel(in_ref, amp_ref, pow_ref, res_ref, wide_ref, ready_ref, sems):
    segs, dests, lines, _ = in_ref.shape
    rows = 4
    tiles = lines // 8
    copies = []
    for d in range(dests):
        for s in range(segs):
            for tile in range(tiles - 1):
                wide_ref[d % 2, tile, 8 * s : 8 * s + 8, :] = in_ref[s, d, 8 * tile : 8 * tile + 8, :].astype(F32)
        for kc in range(8 * (tiles - 1) // rows):
            at = slice(kc * 128, (kc + 1) * 128)
            for fl in range(rows // 2):
                power = jnp.zeros((segs, 128), F32)
                for c in range(2):
                    line = kc * rows + 2 * c + fl
                    value = wide_ref[d % 2, line // 8, pl.ds(line % 8, segs, stride=8), :]
                    ready_ref[d, 2 * fl + c, :, at] = value
                    power = power + value * value
                pow_ref[2 * d + fl : 2 * d + fl + 1, at] = jnp.sum(power, axis=0, keepdims=True) * (1.0 / segs)
        copies.append(pltpu.make_async_copy(ready_ref.at[d], amp_ref.at[pl.ds(d * rows, rows)], sems.at[d]))
        copies[-1].start()

    owner = lax.axis_index("mode")
    for s in range(segs):
        wide_ref[0, 0, 8 * s : 8 * s + 8, :] = in_ref[s, owner, 8 * (tiles - 1) :, :].astype(F32)
    for half in range(2):
        for fl in range(2):
            for c in range(2):
                line = half * rows + 2 * c + fl
                res_ref[2 * fl + c, :, half * 128 : (half + 1) * 128] = wide_ref[0, 0, pl.ds(line, segs, stride=8), :]
    for copy in copies:
        copy.wait()


def expand_call(recv):
    segs, dests, lines, _ = recv.shape
    rows = 4
    modes = (lines - 8) // rows * 128
    return pl.pallas_call(
        expand_kernel,
        in_specs=[VMEM],
        out_specs=[pl.BlockSpec(memory_space=pl.ANY), VMEM, VMEM],
        out_shape=[
            jax.ShapeDtypeStruct((dests * rows, segs, modes), F32),
            jax.ShapeDtypeStruct((dests * rows // 2, modes), F32),
            jax.ShapeDtypeStruct((rows, segs, 256), F32),
        ],
        scratch_shapes=[
            pltpu.VMEM((2, lines // 8 - 1, 8 * segs, 128), F32),
            pltpu.VMEM((dests, rows, segs, modes), F32),
            pltpu.SemaphoreType.DMA((dests,)),
        ],
        compiler_params=pltpu.CompilerParams(vmem_limit_bytes=12 << 20),
        name="expand",
        cost_estimate=pl.CostEstimate(flops=1 << 21, bytes_accessed=3 << 20, transcendentals=0),
    )(recv)


def on_device(signal, mic_axial, mic_azimuth, mode_m, mode_n, freq_bins):
    segs = lax.axis_size("mic")
    owners = lax.axis_size("mode")
    freqs = freq_bins.shape[0]
    own = freqs // owners
    codes = lax.all_to_all(codes_call(mic_azimuth, mic_axial, segs), "mic", 0, 0, tiled=True)
    spectra = spectra_call(freq_bins, mode_m, mode_n, signal[0], owners)
    recv = lax.all_to_all(spectra, "mode", 0, 0, tiled=True)
    azim, seeds = basis_call(freq_bins, codes, owners)
    slots = solve_call(recv, azim, seeds, segs)
    shape = slots.shape
    slots = lax.all_to_all(slots.reshape(segs * owners, *shape[2:]), ("mic", "mode"), 0, 0, tiled=True)
    amplitude, power, residual = expand_call(slots.reshape(shape))
    modes = mode_m.shape[0]
    return (
        amplitude.reshape(freqs, 2, segs, modes),
        power,
        residual.reshape(own, 2, segs, residual.shape[2]),
    )


def solution(mesh):
    in_specs = (P("mic", "mode", None), P("mic"), P("mic"), P("mode"), P("mode"), P())
    out_specs = (P(None, None, None, "mode"), P(None, "mode"), P("mode", None, None, "mic"))
    return jax.shard_map(
        on_device, mesh=mesh, in_specs=in_specs, out_specs=out_specs, check_vma=False
    )
```

```python
import jax
import jax.numpy as jnp
from jax import lax
from jax.experimental import pallas as pl
from jax.experimental.pallas import tpu as pltpu
from jax.sharding import PartitionSpec as P

ITERS = 2
AXIAL = 64
NRAD = 32
ORDERS = 256
HALF = ORDERS // 2
EPS = 1e-06
SIN_COEFS = (1.5707963200919937, -0.6459637612912833, 0.07968992686556589, -0.0046741574942986315, 0.0001516785309118288)
BF16 = jnp.bfloat16
F32 = jnp.float32
VMEM = pl.BlockSpec(memory_space=pltpu.VMEM)
SMEM = pl.BlockSpec(memory_space=pltpu.SMEM)
HBM = pl.BlockSpec(memory_space=pltpu.HBM)


def cos_turns(turns):
    z = 1.0 - 4.0 * jnp.abs(turns - jnp.round(turns))
    square = z * z
    total = SIN_COEFS[-1] * square + SIN_COEFS[-2]
    for coef in SIN_COEFS[-3::-1]:
        total = total * square + coef
    return total * z


def sin_turns(turns):
    return cos_turns(turns - 0.25)


def turn_by(re, im, step_re, step_im):
    return re * step_re - im * step_im, re * step_im + im * step_re


def iota(shape, axis):
    return lax.broadcasted_iota(jnp.int32, shape, axis)


def nt_dot(a, b):
    return lax.dot_general(a, b, (((1,), (1,)), ((), ())), preferred_element_type=F32)


def groups(x):
    return x.reshape(x.shape[0] // 8, 8, x.shape[1])


def periodic(x):
    x = x + pltpu.roll(x, 4, 0)
    return x + pltpu.roll(x, 2, 0)


def codes_kernel(azimuth_hbm, axial_hbm, out_hbm, azimuth_ref, axial_ref, out_ref, sems):
    loads = [
        pltpu.make_async_copy(azimuth_hbm, azimuth_ref, sems.at[0]),
        pltpu.make_async_copy(axial_hbm, axial_ref, sems.at[1]),
    ]
    for load in loads:
        load.start()
    for load in loads:
        load.wait()
    code = azimuth_ref[...] * AXIAL + axial_ref[...]
    for copy in range(out_ref.shape[0]):
        out_ref[copy] = code
    store = pltpu.make_async_copy(out_ref, out_hbm, sems.at[2])
    store.start()
    store.wait()


def codes_call(azimuth, axial, copies):
    mics = azimuth.shape[0]
    return pl.pallas_call(
        codes_kernel,
        in_specs=[HBM] * 2,
        out_specs=HBM,
        out_shape=jax.ShapeDtypeStruct((copies, 1, mics), jnp.int32),
        scratch_shapes=[
            pltpu.VMEM((1, mics), jnp.int32),
            pltpu.VMEM((1, mics), jnp.int32),
            pltpu.VMEM((copies, 1, mics), jnp.int32),
            pltpu.SemaphoreType.DMA((3,)),
        ],
        name="codes",
        cost_estimate=pl.CostEstimate(flops=1 << 10, bytes_accessed=1 << 14, transcendentals=0),
    )(azimuth.reshape(1, -1), axial.reshape(1, -1))


def spectra_kernel(
    freq_hbm, m_hbm, n_hbm, signal_hbm, out_hbm, freq_ref, m_ref, n_ref, analysis_ref, signal_ref, out_ref, small_sems, sems, out_sems
):
    loads = [
        pltpu.make_async_copy(freq_hbm, freq_ref, small_sems.at[0]),
        pltpu.make_async_copy(m_hbm, m_ref, small_sems.at[1]),
        pltpu.make_async_copy(n_hbm, n_ref, small_sems.at[2]),
    ]
    for load in loads:
        load.start()
    mics = signal_ref.shape[0]
    pieces = sems.shape[0]
    tall = mics // pieces
    copies = []
    for k in range(pieces):
        part = pl.ds(k * tall, tall)
        copies.append(pltpu.make_async_copy(signal_hbm.at[part], signal_ref.at[part], sems.at[k]))
        copies[-1].start()
    for load in loads:
        load.wait()
    rows, seglen = analysis_ref.shape
    dests = out_ref.shape[0]
    freqs = rows // 2
    own = freqs // dests
    row = iota((freqs, 128), 0)
    freq = jnp.zeros((freqs, 128), jnp.int32)
    for f in range(freqs):
        freq = jnp.where(row == f, freq_ref[f], freq)
    freq = freq.astype(F32)
    lane = iota((freqs, 128), 1).astype(F32)
    start = freq * lane * (1.0 / seglen)
    step = freq * (128.0 / seglen)
    re, im = cos_turns(start), -sin_turns(start)
    step_re, step_im = cos_turns(step), -sin_turns(step)
    scale = (3.0 * seglen / 8.0) ** (-0.5)
    for block in range(seglen // 128):
        sample = iota((8, 128), 1).astype(F32) + block * 128.0
        window = (0.5 - 0.5 * cos_turns(sample * (1.0 / seglen)))[None] * scale
        at = slice(block * 128, (block + 1) * 128)
        analysis_ref[0:freqs, at] = (groups(re) * window).reshape(freqs, 128).astype(BF16)
        analysis_ref[freqs:, at] = (groups(im) * window).reshape(freqs, 128).astype(BF16)
        re, im = turn_by(re, im, step_re, step_im)

    m = m_ref[...]
    code = (jnp.where(m >= 0, m, HALF - 1 - m) * NRAD + n_ref[...]).astype(F32)
    tail = jnp.concatenate([code[:, :mics], code[:, mics:], jnp.zeros((2, mics), F32)], axis=0)
    for d in range(dests):
        out_ref[d, 2 * own :, :] = tail
    width = 128
    stores = []
    for block in range(mics // width):
        at = slice(block * width, (block + 1) * width)
        for k in range(block * width // tall, (block + 1) * width // tall):
            copies[k].wait()
        spectra = nt_dot(analysis_ref[...], signal_ref[at, :])
        for d in range(dests):
            out_ref[d, 0:own, at] = spectra[d * own : (d + 1) * own]
            out_ref[d, own : 2 * own, at] = spectra[freqs + d * own : freqs + (d + 1) * own]
        part = pl.ds(block * width, width)
        stores.append(pltpu.make_async_copy(out_ref.at[:, :, part], out_hbm.at[:, :, part], out_sems.at[block]))
        stores[-1].start()
    for store in stores:
        store.wait()


def spectra_call(freq_bins, mode_m, mode_n, signal, dests):
    mics, seglen = signal.shape
    modes = mode_m.shape[0]
    rows = 2 * freq_bins.shape[0]
    return pl.pallas_call(
        spectra_kernel,
        in_specs=[HBM] * 4,
        out_specs=HBM,
        out_shape=jax.ShapeDtypeStruct((dests, 8, mics), F32),
        scratch_shapes=[
            pltpu.SMEM(freq_bins.shape, jnp.int32),
            pltpu.VMEM((1, modes), jnp.int32),
            pltpu.VMEM((1, modes), jnp.int32),
            pltpu.VMEM((rows, seglen), BF16),
            pltpu.VMEM((mics, seglen), BF16),
            pltpu.VMEM((dests, 8, mics), F32),
            pltpu.SemaphoreType.DMA((3,)),
            pltpu.SemaphoreType.DMA((mics // 32,)),
            pltpu.SemaphoreType.DMA((mics // 128,)),
        ],
        name="spectra",
        cost_estimate=pl.CostEstimate(flops=2 * rows * mics * seglen, bytes_accessed=mics * seglen * 2, transcendentals=0),
    )(freq_bins, mode_m.reshape(1, -1), mode_n.reshape(1, -1), signal)


def basis_kernel(freq_ref, code_ref, azim_ref, seed_ref):
    blocks, _, width = code_ref.shape
    chunks, _, per = azim_ref.shape
    base = 2 * lax.axis_index("mode")
    odd = (iota((8, width), 0) & 1) == 1
    freq = jnp.where(odd, freq_ref[base + 1], freq_ref[base]).astype(F32)
    row = iota((8, width), 0).astype(F32)
    radial = (iota((8, width), 0) >> 1).astype(F32)

    @pl.loop(0, chunks)
    def _(ch):
        for piece in range(per // width):
            at = slice(piece * width, (piece + 1) * width)
            code = jnp.broadcast_to(code_ref[ch * (per // width) + piece], (8, width))
            azimuth = (code >> 6).astype(F32)
            axial = (code & (AXIAL - 1)).astype(F32)
            turns = azimuth * (row + 0.5) * (1.0 / 512)
            re, im = cos_turns(turns), sin_turns(turns)
            turns = azimuth * (8.0 / 512)
            step_re, step_im = cos_turns(turns), sin_turns(turns)
            next_re, next_im = turn_by(re, im, step_re, step_im)
            step_re, step_im = turn_by(step_re, step_im, step_re, step_im)
            re = jnp.stack([re, next_re])
            im = jnp.stack([im, next_im])
            for a in range(HALF // 16):
                azim_ref[ch, 16 * a : 16 * a + 16, at] = re.reshape(16, width).astype(BF16)
                azim_ref[ch, HALF + 16 * a : HALF + 16 * a + 16, at] = im.reshape(16, width).astype(BF16)
                if a + 1 < HALF // 16:
                    re, im = turn_by(re, im, step_re[None], step_im[None])
            turns = (axial * freq * (2.0 * NRAD - radial) - azimuth * 32.0) * (1.0 / 32768)
            re, im = cos_turns(turns), sin_turns(turns)
            turns = axial * freq * (-4.0 / 32768)
            step_re, step_im = cos_turns(turns), sin_turns(turns)
            for k, value in enumerate((re, im, step_re, step_im)):
                seed_ref[ch, k, :, at] = value


def basis_call(freq_bins, codes, chunks):
    blocks, _, width = codes.shape
    per = blocks * width // chunks
    return pl.pallas_call(
        basis_kernel,
        in_specs=[SMEM, VMEM],
        out_specs=[VMEM] * 2,
        out_shape=[
            jax.ShapeDtypeStruct((chunks, ORDERS, per), BF16),
            jax.ShapeDtypeStruct((chunks, 4, 8, per), F32),
        ],
        compiler_params=pltpu.CompilerParams(vmem_limit_bytes=12 << 20),
        name="basis",
        cost_estimate=pl.CostEstimate(flops=40 * ORDERS * per * chunks, bytes_accessed=3 << 20, transcendentals=0),
    )(freq_bins, codes)


def solve_kernel(
    recv_ref, azim_ref, seed_ref, out_ref, rad_ref, res_ref, image_ref, field_ref, onehot_ref, dir_ref, grown_ref, rows_ref
):
    chunks, _, per = recv_ref.shape
    mics = chunks * per
    stack = 2 * NRAD
    odd = (iota((8, per), 0) & 1) == 1
    for ch in range(chunks):
        for c in range(2):
            res_ref[ch, c] = jnp.where(odd, recv_ref[ch, 2 * c + 1 : 2 * c + 2, :], recv_ref[ch, 2 * c : 2 * c + 1, :])

        re, im, step_re, step_im = (seed_ref[ch, k] for k in range(4))
        for a in range(stack // 8):
            rad_ref[ch, 0, 8 * a : 8 * a + 8] = re
            rad_ref[ch, 1, 8 * a : 8 * a + 8] = im
            if a + 1 < stack // 8:
                re, im = turn_by(re, im, step_re, step_im)

    order_rows = iota((ORDERS, 128), 0).astype(F32).astype(BF16)
    radial_rows = (iota((stack, 128), 0) >> 1).astype(F32).astype(BF16)
    one, zero = jnp.ones((), BF16), jnp.zeros((), BF16)
    counts = jnp.zeros((stack, ORDERS), F32)

    def modes_of(k):
        return jnp.concatenate([onehot_ref[k, q] for q in range(per // 128)], axis=1)

    for ch in range(chunks):
        for part in range(2):
            code = recv_ref[ch, 4 + part : 5 + part, :]
            order = jnp.floor(code * (1.0 / NRAD))
            radius = (code - order * NRAD).astype(BF16)
            order = order.astype(BF16)
            picks = []
            for q in range(per // 128):
                at = slice(q * 128, (q + 1) * 128)
                onehot_ref[2 * ch + part, q] = jnp.where(order_rows == order[:, at], one, zero)
                picks.append(jnp.where(radial_rows == radius[:, at], one, zero))
            counts = counts + nt_dot(jnp.concatenate(picks, axis=1), modes_of(2 * ch + part))

    weight = (mics ** (-0.5)) * lax.rsqrt(1.0 + (iota((stack, ORDERS), 0) >> 1).astype(F32))
    counts_weight = counts * weight

    def scaled(column, x):
        return (column[None] * groups(x)).reshape(x.shape)

    def row_sums(x):
        return periodic(jnp.sum(jnp.sum(groups(x), axis=0), axis=1, keepdims=True))

    def adjoint(advance):
        out = jnp.zeros((2 * stack, ORDERS), F32)
        for ch in range(chunks):
            re, im = advance(ch, 0)[None], advance(ch, 1)[None]
            ec, es = groups(rad_ref[ch, 0]), groups(rad_ref[ch, 1])
            field_ref[ch, 0:stack] = (re * ec + im * es).reshape(stack, per).astype(BF16)
            field_ref[ch, stack:] = (im * ec - re * es).reshape(stack, per).astype(BF16)
            out = out + nt_dot(field_ref[ch], azim_ref[ch])
        re, im = out[:stack], out[stack:]
        rc, rs, ic, ics = re[:, :HALF], re[:, HALF:], im[:, :HALF], im[:, HALF:]
        g_re = jnp.concatenate([rc + ics, rc - ics], axis=1) * weight
        g_im = jnp.concatenate([ic - rs, ic + rs], axis=1) * weight
        return g_re, g_im, row_sums(counts * (g_re * g_re + g_im * g_im))

    def forward():
        x_re, x_im = dir_ref[0] * counts_weight, dir_ref[1] * counts_weight
        p_re, m_re, p_im, m_im = x_re[:, :HALF], x_re[:, HALF:], x_im[:, :HALF], x_im[:, HALF:]
        rows_ref[0:stack] = jnp.concatenate([p_re + m_re, m_im - p_im], axis=1).astype(BF16)
        rows_ref[stack:] = jnp.concatenate([p_im + m_im, p_re - m_re], axis=1).astype(BF16)
        norm = jnp.zeros((8, per), F32)
        for ch in range(chunks):
            out = jnp.dot(rows_ref[...], azim_ref[ch], preferred_element_type=F32)
            t_re, t_im = out[:stack], out[stack:]
            ec, es = rad_ref[ch, 0], rad_ref[ch, 1]
            i_re = periodic(jnp.sum(groups(ec * t_re - es * t_im), axis=0))
            i_im = periodic(jnp.sum(groups(ec * t_im + es * t_re), axis=0))
            image_ref[ch, 0] = i_re
            image_ref[ch, 1] = i_im
            norm = norm + (i_re * i_re + i_im * i_im)
        return jnp.sum(norm, axis=1, keepdims=True)

    g_re, g_im, norm = adjoint(lambda ch, c: res_ref[ch, c])
    dir_ref[0] = g_re
    dir_ref[1] = g_im
    for sweep in range(ITERS):
        step = norm / (forward() + EPS)

        def advance(ch, c, step=step):
            value = res_ref[ch, c] - step * image_ref[ch, c]
            res_ref[ch, c] = value
            return value

        for c in range(2):
            grown = scaled(step, dir_ref[c])
            grown_ref[c] = grown if sweep == 0 else grown_ref[c] + grown
        if sweep + 1 < ITERS:
            g_re, g_im, next_norm = adjoint(advance)
            momentum = next_norm / (norm + EPS)
            dir_ref[0] = g_re + scaled(momentum, dir_ref[0])
            dir_ref[1] = g_im + scaled(momentum, dir_ref[1])
            norm = next_norm

    copies, _, lines, _ = out_ref.shape
    width = mics // copies
    upper = (iota((8, per), 0) & 2) == 0
    first = iota((8, 128), 0) < 4
    for ch in range(chunks):
        value = jnp.where(upper, advance(ch, 0), advance(ch, 1))
        for piece in range(per // width):
            left, right = value[:, piece * width : piece * width + 128], value[:, piece * width + 128 : (piece + 1) * width]
            packed = jnp.where(first, left, right).astype(BF16)
            for owner in range(chunks):
                out_ref[ch * (per // width) + piece, owner, lines - 8 :, :] = packed

    rows_ref[0:stack] = grown_ref[0].astype(BF16)
    rows_ref[stack:] = grown_ref[1].astype(BF16)
    radial_rows = (iota((stack, per), 0) >> 1).astype(F32)
    for ch in range(chunks):
        tiles = []
        for part in range(2):
            code = recv_ref[ch, 4 + part : 5 + part, :]
            radius = code - jnp.floor(code * (1.0 / NRAD)) * NRAD
            picked = jnp.dot(rows_ref[...], modes_of(2 * ch + part), preferred_element_type=F32)
            mask = radial_rows == radius
            re = periodic(jnp.sum(groups(jnp.where(mask, picked[:stack], 0.0)), axis=0))
            im = periodic(jnp.sum(groups(jnp.where(mask, picked[stack:], 0.0)), axis=0))
            value = jnp.where(upper, re, im)
            for q in range(0, per // 128, 2):
                tiles.append(jnp.where(first, value[:, q * 128 : (q + 1) * 128], value[:, (q + 1) * 128 : (q + 2) * 128]))
        packed = jnp.concatenate(tiles, axis=0).astype(BF16)
        for copy in range(copies):
            out_ref[copy, ch, 0 : lines - 8, :] = packed


def solve_call(recv, azim, seeds, copies):
    chunks, _, per = recv.shape
    modes, stack = 2 * chunks * per, 2 * NRAD
    return pl.pallas_call(
        solve_kernel,
        in_specs=[VMEM] * 3,
        out_specs=VMEM,
        out_shape=jax.ShapeDtypeStruct((copies, chunks, 4 * modes // chunks // 128 + 8, 128), BF16),
        scratch_shapes=[
            pltpu.VMEM((chunks, 2, stack, per), F32),
            pltpu.VMEM((chunks, 2, 8, per), F32),
            pltpu.VMEM((chunks, 2, 8, per), F32),
            pltpu.VMEM((chunks, 2 * stack, per), BF16),
            pltpu.VMEM((2 * chunks, per // 128, ORDERS, 128), BF16),
            pltpu.VMEM((2, stack, ORDERS), F32),
            pltpu.VMEM((2, stack, ORDERS), F32),
            pltpu.VMEM((2 * stack, ORDERS), BF16),
        ],
        compiler_params=pltpu.CompilerParams(vmem_limit_bytes=14 << 20),
        name="solve",
        cost_estimate=pl.CostEstimate(flops=10 * 256 * 4096 * 128, bytes_accessed=8 << 20, transcendentals=0),
    )(recv, azim, seeds)


def expand_kernel(in_ref, amp_hbm, pow_hbm, res_hbm, wide_ref, ready_ref, pow_ref, res_ref, sems):
    segs, dests, lines, _ = in_ref.shape
    rows = 4
    tiles = lines // 8
    owner = lax.axis_index("mode")
    for s in range(segs):
        wide_ref[1, 0, 8 * s : 8 * s + 8, :] = in_ref[s, owner, 8 * (tiles - 1) :, :].astype(F32)
    for half in range(2):
        for fl in range(2):
            for c in range(2):
                line = half * rows + 2 * c + fl
                res_ref[2 * fl + c, :, half * 128 : (half + 1) * 128] = wide_ref[1, 0, pl.ds(line, segs, stride=8), :]
    copies = [pltpu.make_async_copy(res_ref, res_hbm, sems.at[dests])]
    copies[-1].start()
    for d in range(dests):
        for s in range(segs):
            for tile in range(tiles - 1):
                wide_ref[d % 2, tile, 8 * s : 8 * s + 8, :] = in_ref[s, d, 8 * tile : 8 * tile + 8, :].astype(F32)
        for kc in range(8 * (tiles - 1) // rows):
            at = slice(kc * 128, (kc + 1) * 128)
            for fl in range(rows // 2):
                power = jnp.zeros((segs, 128), F32)
                for c in range(2):
                    line = kc * rows + 2 * c + fl
                    value = wide_ref[d % 2, line // 8, pl.ds(line % 8, segs, stride=8), :]
                    ready_ref[d, 2 * fl + c, :, at] = value
                    power = power + value * value
                pow_ref[2 * d + fl : 2 * d + fl + 1, at] = jnp.sum(power, axis=0, keepdims=True) * (1.0 / segs)
        copies.append(pltpu.make_async_copy(ready_ref.at[d], amp_hbm.at[pl.ds(d * rows, rows)], sems.at[d]))
        copies[-1].start()
    copies.append(pltpu.make_async_copy(pow_ref, pow_hbm, sems.at[dests + 1]))
    copies[-1].start()
    for copy in copies:
        copy.wait()


def expand_call(recv):
    segs, dests, lines, _ = recv.shape
    rows = 4
    modes = (lines - 8) // rows * 128
    return pl.pallas_call(
        expand_kernel,
        in_specs=[VMEM],
        out_specs=[HBM] * 3,
        out_shape=[
            jax.ShapeDtypeStruct((dests * rows, segs, modes), F32),
            jax.ShapeDtypeStruct((dests * rows // 2, modes), F32),
            jax.ShapeDtypeStruct((rows, segs, 256), F32),
        ],
        scratch_shapes=[
            pltpu.VMEM((2, lines // 8 - 1, 8 * segs, 128), F32),
            pltpu.VMEM((dests, rows, segs, modes), F32),
            pltpu.VMEM((dests * rows // 2, modes), F32),
            pltpu.VMEM((rows, segs, 256), F32),
            pltpu.SemaphoreType.DMA((dests + 2,)),
        ],
        compiler_params=pltpu.CompilerParams(vmem_limit_bytes=12 << 20),
        name="expand",
        cost_estimate=pl.CostEstimate(flops=1 << 21, bytes_accessed=3 << 20, transcendentals=0),
    )(recv)


def on_device(signal, mic_axial, mic_azimuth, mode_m, mode_n, freq_bins):
    segs = lax.axis_size("mic")
    owners = lax.axis_size("mode")
    freqs = freq_bins.shape[0]
    own = freqs // owners
    codes = lax.all_to_all(codes_call(mic_azimuth, mic_axial, segs), "mic", 0, 0, tiled=True)
    spectra = spectra_call(freq_bins, mode_m, mode_n, signal[0], owners)
    recv = lax.all_to_all(spectra, "mode", 0, 0, tiled=True)
    azim, seeds = basis_call(freq_bins, codes, owners)
    slots = solve_call(recv, azim, seeds, segs)
    shape = slots.shape
    slots = lax.all_to_all(slots.reshape(segs * owners, *shape[2:]), ("mic", "mode"), 0, 0, tiled=True)
    amplitude, power, residual = expand_call(slots.reshape(shape))
    modes = mode_m.shape[0]
    return (
        amplitude.reshape(freqs, 2, segs, modes),
        power,
        residual.reshape(own, 2, segs, residual.shape[2]),
    )


def solution(mesh):
    in_specs = (P("mic", "mode", None), P("mic"), P("mic"), P("mode"), P("mode"), P())
    out_specs = (P(None, None, None, "mode"), P(None, "mode"), P("mode", None, None, "mic"))
    return jax.shard_map(
        on_device, mesh=mesh, in_specs=in_specs, out_specs=out_specs, check_vma=False
    )
```

```python
import jax
import jax.numpy as jnp
from jax import lax
from jax.experimental import pallas as pl
from jax.experimental.pallas import tpu as pltpu
from jax.sharding import PartitionSpec as P

ITERS = 2
AXIAL = 64
NRAD = 32
ORDERS = 256
HALF = ORDERS // 2
EPS = 1e-06
SIN_COEFS = (1.5707963200919937, -0.6459637612912833, 0.07968992686556589, -0.0046741574942986315, 0.0001516785309118288)
BF16 = jnp.bfloat16
F32 = jnp.float32
VMEM = pl.BlockSpec(memory_space=pltpu.VMEM)
SMEM = pl.BlockSpec(memory_space=pltpu.SMEM)
HBM = pl.BlockSpec(memory_space=pltpu.HBM)


def cos_turns(turns):
    z = 1.0 - 4.0 * jnp.abs(turns - jnp.round(turns))
    square = z * z
    total = SIN_COEFS[-1] * square + SIN_COEFS[-2]
    for coef in SIN_COEFS[-3::-1]:
        total = total * square + coef
    return total * z


def sin_turns(turns):
    return cos_turns(turns - 0.25)


def turn_by(re, im, step_re, step_im):
    return re * step_re - im * step_im, re * step_im + im * step_re


def iota(shape, axis):
    return lax.broadcasted_iota(jnp.int32, shape, axis)


def nt_dot(a, b):
    return lax.dot_general(a, b, (((1,), (1,)), ((), ())), preferred_element_type=F32)


def groups(x):
    return x.reshape(x.shape[0] // 8, 8, x.shape[1])


def periodic(x):
    x = x + pltpu.roll(x, 4, 0)
    return x + pltpu.roll(x, 2, 0)


def codes_kernel(azimuth_hbm, axial_hbm, out_hbm, azimuth_ref, axial_ref, out_ref, sems):
    loads = [
        pltpu.make_async_copy(azimuth_hbm, azimuth_ref, sems.at[0]),
        pltpu.make_async_copy(axial_hbm, axial_ref, sems.at[1]),
    ]
    for load in loads:
        load.start()
    for load in loads:
        load.wait()
    code = azimuth_ref[...] * AXIAL + axial_ref[...]
    for copy in range(out_ref.shape[0]):
        out_ref[copy] = code
    store = pltpu.make_async_copy(out_ref, out_hbm, sems.at[2])
    store.start()
    store.wait()


def codes_call(azimuth, axial, copies):
    mics = azimuth.shape[0]
    return pl.pallas_call(
        codes_kernel,
        in_specs=[HBM] * 2,
        out_specs=HBM,
        out_shape=jax.ShapeDtypeStruct((copies, 1, mics), jnp.int32),
        scratch_shapes=[
            pltpu.VMEM((1, mics), jnp.int32),
            pltpu.VMEM((1, mics), jnp.int32),
            pltpu.VMEM((copies, 1, mics), jnp.int32),
            pltpu.SemaphoreType.DMA((3,)),
        ],
        name="codes",
        cost_estimate=pl.CostEstimate(flops=1 << 10, bytes_accessed=1 << 14, transcendentals=0),
    )(azimuth.reshape(1, -1), axial.reshape(1, -1))


def spectra_kernel(
    freq_hbm, m_hbm, n_hbm, signal_hbm, out_ref, freq_ref, m_ref, n_ref, analysis_ref, signal_ref, small_sems, sems
):
    loads = [
        pltpu.make_async_copy(freq_hbm, freq_ref, small_sems.at[0]),
        pltpu.make_async_copy(m_hbm, m_ref, small_sems.at[1]),
        pltpu.make_async_copy(n_hbm, n_ref, small_sems.at[2]),
    ]
    for load in loads:
        load.start()
    pieces, mics, span = signal_ref.shape
    copies = []
    for k in range(pieces):
        copies.append(pltpu.make_async_copy(signal_hbm.at[:, pl.ds(k * span, span)], signal_ref.at[k], sems.at[k]))
        copies[-1].start()
    for load in loads:
        load.wait()
    rows, seglen = analysis_ref.shape
    dests = out_ref.shape[0]
    freqs = rows // 2
    own = freqs // dests
    row = iota((freqs, 128), 0)
    freq = jnp.zeros((freqs, 128), jnp.int32)
    for f in range(freqs):
        freq = jnp.where(row == f, freq_ref[f], freq)
    freq = freq.astype(F32)
    lane = iota((freqs, 128), 1).astype(F32)
    start = freq * lane * (1.0 / seglen)
    step = freq * (128.0 / seglen)
    re, im = cos_turns(start), -sin_turns(start)
    step_re, step_im = cos_turns(step), -sin_turns(step)
    scale = (3.0 * seglen / 8.0) ** (-0.5)
    for block in range(seglen // 128):
        sample = iota((8, 128), 1).astype(F32) + block * 128.0
        window = (0.5 - 0.5 * cos_turns(sample * (1.0 / seglen)))[None] * scale
        at = slice(block * 128, (block + 1) * 128)
        analysis_ref[0:freqs, at] = (groups(re) * window).reshape(freqs, 128).astype(BF16)
        analysis_ref[freqs:, at] = (groups(im) * window).reshape(freqs, 128).astype(BF16)
        re, im = turn_by(re, im, step_re, step_im)

    m = m_ref[...]
    code = (jnp.where(m >= 0, m, HALF - 1 - m) * NRAD + n_ref[...]).astype(F32)
    tail = jnp.concatenate([code[:, :mics], code[:, mics:], jnp.zeros((2, mics), F32)], axis=0)
    for d in range(dests):
        out_ref[d, 2 * own :, :] = tail
    spectra = jnp.zeros((rows, mics), F32)
    for k in range(pieces):
        copies[k].wait()
        spectra = spectra + nt_dot(analysis_ref[:, k * span : (k + 1) * span], signal_ref[k])
    for d in range(dests):
        out_ref[d, 0:own, :] = spectra[d * own : (d + 1) * own]
        out_ref[d, own : 2 * own, :] = spectra[freqs + d * own : freqs + (d + 1) * own]


def spectra_call(freq_bins, mode_m, mode_n, signal, dests):
    mics, seglen = signal.shape
    modes = mode_m.shape[0]
    rows = 2 * freq_bins.shape[0]
    return pl.pallas_call(
        spectra_kernel,
        in_specs=[HBM] * 4,
        out_specs=VMEM,
        out_shape=jax.ShapeDtypeStruct((dests, 8, mics), F32),
        scratch_shapes=[
            pltpu.SMEM(freq_bins.shape, jnp.int32),
            pltpu.VMEM((1, modes), jnp.int32),
            pltpu.VMEM((1, modes), jnp.int32),
            pltpu.VMEM((rows, seglen), BF16),
            pltpu.VMEM((8, mics, seglen // 8), BF16),
            pltpu.SemaphoreType.DMA((3,)),
            pltpu.SemaphoreType.DMA((8,)),
        ],
        name="spectra",
        cost_estimate=pl.CostEstimate(flops=2 * rows * mics * seglen, bytes_accessed=mics * seglen * 2, transcendentals=0),
    )(freq_bins, mode_m.reshape(1, -1), mode_n.reshape(1, -1), signal)


def basis_kernel(freq_ref, code_ref, azim_ref, seed_ref):
    blocks, _, width = code_ref.shape
    chunks, _, per = azim_ref.shape
    base = 2 * lax.axis_index("mode")
    odd = (iota((8, width), 0) & 1) == 1
    freq = jnp.where(odd, freq_ref[base + 1], freq_ref[base]).astype(F32)
    row = iota((8, width), 0).astype(F32)
    radial = (iota((8, width), 0) >> 1).astype(F32)

    @pl.loop(0, chunks)
    def _(ch):
        for piece in range(per // width):
            at = slice(piece * width, (piece + 1) * width)
            code = jnp.broadcast_to(code_ref[ch * (per // width) + piece], (8, width))
            azimuth = (code >> 6).astype(F32)
            axial = (code & (AXIAL - 1)).astype(F32)
            turns = azimuth * (row + 0.5) * (1.0 / 512)
            re, im = cos_turns(turns), sin_turns(turns)
            turns = azimuth * (8.0 / 512)
            step_re, step_im = cos_turns(turns), sin_turns(turns)
            next_re, next_im = turn_by(re, im, step_re, step_im)
            step_re, step_im = turn_by(step_re, step_im, step_re, step_im)
            re = jnp.stack([re, next_re])
            im = jnp.stack([im, next_im])
            for a in range(HALF // 16):
                azim_ref[ch, 16 * a : 16 * a + 16, at] = re.reshape(16, width).astype(BF16)
                azim_ref[ch, HALF + 16 * a : HALF + 16 * a + 16, at] = im.reshape(16, width).astype(BF16)
                if a + 1 < HALF // 16:
                    re, im = turn_by(re, im, step_re[None], step_im[None])
            turns = (axial * freq * (2.0 * NRAD - radial) - azimuth * 32.0) * (1.0 / 32768)
            re, im = cos_turns(turns), sin_turns(turns)
            turns = axial * freq * (-4.0 / 32768)
            step_re, step_im = cos_turns(turns), sin_turns(turns)
            for k, value in enumerate((re, im, step_re, step_im)):
                seed_ref[ch, k, :, at] = value


def basis_call(freq_bins, codes, chunks):
    blocks, _, width = codes.shape
    per = blocks * width // chunks
    return pl.pallas_call(
        basis_kernel,
        in_specs=[SMEM, VMEM],
        out_specs=[VMEM] * 2,
        out_shape=[
            jax.ShapeDtypeStruct((chunks, ORDERS, per), BF16),
            jax.ShapeDtypeStruct((chunks, 4, 8, per), F32),
        ],
        compiler_params=pltpu.CompilerParams(vmem_limit_bytes=12 << 20),
        name="basis",
        cost_estimate=pl.CostEstimate(flops=40 * ORDERS * per * chunks, bytes_accessed=3 << 20, transcendentals=0),
    )(freq_bins, codes)


def solve_kernel(
    recv_ref, azim_ref, seed_ref, out_ref, rad_ref, res_ref, image_ref, field_ref, onehot_ref, dir_ref, grown_ref, rows_ref, pick_ref
):
    chunks, _, per = recv_ref.shape
    mics = chunks * per
    stack = 2 * NRAD
    odd = (iota((8, per), 0) & 1) == 1
    for ch in range(chunks):
        for c in range(2):
            res_ref[ch, c] = jnp.where(odd, recv_ref[ch, 2 * c + 1 : 2 * c + 2, :], recv_ref[ch, 2 * c : 2 * c + 1, :])

        re, im, step_re, step_im = (seed_ref[ch, k] for k in range(4))
        for a in range(stack // 8):
            rad_ref[ch, 0, 8 * a : 8 * a + 8] = re
            rad_ref[ch, 1, 8 * a : 8 * a + 8] = im
            if a + 1 < stack // 8:
                re, im = turn_by(re, im, step_re, step_im)

    low_rows = iota((HALF, 128), 0).astype(F32).astype(BF16)
    high_rows = (iota((2 * stack, 128), 0) >> 1).astype(F32).astype(BF16)
    one, zero = jnp.ones((), BF16), jnp.zeros((), BF16)
    counts = jnp.zeros((2 * stack, HALF), F32)

    def split_code(ch, part):
        code = recv_ref[ch, 4 + part : 5 + part, :]
        order = jnp.floor(code * (1.0 / NRAD))
        upper = order >= HALF
        return code - order * NRAD, jnp.where(upper, order - HALF, order), upper

    def modes_of(k):
        return jnp.concatenate([onehot_ref[k, q] for q in range(per // 128)], axis=1)

    for ch in range(chunks):
        for part in range(2):
            radius, low, upper = split_code(ch, part)
            high = jnp.where(upper, radius + NRAD, radius).astype(BF16)
            low = low.astype(BF16)
            picks = []
            for q in range(per // 128):
                at = slice(q * 128, (q + 1) * 128)
                onehot_ref[2 * ch + part, q] = jnp.where(low_rows == low[:, at], one, zero)
                picks.append(jnp.where(high_rows == high[:, at], one, zero))
            counts = counts + nt_dot(jnp.concatenate(picks, axis=1), modes_of(2 * ch + part))
    counts = jnp.concatenate([counts[:stack], counts[stack:]], axis=1)

    weight = (mics ** (-0.5)) * lax.rsqrt(1.0 + (iota((stack, ORDERS), 0) >> 1).astype(F32))
    counts_weight = counts * weight

    def scaled(column, x):
        return (column[None] * groups(x)).reshape(x.shape)

    def row_sums(x):
        return periodic(jnp.sum(jnp.sum(groups(x), axis=0), axis=1, keepdims=True))

    def adjoint(advance):
        out = jnp.zeros((2 * stack, ORDERS), F32)
        for ch in range(chunks):
            re, im = advance(ch, 0)[None], advance(ch, 1)[None]
            ec, es = groups(rad_ref[ch, 0]), groups(rad_ref[ch, 1])
            field_ref[ch, 0:stack] = (re * ec + im * es).reshape(stack, per).astype(BF16)
            field_ref[ch, stack:] = (im * ec - re * es).reshape(stack, per).astype(BF16)
            out = out + nt_dot(field_ref[ch], azim_ref[ch])
        re, im = out[:stack], out[stack:]
        rc, rs, ic, ics = re[:, :HALF], re[:, HALF:], im[:, :HALF], im[:, HALF:]
        g_re = jnp.concatenate([rc + ics, rc - ics], axis=1) * weight
        g_im = jnp.concatenate([ic - rs, ic + rs], axis=1) * weight
        return g_re, g_im, row_sums(counts * (g_re * g_re + g_im * g_im))

    def forward():
        x_re, x_im = dir_ref[0] * counts_weight, dir_ref[1] * counts_weight
        p_re, m_re, p_im, m_im = x_re[:, :HALF], x_re[:, HALF:], x_im[:, :HALF], x_im[:, HALF:]
        rows_ref[0:stack] = jnp.concatenate([p_re + m_re, m_im - p_im], axis=1).astype(BF16)
        rows_ref[stack:] = jnp.concatenate([p_im + m_im, p_re - m_re], axis=1).astype(BF16)
        norm = jnp.zeros((8, per), F32)
        for ch in range(chunks):
            out = jnp.dot(rows_ref[...], azim_ref[ch], preferred_element_type=F32)
            t_re, t_im = out[:stack], out[stack:]
            ec, es = rad_ref[ch, 0], rad_ref[ch, 1]
            i_re = periodic(jnp.sum(groups(ec * t_re - es * t_im), axis=0))
            i_im = periodic(jnp.sum(groups(ec * t_im + es * t_re), axis=0))
            image_ref[ch, 0] = i_re
            image_ref[ch, 1] = i_im
            norm = norm + (i_re * i_re + i_im * i_im)
        return jnp.sum(norm, axis=1, keepdims=True)

    g_re, g_im, norm = adjoint(lambda ch, c: res_ref[ch, c])
    dir_ref[0] = g_re
    dir_ref[1] = g_im
    for sweep in range(ITERS):
        step = norm / (forward() + EPS)

        def advance(ch, c, step=step):
            value = res_ref[ch, c] - step * image_ref[ch, c]
            res_ref[ch, c] = value
            return value

        for c in range(2):
            grown = scaled(step, dir_ref[c])
            grown_ref[c] = grown if sweep == 0 else grown_ref[c] + grown
        if sweep + 1 < ITERS:
            g_re, g_im, next_norm = adjoint(advance)
            momentum = next_norm / (norm + EPS)
            dir_ref[0] = g_re + scaled(momentum, dir_ref[0])
            dir_ref[1] = g_im + scaled(momentum, dir_ref[1])
            norm = next_norm

    copies, _, lines, _ = out_ref.shape
    width = mics // copies
    upper = (iota((8, per), 0) & 2) == 0
    first = iota((8, 128), 0) < 4
    for ch in range(chunks):
        value = jnp.where(upper, advance(ch, 0), advance(ch, 1))
        for piece in range(per // width):
            left, right = value[:, piece * width : piece * width + 128], value[:, piece * width + 128 : (piece + 1) * width]
            packed = jnp.where(first, left, right).astype(BF16)
            for owner in range(chunks):
                out_ref[ch * (per // width) + piece, owner, lines - 8 :, :] = packed

    for c in range(2):
        for half in range(2):
            begin = (2 * c + half) * stack
            pick_ref[begin : begin + stack] = grown_ref[c, :, half * HALF : (half + 1) * HALF].astype(BF16)
    radial_rows = (iota((stack, per), 0) >> 1).astype(F32)
    for ch in range(chunks):
        tiles = []
        for part in range(2):
            radius, _, minus = split_code(ch, part)
            picked = jnp.dot(pick_ref[...], modes_of(2 * ch + part), preferred_element_type=F32)
            mask = radial_rows == radius
            sides = []
            for c in range(2):
                plus_rows = picked[2 * c * stack : (2 * c + 1) * stack]
                minus_rows = picked[(2 * c + 1) * stack : (2 * c + 2) * stack]
                side = jnp.where(mask, jnp.where(minus, minus_rows, plus_rows), 0.0)
                sides.append(periodic(jnp.sum(groups(side), axis=0)))
            re, im = sides
            value = jnp.where(upper, re, im)
            for q in range(0, per // 128, 2):
                tiles.append(jnp.where(first, value[:, q * 128 : (q + 1) * 128], value[:, (q + 1) * 128 : (q + 2) * 128]))
        packed = jnp.concatenate(tiles, axis=0).astype(BF16)
        for copy in range(copies):
            out_ref[copy, ch, 0 : lines - 8, :] = packed


def solve_call(recv, azim, seeds, copies):
    chunks, _, per = recv.shape
    modes, stack = 2 * chunks * per, 2 * NRAD
    return pl.pallas_call(
        solve_kernel,
        in_specs=[VMEM] * 3,
        out_specs=VMEM,
        out_shape=jax.ShapeDtypeStruct((copies, chunks, 4 * modes // chunks // 128 + 8, 128), BF16),
        scratch_shapes=[
            pltpu.VMEM((chunks, 2, stack, per), F32),
            pltpu.VMEM((chunks, 2, 8, per), F32),
            pltpu.VMEM((chunks, 2, 8, per), F32),
            pltpu.VMEM((chunks, 2 * stack, per), BF16),
            pltpu.VMEM((2 * chunks, per // 128, HALF, 128), BF16),
            pltpu.VMEM((2, stack, ORDERS), F32),
            pltpu.VMEM((2, stack, ORDERS), F32),
            pltpu.VMEM((2 * stack, ORDERS), BF16),
            pltpu.VMEM((4 * stack, HALF), BF16),
        ],
        compiler_params=pltpu.CompilerParams(vmem_limit_bytes=14 << 20),
        name="solve",
        cost_estimate=pl.CostEstimate(flops=10 * 256 * 4096 * 128, bytes_accessed=8 << 20, transcendentals=0),
    )(recv, azim, seeds)


def expand_kernel(in_ref, amp_hbm, pow_hbm, res_hbm, wide_ref, ready_ref, pow_ref, res_ref, sems):
    segs, dests, lines, _ = in_ref.shape
    rows = 4
    tiles = lines // 8
    owner = lax.axis_index("mode")
    for s in range(segs):
        wide_ref[1, 0, 8 * s : 8 * s + 8, :] = in_ref[s, owner, 8 * (tiles - 1) :, :].astype(F32)
    for half in range(2):
        for fl in range(2):
            for c in range(2):
                line = half * rows + 2 * c + fl
                res_ref[2 * fl + c, :, half * 128 : (half + 1) * 128] = wide_ref[1, 0, pl.ds(line, segs, stride=8), :]
    copies = [pltpu.make_async_copy(res_ref, res_hbm, sems.at[dests])]
    copies[-1].start()
    for d in range(dests):
        for s in range(segs):
            for tile in range(tiles - 1):
                wide_ref[d % 2, tile, 8 * s : 8 * s + 8, :] = in_ref[s, d, 8 * tile : 8 * tile + 8, :].astype(F32)
        for kc in range(8 * (tiles - 1) // rows):
            at = slice(kc * 128, (kc + 1) * 128)
            for fl in range(rows // 2):
                power = jnp.zeros((segs, 128), F32)
                for c in range(2):
                    line = kc * rows + 2 * c + fl
                    value = wide_ref[d % 2, line // 8, pl.ds(line % 8, segs, stride=8), :]
                    ready_ref[d, 2 * fl + c, :, at] = value
                    power = power + value * value
                pow_ref[2 * d + fl : 2 * d + fl + 1, at] = jnp.sum(power, axis=0, keepdims=True) * (1.0 / segs)
        copies.append(pltpu.make_async_copy(ready_ref.at[d], amp_hbm.at[pl.ds(d * rows, rows)], sems.at[d]))
        copies[-1].start()
    copies.append(pltpu.make_async_copy(pow_ref, pow_hbm, sems.at[dests + 1]))
    copies[-1].start()
    for copy in copies:
        copy.wait()


def expand_call(recv):
    segs, dests, lines, _ = recv.shape
    rows = 4
    modes = (lines - 8) // rows * 128
    return pl.pallas_call(
        expand_kernel,
        in_specs=[VMEM],
        out_specs=[HBM] * 3,
        out_shape=[
            jax.ShapeDtypeStruct((dests * rows, segs, modes), F32),
            jax.ShapeDtypeStruct((dests * rows // 2, modes), F32),
            jax.ShapeDtypeStruct((rows, segs, 256), F32),
        ],
        scratch_shapes=[
            pltpu.VMEM((2, lines // 8 - 1, 8 * segs, 128), F32),
            pltpu.VMEM((dests, rows, segs, modes), F32),
            pltpu.VMEM((dests * rows // 2, modes), F32),
            pltpu.VMEM((rows, segs, 256), F32),
            pltpu.SemaphoreType.DMA((dests + 2,)),
        ],
        compiler_params=pltpu.CompilerParams(vmem_limit_bytes=12 << 20),
        name="expand",
        cost_estimate=pl.CostEstimate(flops=1 << 21, bytes_accessed=3 << 20, transcendentals=0),
    )(recv)


def on_device(signal, mic_axial, mic_azimuth, mode_m, mode_n, freq_bins):
    segs = lax.axis_size("mic")
    owners = lax.axis_size("mode")
    freqs = freq_bins.shape[0]
    own = freqs // owners
    codes = lax.all_to_all(codes_call(mic_azimuth, mic_axial, segs), "mic", 0, 0, tiled=True)
    spectra = spectra_call(freq_bins, mode_m, mode_n, signal[0], owners)
    recv = lax.all_to_all(spectra, "mode", 0, 0, tiled=True)
    azim, seeds = basis_call(freq_bins, codes, owners)
    slots = solve_call(recv, azim, seeds, segs)
    shape = slots.shape
    slots = lax.all_to_all(slots.reshape(segs * owners, *shape[2:]), ("mic", "mode"), 0, 0, tiled=True)
    amplitude, power, residual = expand_call(slots.reshape(shape))
    modes = mode_m.shape[0]
    return (
        amplitude.reshape(freqs, 2, segs, modes),
        power,
        residual.reshape(own, 2, segs, residual.shape[2]),
    )


def solution(mesh):
    in_specs = (P("mic", "mode", None), P("mic"), P("mic"), P("mode"), P("mode"), P())
    out_specs = (P(None, None, None, "mode"), P(None, "mode"), P("mode", None, None, "mic"))
    return jax.shard_map(
        on_device, mesh=mesh, in_specs=in_specs, out_specs=out_specs, check_vma=False
    )
```

```python
import jax
import jax.numpy as jnp
from jax import lax
from jax.experimental import pallas as pl
from jax.experimental.pallas import tpu as pltpu
from jax.sharding import PartitionSpec as P


ITERS = 2
AXIAL = 64
NRAD = 32
ORDERS = 256
HALF = ORDERS // 2
EPS = 1e-06
SIDE = 4
SIN_COEFS = (1.5707963200919937, -0.6459637612912833, 0.07968992686556589, -0.0046741574942986315, 0.0001516785309118288)
BF16 = jnp.bfloat16
F32 = jnp.float32
VMEM = pl.BlockSpec(memory_space=pltpu.VMEM)
SMEM = pl.BlockSpec(memory_space=pltpu.SMEM)
HBM = pl.BlockSpec(memory_space=pltpu.HBM)


def cos_turns(turns):
    z = 1.0 - 4.0 * jnp.abs(turns - jnp.round(turns))
    square = z * z
    total = SIN_COEFS[-1] * square + SIN_COEFS[-2]
    for coef in SIN_COEFS[-3::-1]:
        total = total * square + coef
    return total * z


def sin_turns(turns):
    return cos_turns(turns - 0.25)


def turn_by(re, im, step_re, step_im):
    return re * step_re - im * step_im, re * step_im + im * step_re


def iota(shape, axis):
    return lax.broadcasted_iota(jnp.int32, shape, axis)


def nt_dot(a, b):
    return lax.dot_general(a, b, (((1,), (1,)), ((), ())), preferred_element_type=F32)


def groups(x):
    return x.reshape(x.shape[0] // 8, 8, x.shape[1])


def periodic(x):
    x = x + pltpu.roll(x, 4, 0)
    return x + pltpu.roll(x, 2, 0)


def codes_kernel(azimuth_hbm, axial_hbm, out_hbm, azimuth_ref, axial_ref, out_ref, sems):
    loads = [
        pltpu.make_async_copy(azimuth_hbm, azimuth_ref, sems.at[0]),
        pltpu.make_async_copy(axial_hbm, axial_ref, sems.at[1]),
    ]
    for load in loads:
        load.start()
    for load in loads:
        load.wait()
    code = azimuth_ref[...] * AXIAL + axial_ref[...]
    for copy in range(out_ref.shape[0]):
        out_ref[copy] = code
    store = pltpu.make_async_copy(out_ref, out_hbm, sems.at[2])
    store.start()
    store.wait()


def codes_call(azimuth, axial, copies):
    mics = azimuth.shape[0]
    return pl.pallas_call(
        codes_kernel,
        in_specs=[HBM] * 2,
        out_specs=HBM,
        out_shape=jax.ShapeDtypeStruct((copies, 1, mics), jnp.int32),
        scratch_shapes=[
            pltpu.VMEM((1, mics), jnp.int32),
            pltpu.VMEM((1, mics), jnp.int32),
            pltpu.VMEM((copies, 1, mics), jnp.int32),
            pltpu.SemaphoreType.DMA((3,)),
        ],
        name="codes",
        cost_estimate=pl.CostEstimate(flops=1 << 10, bytes_accessed=1 << 14, transcendentals=0),
    )(azimuth.reshape(1, -1), axial.reshape(1, -1))


def spectra_kernel(
    freq_hbm, m_hbm, n_hbm, signal_hbm, out_ref, freq_ref, m_ref, n_ref, analysis_ref, signal_ref, small_sems, sems
):
    loads = [
        pltpu.make_async_copy(freq_hbm, freq_ref, small_sems.at[0]),
        pltpu.make_async_copy(m_hbm, m_ref, small_sems.at[1]),
        pltpu.make_async_copy(n_hbm, n_ref, small_sems.at[2]),
    ]
    for load in loads:
        load.start()
    pieces, mics, span = signal_ref.shape
    copies = []
    for k in range(pieces):
        copies.append(pltpu.make_async_copy(signal_hbm.at[:, pl.ds(k * span, span)], signal_ref.at[k], sems.at[k]))
        copies[-1].start()
    for load in loads:
        load.wait()
    rows, seglen = analysis_ref.shape
    dests = out_ref.shape[0]
    freqs = rows // 2
    own = freqs // dests
    row = iota((freqs, 128), 0)
    freq = jnp.zeros((freqs, 128), jnp.int32)
    for f in range(freqs):
        freq = jnp.where(row == f, freq_ref[f], freq)
    freq = freq.astype(F32)
    lane = iota((freqs, 128), 1).astype(F32)
    start = freq * lane * (1.0 / seglen)
    step = freq * (128.0 / seglen)
    re, im = cos_turns(start), -sin_turns(start)
    step_re, step_im = cos_turns(step), -sin_turns(step)
    scale = (3.0 * seglen / 8.0) ** (-0.5)
    for block in range(seglen // 128):
        sample = iota((8, 128), 1).astype(F32) + block * 128.0
        window = (0.5 - 0.5 * cos_turns(sample * (1.0 / seglen)))[None] * scale
        at = slice(block * 128, (block + 1) * 128)
        analysis_ref[0:freqs, at] = (groups(re) * window).reshape(freqs, 128).astype(BF16)
        analysis_ref[freqs:, at] = (groups(im) * window).reshape(freqs, 128).astype(BF16)
        re, im = turn_by(re, im, step_re, step_im)

    m = m_ref[...]
    code = (jnp.where(m >= 0, m, HALF - 1 - m) * NRAD + n_ref[...]).astype(F32)
    tail = jnp.concatenate([code[:, :mics], code[:, mics:], jnp.zeros((2, mics), F32)], axis=0)
    for d in range(dests):
        out_ref[d, 2 * own :, :] = tail
    spectra = jnp.zeros((rows, mics), F32)
    for k in range(pieces):
        copies[k].wait()
        spectra = spectra + nt_dot(analysis_ref[:, k * span : (k + 1) * span], signal_ref[k])
    for d in range(dests):
        out_ref[d, 0:own, :] = spectra[d * own : (d + 1) * own]
        out_ref[d, own : 2 * own, :] = spectra[freqs + d * own : freqs + (d + 1) * own]


def spectra_call(freq_bins, mode_m, mode_n, signal, dests):
    mics, seglen = signal.shape
    modes = mode_m.shape[0]
    rows = 2 * freq_bins.shape[0]
    return pl.pallas_call(
        spectra_kernel,
        in_specs=[HBM] * 4,
        out_specs=VMEM,
        out_shape=jax.ShapeDtypeStruct((dests, 8, mics), F32),
        scratch_shapes=[
            pltpu.SMEM(freq_bins.shape, jnp.int32),
            pltpu.VMEM((1, modes), jnp.int32),
            pltpu.VMEM((1, modes), jnp.int32),
            pltpu.VMEM((rows, seglen), BF16),
            pltpu.VMEM((8, mics, seglen // 8), BF16),
            pltpu.SemaphoreType.DMA((3,)),
            pltpu.SemaphoreType.DMA((8,)),
        ],
        name="spectra",
        cost_estimate=pl.CostEstimate(flops=2 * rows * mics * seglen, bytes_accessed=mics * seglen * 2, transcendentals=0),
    )(freq_bins, mode_m.reshape(1, -1), mode_n.reshape(1, -1), signal)


def basis_kernel(freq_ref, code_ref, azim_ref, seed_ref):
    _, _, width = code_ref.shape
    chunks, _, per = azim_ref.shape
    base = 2 * lax.axis_index("mode")
    odd = (iota((8, width), 0) & 1) == 1
    freq = jnp.where(odd, freq_ref[base + 1], freq_ref[base]).astype(F32)
    row = iota((8, width), 0).astype(F32)
    radial = (iota((8, width), 0) >> 1).astype(F32)

    @pl.loop(0, chunks)
    def _(ch):
        for piece in range(per // width):
            at = slice(piece * width, (piece + 1) * width)
            code = jnp.broadcast_to(code_ref[ch * (per // width) + piece], (8, width))
            azimuth = (code >> 6).astype(F32)
            axial = (code & (AXIAL - 1)).astype(F32)
            turns = azimuth * (row + 0.5) * (1.0 / 512)
            re, im = cos_turns(turns), sin_turns(turns)
            turns = azimuth * (8.0 / 512)
            step_re, step_im = cos_turns(turns), sin_turns(turns)
            next_re, next_im = turn_by(re, im, step_re, step_im)
            step_re, step_im = turn_by(step_re, step_im, step_re, step_im)
            re = jnp.stack([re, next_re])
            im = jnp.stack([im, next_im])
            for a in range(HALF // 16):
                azim_ref[ch, 16 * a : 16 * a + 16, at] = re.reshape(16, width).astype(BF16)
                azim_ref[ch, HALF + 16 * a : HALF + 16 * a + 16, at] = im.reshape(16, width).astype(BF16)
                if a + 1 < HALF // 16:
                    re, im = turn_by(re, im, step_re[None], step_im[None])
            turns = (axial * freq * (2.0 * NRAD - radial) - azimuth * 32.0) * (1.0 / 32768)
            re, im = cos_turns(turns), sin_turns(turns)
            turns = axial * freq * (-4.0 / 32768)
            step_re, step_im = cos_turns(turns), sin_turns(turns)
            for k, value in enumerate((re, im, step_re, step_im)):
                seed_ref[ch, k, :, at] = value


def basis_call(freq_bins, codes, chunks):
    blocks, _, width = codes.shape
    per = blocks * width // chunks
    return pl.pallas_call(
        basis_kernel,
        in_specs=[SMEM, VMEM],
        out_specs=[VMEM] * 2,
        out_shape=[
            jax.ShapeDtypeStruct((chunks, ORDERS, per), BF16),
            jax.ShapeDtypeStruct((chunks, 4, 8, per), F32),
        ],
        compiler_params=pltpu.CompilerParams(vmem_limit_bytes=12 << 20),
        name="basis",
        cost_estimate=pl.CostEstimate(flops=40 * ORDERS * per * chunks, bytes_accessed=3 << 20, transcendentals=0),
    )(freq_bins, codes)


def solve_kernel(
    recv_ref, azim_ref, seed_ref, out_hbm, *refs
):
    pack_refs, (rad_ref, res_ref, image_ref, field_ref, onehot_ref, dir_ref, grown_ref, rows_ref, pick_ref, out_ref, sems) = refs[:SIDE], refs[SIDE:]
    chunks, _, per = recv_ref.shape
    mics = chunks * per
    stack = 2 * NRAD
    odd = (iota((8, per), 0) & 1) == 1
    for ch in range(chunks):
        for c in range(2):
            res_ref[ch, c] = jnp.where(odd, recv_ref[ch, 2 * c + 1 : 2 * c + 2, :], recv_ref[ch, 2 * c : 2 * c + 1, :])

        re, im, step_re, step_im = (seed_ref[ch, k] for k in range(4))
        for a in range(stack // 8):
            rad_ref[ch, 0, 8 * a : 8 * a + 8] = re
            rad_ref[ch, 1, 8 * a : 8 * a + 8] = im
            if a + 1 < stack // 8:
                re, im = turn_by(re, im, step_re, step_im)

    low_rows = iota((HALF, 128), 0).astype(F32).astype(BF16)
    high_rows = (iota((2 * stack, 128), 0) >> 1).astype(F32).astype(BF16)
    one, zero = jnp.ones((), BF16), jnp.zeros((), BF16)
    counts = jnp.zeros((2 * stack, HALF), F32)

    def split_code(ch, part):
        code = recv_ref[ch, 4 + part : 5 + part, :]
        order = jnp.floor(code * (1.0 / NRAD))
        upper = order >= HALF
        return code - order * NRAD, jnp.where(upper, order - HALF, order), upper

    def modes_of(k):
        return jnp.concatenate([onehot_ref[k, q] for q in range(per // 128)], axis=1)

    for ch in range(chunks):
        for part in range(2):
            radius, low, upper = split_code(ch, part)
            high = jnp.where(upper, radius + NRAD, radius).astype(BF16)
            low = low.astype(BF16)
            picks = []
            for q in range(per // 128):
                at = slice(q * 128, (q + 1) * 128)
                onehot_ref[2 * ch + part, q] = jnp.where(low_rows == low[:, at], one, zero)
                picks.append(jnp.where(high_rows == high[:, at], one, zero))
            counts = counts + nt_dot(jnp.concatenate(picks, axis=1), modes_of(2 * ch + part))
    counts = jnp.concatenate([counts[:stack], counts[stack:]], axis=1)

    weight = (mics ** (-0.5)) * lax.rsqrt(1.0 + (iota((stack, ORDERS), 0) >> 1).astype(F32))
    counts_weight = counts * weight

    def scaled(column, x):
        return (column[None] * groups(x)).reshape(x.shape)

    def row_sums(x):
        return periodic(jnp.sum(jnp.sum(groups(x), axis=0), axis=1, keepdims=True))

    def adjoint(advance):
        out = jnp.zeros((2 * stack, ORDERS), F32)
        for ch in range(chunks):
            re, im = advance(ch, 0)[None], advance(ch, 1)[None]
            ec, es = groups(rad_ref[ch, 0]), groups(rad_ref[ch, 1])
            field_ref[ch, 0:stack] = (re * ec + im * es).reshape(stack, per).astype(BF16)
            field_ref[ch, stack:] = (im * ec - re * es).reshape(stack, per).astype(BF16)
            out = out + nt_dot(field_ref[ch], azim_ref[ch])
        re, im = out[:stack], out[stack:]
        rc, rs, ic, ics = re[:, :HALF], re[:, HALF:], im[:, :HALF], im[:, HALF:]
        g_re = jnp.concatenate([rc + ics, rc - ics], axis=1) * weight
        g_im = jnp.concatenate([ic - rs, ic + rs], axis=1) * weight
        return g_re, g_im, row_sums(counts * (g_re * g_re + g_im * g_im))

    def forward():
        x_re, x_im = dir_ref[0] * counts_weight, dir_ref[1] * counts_weight
        p_re, m_re, p_im, m_im = x_re[:, :HALF], x_re[:, HALF:], x_im[:, :HALF], x_im[:, HALF:]
        rows_ref[0:stack] = jnp.concatenate([p_re + m_re, m_im - p_im], axis=1).astype(BF16)
        rows_ref[stack:] = jnp.concatenate([p_im + m_im, p_re - m_re], axis=1).astype(BF16)
        norm = jnp.zeros((8, per), F32)
        for ch in range(chunks):
            out = jnp.dot(rows_ref[...], azim_ref[ch], preferred_element_type=F32)
            t_re, t_im = out[:stack], out[stack:]
            ec, es = rad_ref[ch, 0], rad_ref[ch, 1]
            i_re = periodic(jnp.sum(groups(ec * t_re - es * t_im), axis=0))
            i_im = periodic(jnp.sum(groups(ec * t_im + es * t_re), axis=0))
            image_ref[ch, 0] = i_re
            image_ref[ch, 1] = i_im
            norm = norm + (i_re * i_re + i_im * i_im)
        return jnp.sum(norm, axis=1, keepdims=True)

    g_re, g_im, norm = adjoint(lambda ch, c: res_ref[ch, c])
    dir_ref[0] = g_re
    dir_ref[1] = g_im
    for sweep in range(ITERS):
        step = norm / (forward() + EPS)

        def advance(ch, c, step=step):
            value = res_ref[ch, c] - step * image_ref[ch, c]
            res_ref[ch, c] = value
            return value

        for c in range(2):
            grown = scaled(step, dir_ref[c])
            grown_ref[c] = grown if sweep == 0 else grown_ref[c] + grown
        if sweep + 1 < ITERS:
            g_re, g_im, next_norm = adjoint(advance)
            momentum = next_norm / (norm + EPS)
            dir_ref[0] = g_re + scaled(momentum, dir_ref[0])
            dir_ref[1] = g_im + scaled(momentum, dir_ref[1])
            norm = next_norm

    copies = out_hbm.shape[0]
    width = mics // copies
    upper = (iota((8, per), 0) & 2) == 0
    first = iota((8, 128), 0) < 4
    here = lax.axis_index("mic") // SIDE
    for ch in range(chunks):
        advance(ch, 0)
        advance(ch, 1)
    for distance in range(SIDE):
        there = lax.rem(here + distance, SIDE)
        for y in range(SIDE):
            ch = (there * SIDE * width + (y * width // per) * per) // per
            at = slice(y * width % per, y * width % per + width)
            value = jnp.where(upper[:, at], res_ref[ch, 0, :, at], res_ref[ch, 1, :, at])
            pack_refs[distance][y] = value[0:4]

    for c in range(2):
        for half in range(2):
            begin = (2 * c + half) * stack
            pick_ref[begin : begin + stack] = grown_ref[c, :, half * HALF : (half + 1) * HALF].astype(BF16)
    radial_rows = (iota((stack, per), 0) >> 1).astype(F32)
    stores = []
    for ch in range(chunks):
        tiles = []
        for part in range(2):
            radius, _, minus = split_code(ch, part)
            picked = jnp.dot(pick_ref[...], modes_of(2 * ch + part), preferred_element_type=F32)
            mask = radial_rows == radius
            sides = []
            for c in range(2):
                plus_rows = picked[2 * c * stack : (2 * c + 1) * stack]
                minus_rows = picked[(2 * c + 1) * stack : (2 * c + 2) * stack]
                side = jnp.where(mask, jnp.where(minus, minus_rows, plus_rows), 0.0)
                sides.append(periodic(jnp.sum(groups(side), axis=0)))
            re, im = sides
            value = jnp.where(upper, re, im)
            for q in range(0, per // 128, 2):
                tiles.append(jnp.where(first, value[:, q * 128 : (q + 1) * 128], value[:, (q + 1) * 128 : (q + 2) * 128]))
        out_ref[ch] = jnp.concatenate(tiles, axis=0).astype(BF16)
        for copy in range(copies):
            stores.append(pltpu.make_async_copy(out_ref.at[ch], out_hbm.at[copy, ch], sems.at[ch, copy]))
            stores[-1].start()
    for store in stores:
        store.wait()


def solve_call(recv, azim, seeds, copies):
    chunks, _, per = recv.shape
    modes, stack = 2 * chunks * per, 2 * NRAD
    return pl.pallas_call(
        solve_kernel,
        in_specs=[VMEM] * 3,
        out_specs=[HBM] + [VMEM] * SIDE,
        out_shape=[jax.ShapeDtypeStruct((copies, chunks, 4 * modes // chunks // 128, 128), BF16)]
        + [jax.ShapeDtypeStruct((SIDE, 4, chunks * per // copies), F32)] * SIDE,
        scratch_shapes=[
            pltpu.VMEM((chunks, 2, stack, per), F32),
            pltpu.VMEM((chunks, 2, 8, per), F32),
            pltpu.VMEM((chunks, 2, 8, per), F32),
            pltpu.VMEM((chunks, 2 * stack, per), BF16),
            pltpu.VMEM((2 * chunks, per // 128, HALF, 128), BF16),
            pltpu.VMEM((2, stack, ORDERS), F32),
            pltpu.VMEM((2, stack, ORDERS), F32),
            pltpu.VMEM((2 * stack, ORDERS), BF16),
            pltpu.VMEM((4 * stack, HALF), BF16),
            pltpu.VMEM((chunks, 4 * modes // chunks // 128, 128), BF16),
            pltpu.SemaphoreType.DMA((chunks, copies)),
        ],
        compiler_params=pltpu.CompilerParams(vmem_limit_bytes=14 << 20),
        name="solve",
        cost_estimate=pl.CostEstimate(flops=10 * 256 * 4096 * 128, bytes_accessed=8 << 20, transcendentals=0),
    )(recv, azim, seeds)


def expand_kernel(in_ref, amp_hbm, pow_hbm, wide_ref, ready_ref, pow_ref, sems):
    segs, dests, lines, _ = in_ref.shape
    rows = 4
    tiles = lines // 8
    copies = []
    for d in range(dests):
        for s in range(segs):
            for tile in range(tiles):
                wide_ref[d % 2, tile, 8 * s : 8 * s + 8, :] = in_ref[s, d, 8 * tile : 8 * tile + 8, :].astype(F32)
        for kc in range(lines // rows):
            at = slice(kc * 128, (kc + 1) * 128)
            for fl in range(rows // 2):
                power = jnp.zeros((segs, 128), F32)
                for c in range(2):
                    line = kc * rows + 2 * c + fl
                    value = wide_ref[d % 2, line // 8, pl.ds(line % 8, segs, stride=8), :]
                    ready_ref[d, 2 * fl + c, :, at] = value
                    power = power + value * value
                pow_ref[2 * d + fl : 2 * d + fl + 1, at] = jnp.sum(power, axis=0, keepdims=True) * (1.0 / segs)
        copies.append(pltpu.make_async_copy(ready_ref.at[d], amp_hbm.at[pl.ds(d * rows, rows)], sems.at[d]))
        copies[-1].start()
    copies.append(pltpu.make_async_copy(pow_ref, pow_hbm, sems.at[dests]))
    copies[-1].start()
    for copy in copies:
        copy.wait()


def expand_call(recv):
    segs, dests, lines, _ = recv.shape
    rows = 4
    modes = lines // rows * 128
    return pl.pallas_call(
        expand_kernel,
        in_specs=[VMEM],
        out_specs=[HBM] * 2,
        out_shape=[
            jax.ShapeDtypeStruct((dests * rows, segs, modes), F32),
            jax.ShapeDtypeStruct((dests * rows // 2, modes), F32),
        ],
        scratch_shapes=[
            pltpu.VMEM((2, lines // 8, 8 * segs, 128), F32),
            pltpu.VMEM((dests, rows, segs, modes), F32),
            pltpu.VMEM((dests * rows // 2, modes), F32),
            pltpu.SemaphoreType.DMA((dests + 1,)),
        ],
        compiler_params=pltpu.CompilerParams(vmem_limit_bytes=12 << 20),
        name="expand",
        cost_estimate=pl.CostEstimate(flops=1 << 21, bytes_accessed=3 << 20, transcendentals=0),
    )(recv)


def repack_kernel(*refs):
    here = lax.rem(lax.axis_index("mic"), SIDE)
    for distance in range(SIDE):
        there = lax.rem(here + distance, SIDE)
        for k in range(SIDE):
            refs[SIDE + distance][k] = refs[k][there]


def repack_call(parts):
    return pl.pallas_call(
        repack_kernel,
        in_specs=[VMEM] * SIDE,
        out_specs=[VMEM] * SIDE,
        out_shape=[jax.ShapeDtypeStruct(parts[0].shape, F32)] * SIDE,
        compiler_params=pltpu.CompilerParams(vmem_limit_bytes=4 << 20),
        name="repack",
        cost_estimate=pl.CostEstimate(flops=0, bytes_accessed=1 << 17, transcendentals=0),
    )(*parts)


def turn_kernel(*refs):
    out_ref = refs[SIDE]
    rows, segs, width = out_ref.shape
    mic = lax.axis_index("mic")
    z, y = mic // SIDE, lax.rem(mic, SIDE)
    seg = iota((segs, width), 0)
    totals = [jnp.zeros((segs, width), F32)] * rows
    for dy in range(SIDE):
        for dz in range(SIDE):
            source = lax.rem(z + SIDE - dz, SIDE) * SIDE + lax.rem(y + SIDE - dy, SIDE)
            mask = seg == source
            value = refs[dy][dz]
            totals = [jnp.where(mask, value[k : k + 1], totals[k]) for k in range(rows)]
    for fl in range(2):
        for c in range(2):
            out_ref[2 * fl + c] = totals[2 * c + fl]


def turn_call(parts, segs):
    _, rows, width = parts[0].shape
    return pl.pallas_call(
        turn_kernel,
        in_specs=[VMEM] * SIDE,
        out_specs=VMEM,
        out_shape=jax.ShapeDtypeStruct((rows, segs, width), F32),
        compiler_params=pltpu.CompilerParams(vmem_limit_bytes=4 << 20),
        name="turn",
        cost_estimate=pl.CostEstimate(flops=0, bytes_accessed=1 << 17, transcendentals=0),
    )(*parts)


def on_device(signal, mic_axial, mic_azimuth, mode_m, mode_n, freq_bins):
    segs = lax.axis_size("mic")
    owners = lax.axis_size("mode")
    freqs = freq_bins.shape[0]
    own = freqs // owners
    codes = lax.all_to_all(codes_call(mic_azimuth, mic_axial, segs), "mic", 0, 0, tiled=True)
    spectra = spectra_call(freq_bins, mode_m, mode_n, signal[0], owners)
    recv = lax.all_to_all(spectra, "mode", 0, 0, tiled=True)
    azim, seeds = basis_call(freq_bins, codes, owners)
    slots, *parts = solve_call(recv, azim, seeds, segs)
    shape = slots.shape

    def along(distance, stride):
        pairs = []
        for source in range(segs):
            step = (source // stride + distance) % SIDE - source // stride % SIDE
            pairs.append((source, source + step * stride))
        return pairs

    slots = lax.all_to_all(slots.reshape(segs * owners, *shape[2:]), ("mic", "mode"), 0, 0, tiled=True)
    parts = [parts[0]] + [lax.ppermute(parts[d], "mic", along(d, SIDE)) for d in range(1, SIDE)]
    parts = repack_call(parts)
    parts = [parts[0]] + [lax.ppermute(parts[d], "mic", along(d, 1)) for d in range(1, SIDE)]
    residual = turn_call(parts, segs)
    amplitude, power = expand_call(slots.reshape(shape))
    modes = mode_m.shape[0]
    return (
        amplitude.reshape(freqs, 2, segs, modes),
        power,
        residual.reshape(own, 2, segs, residual.shape[2]),
    )


def solution(mesh):
    in_specs = (P("mic", "mode", None), P("mic"), P("mic"), P("mode"), P("mode"), P())
    out_specs = (P(None, None, None, "mode"), P(None, "mode"), P("mode", None, None, "mic"))
    return jax.shard_map(
        on_device, mesh=mesh, in_specs=in_specs, out_specs=out_specs, check_vma=False
    )
```

```python
import jax
import jax.numpy as jnp
from jax import lax
from jax.experimental import pallas as pl
from jax.experimental.pallas import tpu as pltpu
from jax.sharding import PartitionSpec as P

ITERS = 2
AXIAL = 64
NRAD = 32
ORDERS = 256
HALF = ORDERS // 2
EPS = 1e-06
SIN_COEFS = (1.5707963200919937, -0.6459637612912833, 0.07968992686556589, -0.0046741574942986315, 0.0001516785309118288)
BF16 = jnp.bfloat16
F32 = jnp.float32
VMEM = pl.BlockSpec(memory_space=pltpu.VMEM)
SMEM = pl.BlockSpec(memory_space=pltpu.SMEM)
HBM = pl.BlockSpec(memory_space=pltpu.HBM)


def cos_turns(turns):
    z = 1.0 - 4.0 * jnp.abs(turns - jnp.round(turns))
    square = z * z
    total = SIN_COEFS[-1] * square + SIN_COEFS[-2]
    for coef in SIN_COEFS[-3::-1]:
        total = total * square + coef
    return total * z


def sin_turns(turns):
    return cos_turns(turns - 0.25)


def turn_by(re, im, step_re, step_im):
    return re * step_re - im * step_im, re * step_im + im * step_re


def iota(shape, axis):
    return lax.broadcasted_iota(jnp.int32, shape, axis)


def nt_dot(a, b):
    return lax.dot_general(a, b, (((1,), (1,)), ((), ())), preferred_element_type=F32)


def groups(x):
    return x.reshape(x.shape[0] // 8, 8, x.shape[1])


def periodic(x):
    x = x + pltpu.roll(x, 4, 0)
    return x + pltpu.roll(x, 2, 0)


def codes_kernel(azimuth_hbm, axial_hbm, out_hbm, azimuth_ref, axial_ref, out_ref, sems):
    loads = [
        pltpu.make_async_copy(azimuth_hbm, azimuth_ref, sems.at[0]),
        pltpu.make_async_copy(axial_hbm, axial_ref, sems.at[1]),
    ]
    for load in loads:
        load.start()
    for load in loads:
        load.wait()
    code = azimuth_ref[...] * AXIAL + axial_ref[...]
    for copy in range(out_ref.shape[0]):
        out_ref[copy] = code
    store = pltpu.make_async_copy(out_ref, out_hbm, sems.at[2])
    store.start()
    store.wait()


def codes_call(azimuth, axial, copies):
    mics = azimuth.shape[0]
    return pl.pallas_call(
        codes_kernel,
        in_specs=[HBM] * 2,
        out_specs=HBM,
        out_shape=jax.ShapeDtypeStruct((copies, 1, mics), jnp.int32),
        scratch_shapes=[
            pltpu.VMEM((1, mics), jnp.int32),
            pltpu.VMEM((1, mics), jnp.int32),
            pltpu.VMEM((copies, 1, mics), jnp.int32),
            pltpu.SemaphoreType.DMA((3,)),
        ],
        name="codes",
        cost_estimate=pl.CostEstimate(flops=1 << 10, bytes_accessed=1 << 14, transcendentals=0),
    )(azimuth.reshape(1, -1), axial.reshape(1, -1))


def spectra_kernel(
    freq_hbm, m_hbm, n_hbm, signal_hbm, out_ref, freq_ref, m_ref, n_ref, analysis_ref, signal_ref, small_sems, sems
):
    loads = [
        pltpu.make_async_copy(freq_hbm, freq_ref, small_sems.at[0]),
        pltpu.make_async_copy(m_hbm, m_ref, small_sems.at[1]),
        pltpu.make_async_copy(n_hbm, n_ref, small_sems.at[2]),
    ]
    for load in loads:
        load.start()
    pieces, mics, span = signal_ref.shape
    copies = []
    for k in range(pieces):
        copies.append(pltpu.make_async_copy(signal_hbm.at[:, pl.ds(k * span, span)], signal_ref.at[k], sems.at[k]))
        copies[-1].start()
    for load in loads:
        load.wait()
    rows, seglen = analysis_ref.shape
    dests = out_ref.shape[0]
    freqs = rows // 2
    own = freqs // dests
    row = iota((freqs, 128), 0)
    freq = jnp.zeros((freqs, 128), jnp.int32)
    for f in range(freqs):
        freq = jnp.where(row == f, freq_ref[f], freq)
    freq = freq.astype(F32)
    lane = iota((freqs, 128), 1).astype(F32)
    start = freq * lane * (1.0 / seglen)
    step = freq * (128.0 / seglen)
    re, im = cos_turns(start), -sin_turns(start)
    step_re, step_im = cos_turns(step), -sin_turns(step)
    scale = (3.0 * seglen / 8.0) ** (-0.5)
    for block in range(seglen // 128):
        sample = iota((8, 128), 1).astype(F32) + block * 128.0
        window = (0.5 - 0.5 * cos_turns(sample * (1.0 / seglen)))[None] * scale
        at = slice(block * 128, (block + 1) * 128)
        analysis_ref[0:freqs, at] = (groups(re) * window).reshape(freqs, 128).astype(BF16)
        analysis_ref[freqs:, at] = (groups(im) * window).reshape(freqs, 128).astype(BF16)
        re, im = turn_by(re, im, step_re, step_im)

    m = m_ref[...]
    code = (jnp.where(m >= 0, m, HALF - 1 - m) * NRAD + n_ref[...]).astype(F32)
    tail = jnp.concatenate([code[:, :mics], code[:, mics:], jnp.zeros((2, mics), F32)], axis=0)
    for d in range(dests):
        out_ref[d, 2 * own :, :] = tail
    spectra = jnp.zeros((rows, mics), F32)
    for k in range(pieces):
        copies[k].wait()
        spectra = spectra + nt_dot(analysis_ref[:, k * span : (k + 1) * span], signal_ref[k])
    for d in range(dests):
        for k in range(2 * own):
            out_ref[d, k : k + 1, :] = spectra[k * dests + d : k * dests + d + 1]


def spectra_call(freq_bins, mode_m, mode_n, signal, dests):
    mics, seglen = signal.shape
    modes = mode_m.shape[0]
    rows = 2 * freq_bins.shape[0]
    return pl.pallas_call(
        spectra_kernel,
        in_specs=[HBM] * 4,
        out_specs=VMEM,
        out_shape=jax.ShapeDtypeStruct((dests, 8, mics), F32),
        scratch_shapes=[
            pltpu.SMEM(freq_bins.shape, jnp.int32),
            pltpu.VMEM((1, modes), jnp.int32),
            pltpu.VMEM((1, modes), jnp.int32),
            pltpu.VMEM((rows, seglen), BF16),
            pltpu.VMEM((8, mics, seglen // 8), BF16),
            pltpu.SemaphoreType.DMA((3,)),
            pltpu.SemaphoreType.DMA((8,)),
        ],
        name="spectra",
        cost_estimate=pl.CostEstimate(flops=2 * rows * mics * seglen, bytes_accessed=mics * seglen * 2, transcendentals=0),
    )(freq_bins, mode_m.reshape(1, -1), mode_n.reshape(1, -1), signal)


def basis_kernel(freq_ref, code_ref, azim_ref, seed_ref):
    blocks, _, width = code_ref.shape
    chunks, _, per = azim_ref.shape
    base = lax.axis_index("mode")
    odd = (iota((8, width), 0) & 1) == 1
    freq = jnp.where(odd, freq_ref[base + chunks], freq_ref[base]).astype(F32)
    row = iota((8, width), 0).astype(F32)
    radial = (iota((8, width), 0) >> 1).astype(F32)

    @pl.loop(0, chunks)
    def _(ch):
        for piece in range(per // width):
            at = slice(piece * width, (piece + 1) * width)
            code = jnp.broadcast_to(code_ref[ch * (per // width) + piece], (8, width))
            azimuth = (code >> 6).astype(F32)
            axial = (code & (AXIAL - 1)).astype(F32)
            turns = azimuth * (row + 0.5) * (1.0 / 512)
            re, im = cos_turns(turns), sin_turns(turns)
            turns = azimuth * (8.0 / 512)
            step_re, step_im = cos_turns(turns), sin_turns(turns)
            next_re, next_im = turn_by(re, im, step_re, step_im)
            step_re, step_im = turn_by(step_re, step_im, step_re, step_im)
            re = jnp.stack([re, next_re])
            im = jnp.stack([im, next_im])
            for a in range(HALF // 16):
                azim_ref[ch, 16 * a : 16 * a + 16, at] = re.reshape(16, width).astype(BF16)
                azim_ref[ch, HALF + 16 * a : HALF + 16 * a + 16, at] = im.reshape(16, width).astype(BF16)
                if a + 1 < HALF // 16:
                    re, im = turn_by(re, im, step_re[None], step_im[None])
            turns = (axial * freq * (2.0 * NRAD - radial) - azimuth * 32.0) * (1.0 / 32768)
            re, im = cos_turns(turns), sin_turns(turns)
            turns = axial * freq * (-4.0 / 32768)
            step_re, step_im = cos_turns(turns), sin_turns(turns)
            for k, value in enumerate((re, im, step_re, step_im)):
                seed_ref[ch, k, :, at] = value


def basis_call(freq_bins, codes, chunks):
    blocks, _, width = codes.shape
    per = blocks * width // chunks
    return pl.pallas_call(
        basis_kernel,
        in_specs=[SMEM, VMEM],
        out_specs=[VMEM] * 2,
        out_shape=[
            jax.ShapeDtypeStruct((chunks, ORDERS, per), BF16),
            jax.ShapeDtypeStruct((chunks, 4, 8, per), F32),
        ],
        compiler_params=pltpu.CompilerParams(vmem_limit_bytes=12 << 20),
        name="basis",
        cost_estimate=pl.CostEstimate(flops=40 * ORDERS * per * chunks, bytes_accessed=3 << 20, transcendentals=0),
    )(freq_bins, codes)


def solve_kernel(
    recv_ref, azim_ref, seed_ref, out_ref, rad_ref, res_ref, image_ref, field_ref, onehot_ref, dir_ref, grown_ref, rows_ref, pick_ref
):
    chunks, _, per = recv_ref.shape
    mics = chunks * per
    stack = 2 * NRAD
    odd = (iota((8, per), 0) & 1) == 1
    for ch in range(chunks):
        for c in range(2):
            res_ref[ch, c] = jnp.where(odd, recv_ref[ch, 2 * c + 1 : 2 * c + 2, :], recv_ref[ch, 2 * c : 2 * c + 1, :])

        re, im, step_re, step_im = (seed_ref[ch, k] for k in range(4))
        for a in range(stack // 8):
            rad_ref[ch, 0, 8 * a : 8 * a + 8] = re
            rad_ref[ch, 1, 8 * a : 8 * a + 8] = im
            if a + 1 < stack // 8:
                re, im = turn_by(re, im, step_re, step_im)

    low_rows = iota((HALF, 128), 0).astype(F32).astype(BF16)
    high_rows = (iota((2 * stack, 128), 0) >> 1).astype(F32).astype(BF16)
    one, zero = jnp.ones((), BF16), jnp.zeros((), BF16)
    counts = jnp.zeros((2 * stack, HALF), F32)

    def split_code(ch, part):
        code = recv_ref[ch, 4 + part : 5 + part, :]
        order = jnp.floor(code * (1.0 / NRAD))
        upper = order >= HALF
        return code - order * NRAD, jnp.where(upper, order - HALF, order), upper

    def modes_of(k):
        return jnp.concatenate([onehot_ref[k, q] for q in range(per // 128)], axis=1)

    for ch in range(chunks):
        for part in range(2):
            radius, low, upper = split_code(ch, part)
            high = jnp.where(upper, radius + NRAD, radius).astype(BF16)
            low = low.astype(BF16)
            picks = []
            for q in range(per // 128):
                at = slice(q * 128, (q + 1) * 128)
                onehot_ref[2 * ch + part, q] = jnp.where(low_rows == low[:, at], one, zero)
                picks.append(jnp.where(high_rows == high[:, at], one, zero))
            counts = counts + nt_dot(jnp.concatenate(picks, axis=1), modes_of(2 * ch + part))
    counts = jnp.concatenate([counts[:stack], counts[stack:]], axis=1)

    weight = (mics ** (-0.5)) * lax.rsqrt(1.0 + (iota((stack, ORDERS), 0) >> 1).astype(F32))
    counts_weight = counts * weight

    def scaled(column, x):
        return (column[None] * groups(x)).reshape(x.shape)

    def row_sums(x):
        return periodic(jnp.sum(jnp.sum(groups(x), axis=0), axis=1, keepdims=True))

    def adjoint(advance):
        out = jnp.zeros((2 * stack, ORDERS), F32)
        for ch in range(chunks):
            re, im = advance(ch, 0)[None], advance(ch, 1)[None]
            ec, es = groups(rad_ref[ch, 0]), groups(rad_ref[ch, 1])
            field_ref[ch, 0:stack] = (re * ec + im * es).reshape(stack, per).astype(BF16)
            field_ref[ch, stack:] = (im * ec - re * es).reshape(stack, per).astype(BF16)
            out = out + nt_dot(field_ref[ch], azim_ref[ch])
        re, im = out[:stack], out[stack:]
        rc, rs, ic, ics = re[:, :HALF], re[:, HALF:], im[:, :HALF], im[:, HALF:]
        g_re = jnp.concatenate([rc + ics, rc - ics], axis=1) * weight
        g_im = jnp.concatenate([ic - rs, ic + rs], axis=1) * weight
        return g_re, g_im, row_sums(counts * (g_re * g_re + g_im * g_im))

    def forward():
        x_re, x_im = dir_ref[0] * counts_weight, dir_ref[1] * counts_weight
        p_re, m_re, p_im, m_im = x_re[:, :HALF], x_re[:, HALF:], x_im[:, :HALF], x_im[:, HALF:]
        rows_ref[0:stack] = jnp.concatenate([p_re + m_re, m_im - p_im], axis=1).astype(BF16)
        rows_ref[stack:] = jnp.concatenate([p_im + m_im, p_re - m_re], axis=1).astype(BF16)
        norm = jnp.zeros((8, per), F32)
        for ch in range(chunks):
            out = jnp.dot(rows_ref[...], azim_ref[ch], preferred_element_type=F32)
            t_re, t_im = out[:stack], out[stack:]
            ec, es = rad_ref[ch, 0], rad_ref[ch, 1]
            i_re = periodic(jnp.sum(groups(ec * t_re - es * t_im), axis=0))
            i_im = periodic(jnp.sum(groups(ec * t_im + es * t_re), axis=0))
            image_ref[ch, 0] = i_re
            image_ref[ch, 1] = i_im
            norm = norm + (i_re * i_re + i_im * i_im)
        return jnp.sum(norm, axis=1, keepdims=True)

    g_re, g_im, norm = adjoint(lambda ch, c: res_ref[ch, c])
    dir_ref[0] = g_re
    dir_ref[1] = g_im
    for sweep in range(ITERS):
        step = norm / (forward() + EPS)

        def advance(ch, c, step=step):
            value = res_ref[ch, c] - step * image_ref[ch, c]
            res_ref[ch, c] = value
            return value

        for c in range(2):
            grown = scaled(step, dir_ref[c])
            grown_ref[c] = grown if sweep == 0 else grown_ref[c] + grown
        if sweep + 1 < ITERS:
            g_re, g_im, next_norm = adjoint(advance)
            momentum = next_norm / (norm + EPS)
            dir_ref[0] = g_re + scaled(momentum, dir_ref[0])
            dir_ref[1] = g_im + scaled(momentum, dir_ref[1])
            norm = next_norm

    copies, _, lines, _, _ = out_ref.shape
    width = mics // copies
    even = (iota((8, per), 0) & 1) == 0
    upper = (iota((8, per), 0) & 2) == 0
    first = iota((8, 128), 0) < 2
    for ch in range(chunks):
        re, im = advance(ch, 0), advance(ch, 1)
        sides = [jnp.where(even, re, pltpu.roll(im, 1, 0)), jnp.where(even, pltpu.roll(re, 7, 0), im)]
        for piece in range(per // width):
            for fl in range(2):
                left = sides[fl][:, piece * width : piece * width + 128]
                right = sides[fl][:, piece * width + 128 : (piece + 1) * width]
                packed = jnp.where(first, left, right)[0:4].astype(BF16)
                for owner in range(fl * chunks // 2, (fl + 1) * chunks // 2):
                    out_ref[ch * (per // width) + piece, owner, lines - 1] = packed

    for c in range(2):
        for half in range(2):
            begin = (2 * c + half) * stack
            pick_ref[begin : begin + stack] = grown_ref[c, :, half * HALF : (half + 1) * HALF].astype(BF16)
    radial_rows = (iota((stack, per), 0) >> 1).astype(F32)
    first = iota((8, 128), 0) < 4
    for ch in range(chunks):
        tiles = []
        for part in range(2):
            radius, _, minus = split_code(ch, part)
            picked = jnp.dot(pick_ref[...], modes_of(2 * ch + part), preferred_element_type=F32)
            mask = radial_rows == radius
            sides = []
            for c in range(2):
                plus_rows = picked[2 * c * stack : (2 * c + 1) * stack]
                minus_rows = picked[(2 * c + 1) * stack : (2 * c + 2) * stack]
                side = jnp.where(mask, jnp.where(minus, minus_rows, plus_rows), 0.0)
                sides.append(periodic(jnp.sum(groups(side), axis=0)))
            re, im = sides
            value = jnp.where(upper, re, im)
            for q in range(0, per // 128, 2):
                tiles.append(jnp.where(first, value[:, q * 128 : (q + 1) * 128], value[:, (q + 1) * 128 : (q + 2) * 128]))
        for k, tile in enumerate(tiles):
            for half in range(2):
                packed = tile[4 * half : 4 * half + 4].astype(BF16)
                for copy in range(copies):
                    out_ref[copy, ch, 2 * k + half] = packed


def solve_call(recv, azim, seeds, copies):
    chunks, _, per = recv.shape
    modes, stack = 2 * chunks * per, 2 * NRAD
    return pl.pallas_call(
        solve_kernel,
        in_specs=[VMEM] * 3,
        out_specs=VMEM,
        out_shape=jax.ShapeDtypeStruct((copies, chunks, modes // chunks // 128 + 1, 4, 128), BF16),
        scratch_shapes=[
            pltpu.VMEM((chunks, 2, stack, per), F32),
            pltpu.VMEM((chunks, 2, 8, per), F32),
            pltpu.VMEM((chunks, 2, 8, per), F32),
            pltpu.VMEM((chunks, 2 * stack, per), BF16),
            pltpu.VMEM((2 * chunks, per // 128, HALF, 128), BF16),
            pltpu.VMEM((2, stack, ORDERS), F32),
            pltpu.VMEM((2, stack, ORDERS), F32),
            pltpu.VMEM((2 * stack, ORDERS), BF16),
            pltpu.VMEM((4 * stack, HALF), BF16),
        ],
        compiler_params=pltpu.CompilerParams(vmem_limit_bytes=14 << 20),
        name="solve",
        cost_estimate=pl.CostEstimate(flops=10 * 256 * 4096 * 128, bytes_accessed=8 << 20, transcendentals=0),
    )(recv, azim, seeds)


def expand_kernel(in_ref, amp_hbm, pow_hbm, res_hbm, wide_ref, ready_ref, pow_ref, res_ref, sems):
    segs, dests, lines, rows, _ = in_ref.shape
    lines = lines - 1
    owner = lax.rem(2 * lax.axis_index("mode"), dests)
    for f in range(2):
        for s in range(segs):
            wide_ref[1, f, 8 * s : 8 * s + rows, :] = in_ref[s, owner + f, lines].astype(F32)
        for half in range(2):
            for c in range(2):
                value = wide_ref[1, f, pl.ds(2 * half + c, segs, stride=8), :]
                res_ref[2 * f + c, :, half * 128 : (half + 1) * 128] = value
    copies = [pltpu.make_async_copy(res_ref, res_hbm, sems.at[2 * dests])]
    copies[-1].start()
    for d in range(dests):
        for s in range(segs):
            for kc in range(lines):
                begin = 8 * s + rows * (kc % 2)
                wide_ref[d % 2, kc // 2, begin : begin + rows, :] = in_ref[s, d, kc].astype(F32)
        for kc in range(lines):
            at = slice(kc * 128, (kc + 1) * 128)
            for fl in range(rows // 2):
                power = jnp.zeros((segs, 128), F32)
                for c in range(2):
                    value = wide_ref[d % 2, kc // 2, pl.ds(rows * (kc % 2) + 2 * c + fl, segs, stride=8), :]
                    ready_ref[d, fl, c, :, at] = value
                    power = power + value * value
                f = d + fl * dests
                pow_ref[f : f + 1, at] = jnp.sum(power, axis=0, keepdims=True) * (1.0 / segs)
        for fl in range(rows // 2):
            f = d + fl * dests
            copies.append(pltpu.make_async_copy(ready_ref.at[d, fl], amp_hbm.at[pl.ds(2 * f, 2)], sems.at[2 * d + fl]))
            copies[-1].start()
    copies.append(pltpu.make_async_copy(pow_ref, pow_hbm, sems.at[2 * dests + 1]))
    copies[-1].start()
    for copy in copies:
        copy.wait()


def expand_call(recv):
    segs, dests, lines, rows, _ = recv.shape
    modes = (lines - 1) * 128
    return pl.pallas_call(
        expand_kernel,
        in_specs=[VMEM],
        out_specs=[HBM] * 3,
        out_shape=[
            jax.ShapeDtypeStruct((dests * rows, segs, modes), F32),
            jax.ShapeDtypeStruct((dests * rows // 2, modes), F32),
            jax.ShapeDtypeStruct((rows, segs, 256), F32),
        ],
        scratch_shapes=[
            pltpu.VMEM((2, (lines - 1) // 2, 8 * segs, 128), F32),
            pltpu.VMEM((dests, rows // 2, 2, segs, modes), F32),
            pltpu.VMEM((dests * rows // 2, modes), F32),
            pltpu.VMEM((rows, segs, 256), F32),
            pltpu.SemaphoreType.DMA((2 * dests + 2,)),
        ],
        compiler_params=pltpu.CompilerParams(vmem_limit_bytes=12 << 20),
        name="expand",
        cost_estimate=pl.CostEstimate(flops=1 << 21, bytes_accessed=3 << 20, transcendentals=0),
    )(recv)


def on_device(signal, mic_axial, mic_azimuth, mode_m, mode_n, freq_bins):
    segs = lax.axis_size("mic")
    owners = lax.axis_size("mode")
    freqs = freq_bins.shape[0]
    own = freqs // owners
    codes = lax.all_to_all(codes_call(mic_azimuth, mic_axial, segs), "mic", 0, 0, tiled=True)
    spectra = spectra_call(freq_bins, mode_m, mode_n, signal[0], owners)
    recv = lax.all_to_all(spectra, "mode", 0, 0, tiled=True)
    azim, seeds = basis_call(freq_bins, codes, owners)
    slots = solve_call(recv, azim, seeds, segs)
    shape = slots.shape
    slots = lax.all_to_all(slots.reshape(segs * owners, *shape[2:]), ("mic", "mode"), 0, 0, tiled=True)
    amplitude, power, residual = expand_call(slots.reshape(shape))
    modes = mode_m.shape[0]
    return (
        amplitude.reshape(freqs, 2, segs, modes),
        power,
        residual.reshape(own, 2, segs, residual.shape[2]),
    )


def solution(mesh):
    in_specs = (P("mic", "mode", None), P("mic"), P("mic"), P("mode"), P("mode"), P())
    out_specs = (P(None, None, None, "mode"), P(None, "mode"), P("mode", None, None, "mic"))
    return jax.shard_map(
        on_device, mesh=mesh, in_specs=in_specs, out_specs=out_specs, check_vma=False
    )
```

```python
import jax
import jax.numpy as jnp
from jax import lax
from jax.experimental import pallas as pl
from jax.experimental.pallas import tpu as pltpu
from jax.sharding import PartitionSpec as P

ITERS = 2
NRAD = 32
ORDERS = 256
HALF = ORDERS // 2
EPS = 1e-06
SIN_COEFS = (1.5707963200919937, -0.6459637612912833, 0.07968992686556589, -0.0046741574942986315, 0.0001516785309118288)
BF16 = jnp.bfloat16
F32 = jnp.float32
VMEM = pl.BlockSpec(memory_space=pltpu.VMEM)
SMEM = pl.BlockSpec(memory_space=pltpu.SMEM)
HBM = pl.BlockSpec(memory_space=pltpu.HBM)


def cos_turns(turns):
    z = 1.0 - 4.0 * jnp.abs(turns - jnp.round(turns))
    square = z * z
    total = SIN_COEFS[-1] * square + SIN_COEFS[-2]
    for coef in SIN_COEFS[-3::-1]:
        total = total * square + coef
    return total * z


def sin_turns(turns):
    return cos_turns(turns - 0.25)


def turn_by(re, im, step_re, step_im):
    return re * step_re - im * step_im, re * step_im + im * step_re


def iota(shape, axis):
    return lax.broadcasted_iota(jnp.int32, shape, axis)


def nt_dot(a, b):
    return lax.dot_general(a, b, (((1,), (1,)), ((), ())), preferred_element_type=F32)


def groups(x):
    return x.reshape(x.shape[0] // 8, 8, x.shape[1])


def periodic(x):
    x = x + pltpu.roll(x, 4, 0)
    return x + pltpu.roll(x, 2, 0)


def codes_kernel(azimuth_hbm, axial_hbm, out_hbm, sems):
    stores = []
    for copy in range(out_hbm.shape[0]):
        for k, source in enumerate((azimuth_hbm, axial_hbm)):
            stores.append(pltpu.make_async_copy(source, out_hbm.at[copy, k], sems.at[copy, k]))
            stores[-1].start()
    for store in stores:
        store.wait()


def codes_call(azimuth, axial, copies):
    mics = azimuth.shape[0]
    return pl.pallas_call(
        codes_kernel,
        in_specs=[HBM] * 2,
        out_specs=HBM,
        out_shape=jax.ShapeDtypeStruct((copies, 2, 1, mics), jnp.int32),
        scratch_shapes=[pltpu.SemaphoreType.DMA((copies, 2))],
        name="codes",
        cost_estimate=pl.CostEstimate(flops=1 << 10, bytes_accessed=1 << 14, transcendentals=0),
    )(azimuth.reshape(1, -1), axial.reshape(1, -1))


def spectra_kernel(
    freq_hbm, m_hbm, n_hbm, signal_hbm, out_ref, freq_ref, m_ref, n_ref, analysis_ref, signal_ref, small_sems, sems
):
    loads = [
        pltpu.make_async_copy(freq_hbm, freq_ref, small_sems.at[0]),
        pltpu.make_async_copy(m_hbm, m_ref, small_sems.at[1]),
        pltpu.make_async_copy(n_hbm, n_ref, small_sems.at[2]),
    ]
    for load in loads:
        load.start()
    pieces, mics, span = signal_ref.shape
    copies = []
    for k in range(pieces):
        copies.append(pltpu.make_async_copy(signal_hbm.at[:, pl.ds(k * span, span)], signal_ref.at[k], sems.at[k]))
        copies[-1].start()
    for load in loads:
        load.wait()
    rows, seglen = analysis_ref.shape
    dests = out_ref.shape[0]
    freqs = rows // 2
    own = freqs // dests
    row = iota((freqs, 128), 0)
    freq = jnp.zeros((freqs, 128), jnp.int32)
    for f in range(freqs):
        freq = jnp.where(row == f, freq_ref[f], freq)
    freq = freq.astype(F32)
    lane = iota((freqs, 128), 1).astype(F32)
    start = freq * lane * (1.0 / seglen)
    step = freq * (128.0 / seglen)
    re, im = cos_turns(start), -sin_turns(start)
    step_re, step_im = cos_turns(step), -sin_turns(step)
    scale = (3.0 * seglen / 8.0) ** (-0.5)
    for block in range(seglen // 128):
        sample = iota((8, 128), 1).astype(F32) + block * 128.0
        window = (0.5 - 0.5 * cos_turns(sample * (1.0 / seglen)))[None] * scale
        at = slice(block * 128, (block + 1) * 128)
        analysis_ref[0:freqs, at] = (groups(re) * window).reshape(freqs, 128).astype(BF16)
        analysis_ref[freqs:, at] = (groups(im) * window).reshape(freqs, 128).astype(BF16)
        re, im = turn_by(re, im, step_re, step_im)

    m = m_ref[...]
    code = (jnp.where(m >= 0, m, HALF - 1 - m) * NRAD + n_ref[...]).astype(F32)
    tail = jnp.concatenate([code[:, :mics], code[:, mics:], jnp.zeros((2, mics), F32)], axis=0)
    for d in range(dests):
        out_ref[d, 2 * own :, :] = tail
    spectra = jnp.zeros((rows, mics), F32)
    for k in range(pieces):
        copies[k].wait()
        spectra = spectra + nt_dot(analysis_ref[:, k * span : (k + 1) * span], signal_ref[k])
    for d in range(dests):
        for k in range(2 * own):
            out_ref[d, k : k + 1, :] = spectra[k * dests + d : k * dests + d + 1]


def spectra_call(freq_bins, mode_m, mode_n, signal, dests):
    mics, seglen = signal.shape
    modes = mode_m.shape[0]
    rows = 2 * freq_bins.shape[0]
    return pl.pallas_call(
        spectra_kernel,
        in_specs=[HBM] * 4,
        out_specs=VMEM,
        out_shape=jax.ShapeDtypeStruct((dests, 8, mics), F32),
        scratch_shapes=[
            pltpu.SMEM(freq_bins.shape, jnp.int32),
            pltpu.VMEM((1, modes), jnp.int32),
            pltpu.VMEM((1, modes), jnp.int32),
            pltpu.VMEM((rows, seglen), BF16),
            pltpu.VMEM((8, mics, seglen // 8), BF16),
            pltpu.SemaphoreType.DMA((3,)),
            pltpu.SemaphoreType.DMA((8,)),
        ],
        name="spectra",
        cost_estimate=pl.CostEstimate(flops=2 * rows * mics * seglen, bytes_accessed=mics * seglen * 2, transcendentals=0),
    )(freq_bins, mode_m.reshape(1, -1), mode_n.reshape(1, -1), signal)


def basis_kernel(freq_ref, code_ref, azim_ref, seed_ref):
    blocks, _, _, width = code_ref.shape
    chunks, _, per = azim_ref.shape
    base = lax.axis_index("mode")
    odd = (iota((8, width), 0) & 1) == 1
    freq = jnp.where(odd, freq_ref[base + chunks], freq_ref[base]).astype(F32)
    row = iota((8, width), 0).astype(F32)
    radial = (iota((8, width), 0) >> 1).astype(F32)

    @pl.loop(0, chunks)
    def _(ch):
        for piece in range(per // width):
            at = slice(piece * width, (piece + 1) * width)
            block = ch * (per // width) + piece
            azimuth = jnp.broadcast_to(code_ref[block, 0], (8, width)).astype(F32)
            axial = jnp.broadcast_to(code_ref[block, 1], (8, width)).astype(F32)
            turns = azimuth * (row + 0.5) * (1.0 / 512)
            re, im = cos_turns(turns), sin_turns(turns)
            turns = azimuth * (8.0 / 512)
            step_re, step_im = cos_turns(turns), sin_turns(turns)
            next_re, next_im = turn_by(re, im, step_re, step_im)
            step_re, step_im = turn_by(step_re, step_im, step_re, step_im)
            re = jnp.stack([re, next_re])
            im = jnp.stack([im, next_im])
            for a in range(HALF // 16):
                azim_ref[ch, 16 * a : 16 * a + 16, at] = re.reshape(16, width).astype(BF16)
                azim_ref[ch, HALF + 16 * a : HALF + 16 * a + 16, at] = im.reshape(16, width).astype(BF16)
                if a + 1 < HALF // 16:
                    re, im = turn_by(re, im, step_re[None], step_im[None])
            turns = (axial * freq * (2.0 * NRAD - radial) - azimuth * 32.0) * (1.0 / 32768)
            re, im = cos_turns(turns), sin_turns(turns)
            turns = axial * freq * (-4.0 / 32768)
            step_re, step_im = cos_turns(turns), sin_turns(turns)
            for k, value in enumerate((re, im, step_re, step_im)):
                seed_ref[ch, k, :, at] = value


def basis_call(freq_bins, codes, chunks):
    blocks, _, _, width = codes.shape
    per = blocks * width // chunks
    return pl.pallas_call(
        basis_kernel,
        in_specs=[SMEM, VMEM],
        out_specs=[VMEM] * 2,
        out_shape=[
            jax.ShapeDtypeStruct((chunks, ORDERS, per), BF16),
            jax.ShapeDtypeStruct((chunks, 4, 8, per), F32),
        ],
        compiler_params=pltpu.CompilerParams(vmem_limit_bytes=12 << 20),
        name="basis",
        cost_estimate=pl.CostEstimate(flops=40 * ORDERS * per * chunks, bytes_accessed=3 << 20, transcendentals=0),
    )(freq_bins, codes)


def solve_kernel(
    recv_ref, azim_ref, seed_ref, out_ref, rad_ref, res_ref, image_ref, field_ref, onehot_ref, dir_ref, grown_ref, rows_ref, pick_ref
):
    chunks, _, per = recv_ref.shape
    mics = chunks * per
    stack = 2 * NRAD
    odd = (iota((8, per), 0) & 1) == 1
    for ch in range(chunks):
        for c in range(2):
            res_ref[ch, c] = jnp.where(odd, recv_ref[ch, 2 * c + 1 : 2 * c + 2, :], recv_ref[ch, 2 * c : 2 * c + 1, :])

        re, im, step_re, step_im = (seed_ref[ch, k] for k in range(4))
        for a in range(stack // 8):
            rad_ref[ch, 0, 8 * a : 8 * a + 8] = re
            rad_ref[ch, 1, 8 * a : 8 * a + 8] = im
            if a + 1 < stack // 8:
                re, im = turn_by(re, im, step_re, step_im)

    low_rows = iota((HALF, 128), 0).astype(F32).astype(BF16)
    high_rows = (iota((2 * stack, 128), 0) >> 1).astype(F32).astype(BF16)
    one, zero = jnp.ones((), BF16), jnp.zeros((), BF16)
    counts = jnp.zeros((2 * stack, HALF), F32)

    def split_code(ch, part):
        code = recv_ref[ch, 4 + part : 5 + part, :]
        order = jnp.floor(code * (1.0 / NRAD))
        upper = order >= HALF
        return code - order * NRAD, jnp.where(upper, order - HALF, order), upper

    def modes_of(k):
        return jnp.concatenate([onehot_ref[k, q] for q in range(per // 128)], axis=1)

    for ch in range(chunks):
        for part in range(2):
            radius, low, upper = split_code(ch, part)
            high = jnp.where(upper, radius + NRAD, radius).astype(BF16)
            low = low.astype(BF16)
            picks = []
            for q in range(per // 128):
                at = slice(q * 128, (q + 1) * 128)
                onehot_ref[2 * ch + part, q] = jnp.where(low_rows == low[:, at], one, zero)
                picks.append(jnp.where(high_rows == high[:, at], one, zero))
            counts = counts + nt_dot(jnp.concatenate(picks, axis=1), modes_of(2 * ch + part))
    counts = jnp.concatenate([counts[:stack], counts[stack:]], axis=1)

    weight = (mics ** (-0.5)) * lax.rsqrt(1.0 + (iota((stack, ORDERS), 0) >> 1).astype(F32))
    counts_weight = counts * weight

    def scaled(column, x):
        return (column[None] * groups(x)).reshape(x.shape)

    def row_sums(x):
        return periodic(jnp.sum(jnp.sum(groups(x), axis=0), axis=1, keepdims=True))

    def adjoint(advance):
        out = jnp.zeros((2 * stack, ORDERS), F32)
        for ch in range(chunks):
            re, im = advance(ch, 0)[None], advance(ch, 1)[None]
            ec, es = groups(rad_ref[ch, 0]), groups(rad_ref[ch, 1])
            field_ref[ch, 0:stack] = (re * ec + im * es).reshape(stack, per).astype(BF16)
            field_ref[ch, stack:] = (im * ec - re * es).reshape(stack, per).astype(BF16)
            out = out + nt_dot(field_ref[ch], azim_ref[ch])
        re, im = out[:stack], out[stack:]
        rc, rs, ic, ics = re[:, :HALF], re[:, HALF:], im[:, :HALF], im[:, HALF:]
        g_re = jnp.concatenate([rc + ics, rc - ics], axis=1) * weight
        g_im = jnp.concatenate([ic - rs, ic + rs], axis=1) * weight
        return g_re, g_im, row_sums(counts * (g_re * g_re + g_im * g_im))

    def forward():
        x_re, x_im = dir_ref[0] * counts_weight, dir_ref[1] * counts_weight
        p_re, m_re, p_im, m_im = x_re[:, :HALF], x_re[:, HALF:], x_im[:, :HALF], x_im[:, HALF:]
        rows_ref[0:stack] = jnp.concatenate([p_re + m_re, m_im - p_im], axis=1).astype(BF16)
        rows_ref[stack:] = jnp.concatenate([p_im + m_im, p_re - m_re], axis=1).astype(BF16)
        norm = jnp.zeros((8, per), F32)
        for ch in range(chunks):
            out = jnp.dot(rows_ref[...], azim_ref[ch], preferred_element_type=F32)
            t_re, t_im = out[:stack], out[stack:]
            ec, es = rad_ref[ch, 0], rad_ref[ch, 1]
            i_re = periodic(jnp.sum(groups(ec * t_re - es * t_im), axis=0))
            i_im = periodic(jnp.sum(groups(ec * t_im + es * t_re), axis=0))
            image_ref[ch, 0] = i_re
            image_ref[ch, 1] = i_im
            norm = norm + (i_re * i_re + i_im * i_im)
        return jnp.sum(norm, axis=1, keepdims=True)

    g_re, g_im, norm = adjoint(lambda ch, c: res_ref[ch, c])
    dir_ref[0] = g_re
    dir_ref[1] = g_im
    for sweep in range(ITERS):
        step = norm / (forward() + EPS)

        def advance(ch, c, step=step):
            value = res_ref[ch, c] - step * image_ref[ch, c]
            res_ref[ch, c] = value
            return value

        for c in range(2):
            grown = scaled(step, dir_ref[c])
            grown_ref[c] = grown if sweep == 0 else grown_ref[c] + grown
        if sweep + 1 < ITERS:
            g_re, g_im, next_norm = adjoint(advance)
            momentum = next_norm / (norm + EPS)
            dir_ref[0] = g_re + scaled(momentum, dir_ref[0])
            dir_ref[1] = g_im + scaled(momentum, dir_ref[1])
            norm = next_norm

    copies, _, lines, _, _ = out_ref.shape
    width = mics // copies
    even = (iota((8, per), 0) & 1) == 0
    upper = (iota((8, per), 0) & 2) == 0
    first = iota((8, 128), 0) < 2
    for ch in range(chunks):
        re, im = advance(ch, 0), advance(ch, 1)
        sides = [jnp.where(even, re, pltpu.roll(im, 1, 0)), jnp.where(even, pltpu.roll(re, 7, 0), im)]
        for piece in range(per // width):
            for fl in range(2):
                left = sides[fl][:, piece * width : piece * width + 128]
                right = sides[fl][:, piece * width + 128 : (piece + 1) * width]
                packed = jnp.where(first, left, right)[0:4].astype(BF16)
                for owner in range(fl * chunks // 2, (fl + 1) * chunks // 2):
                    out_ref[ch * (per // width) + piece, owner, lines - 1] = packed

    for c in range(2):
        for half in range(2):
            begin = (2 * c + half) * stack
            pick_ref[begin : begin + stack] = grown_ref[c, :, half * HALF : (half + 1) * HALF].astype(BF16)
    radial_rows = (iota((stack, per), 0) >> 1).astype(F32)
    first = iota((8, 128), 0) < 4
    for ch in range(chunks):
        tiles = []
        for part in range(2):
            radius, _, minus = split_code(ch, part)
            picked = jnp.dot(pick_ref[...], modes_of(2 * ch + part), preferred_element_type=F32)
            mask = radial_rows == radius
            sides = []
            for c in range(2):
                plus_rows = picked[2 * c * stack : (2 * c + 1) * stack]
                minus_rows = picked[(2 * c + 1) * stack : (2 * c + 2) * stack]
                side = jnp.where(mask, jnp.where(minus, minus_rows, plus_rows), 0.0)
                sides.append(periodic(jnp.sum(groups(side), axis=0)))
            re, im = sides
            value = jnp.where(upper, re, im)
            for q in range(0, per // 128, 2):
                tiles.append(jnp.where(first, value[:, q * 128 : (q + 1) * 128], value[:, (q + 1) * 128 : (q + 2) * 128]))
        for k, tile in enumerate(tiles):
            for half in range(2):
                packed = tile[4 * half : 4 * half + 4].astype(BF16)
                for copy in range(copies):
                    out_ref[copy, ch, 2 * k + half] = packed


def solve_call(recv, azim, seeds, copies):
    chunks, _, per = recv.shape
    modes, stack = 2 * chunks * per, 2 * NRAD
    return pl.pallas_call(
        solve_kernel,
        in_specs=[VMEM] * 3,
        out_specs=VMEM,
        out_shape=jax.ShapeDtypeStruct((copies, chunks, modes // chunks // 128 + 1, 4, 128), BF16),
        scratch_shapes=[
            pltpu.VMEM((chunks, 2, stack, per), F32),
            pltpu.VMEM((chunks, 2, 8, per), F32),
            pltpu.VMEM((chunks, 2, 8, per), F32),
            pltpu.VMEM((chunks, 2 * stack, per), BF16),
            pltpu.VMEM((2 * chunks, per // 128, HALF, 128), BF16),
            pltpu.VMEM((2, stack, ORDERS), F32),
            pltpu.VMEM((2, stack, ORDERS), F32),
            pltpu.VMEM((2 * stack, ORDERS), BF16),
            pltpu.VMEM((4 * stack, HALF), BF16),
        ],
        compiler_params=pltpu.CompilerParams(vmem_limit_bytes=14 << 20),
        name="solve",
        cost_estimate=pl.CostEstimate(flops=10 * 256 * 4096 * 128, bytes_accessed=8 << 20, transcendentals=0),
    )(recv, azim, seeds)


def expand_kernel(in_ref, amp_hbm, pow_hbm, res_hbm, wide_ref, ready_ref, pow_ref, res_ref, sems):
    segs, dests, lines, rows, _ = in_ref.shape
    lines = lines - 1
    owner = lax.rem(2 * lax.axis_index("mode"), dests)
    for f in range(2):
        for s in range(segs):
            wide_ref[1, f, 8 * s : 8 * s + rows, :] = in_ref[s, owner + f, lines].astype(F32)
        for half in range(2):
            for c in range(2):
                value = wide_ref[1, f, pl.ds(2 * half + c, segs, stride=8), :]
                res_ref[2 * f + c, :, half * 128 : (half + 1) * 128] = value
    copies = [pltpu.make_async_copy(res_ref, res_hbm, sems.at[2 * dests])]
    copies[-1].start()
    for d in range(dests):
        for s in range(segs):
            for kc in range(lines):
                begin = 8 * s + rows * (kc % 2)
                wide_ref[d % 2, kc // 2, begin : begin + rows, :] = in_ref[s, d, kc].astype(F32)
        for kc in range(lines):
            at = slice(kc * 128, (kc + 1) * 128)
            for fl in range(rows // 2):
                power = jnp.zeros((segs, 128), F32)
                for c in range(2):
                    value = wide_ref[d % 2, kc // 2, pl.ds(rows * (kc % 2) + 2 * c + fl, segs, stride=8), :]
                    ready_ref[d, fl, c, :, at] = value
                    power = power + value * value
                f = d + fl * dests
                pow_ref[f : f + 1, at] = jnp.sum(power, axis=0, keepdims=True) * (1.0 / segs)
        for fl in range(rows // 2):
            f = d + fl * dests
            copies.append(pltpu.make_async_copy(ready_ref.at[d, fl], amp_hbm.at[pl.ds(2 * f, 2)], sems.at[2 * d + fl]))
            copies[-1].start()
    copies.append(pltpu.make_async_copy(pow_ref, pow_hbm, sems.at[2 * dests + 1]))
    copies[-1].start()
    for copy in copies:
        copy.wait()


def expand_call(recv):
    segs, dests, lines, rows, _ = recv.shape
    modes = (lines - 1) * 128
    return pl.pallas_call(
        expand_kernel,
        in_specs=[VMEM],
        out_specs=[HBM] * 3,
        out_shape=[
            jax.ShapeDtypeStruct((dests * rows, segs, modes), F32),
            jax.ShapeDtypeStruct((dests * rows // 2, modes), F32),
            jax.ShapeDtypeStruct((rows, segs, 256), F32),
        ],
        scratch_shapes=[
            pltpu.VMEM((2, (lines - 1) // 2, 8 * segs, 128), F32),
            pltpu.VMEM((dests, rows // 2, 2, segs, modes), F32),
            pltpu.VMEM((dests * rows // 2, modes), F32),
            pltpu.VMEM((rows, segs, 256), F32),
            pltpu.SemaphoreType.DMA((2 * dests + 2,)),
        ],
        compiler_params=pltpu.CompilerParams(vmem_limit_bytes=12 << 20),
        name="expand",
        cost_estimate=pl.CostEstimate(flops=1 << 21, bytes_accessed=3 << 20, transcendentals=0),
    )(recv)


def on_device(signal, mic_axial, mic_azimuth, mode_m, mode_n, freq_bins):
    segs = lax.axis_size("mic")
    owners = lax.axis_size("mode")
    freqs = freq_bins.shape[0]
    own = freqs // owners
    codes = lax.all_to_all(codes_call(mic_azimuth, mic_axial, segs), "mic", 0, 0, tiled=True)
    spectra = spectra_call(freq_bins, mode_m, mode_n, signal[0], owners)
    recv = lax.all_to_all(spectra, "mode", 0, 0, tiled=True)
    azim, seeds = basis_call(freq_bins, codes, owners)
    slots = solve_call(recv, azim, seeds, segs)
    shape = slots.shape
    slots = lax.all_to_all(slots.reshape(segs * owners, *shape[2:]), ("mic", "mode"), 0, 0, tiled=True)
    amplitude, power, residual = expand_call(slots.reshape(shape))
    modes = mode_m.shape[0]
    return (
        amplitude.reshape(freqs, 2, segs, modes),
        power,
        residual.reshape(own, 2, segs, residual.shape[2]),
    )


def solution(mesh):
    in_specs = (P("mic", "mode", None), P("mic"), P("mic"), P("mode"), P("mode"), P())
    out_specs = (P(None, None, None, "mode"), P(None, "mode"), P("mode", None, None, "mic"))
    return jax.shard_map(
        on_device, mesh=mesh, in_specs=in_specs, out_specs=out_specs, check_vma=False
    )
```

```python
import jax
import jax.numpy as jnp
from jax import lax
from jax.experimental import pallas as pl
from jax.experimental.pallas import tpu as pltpu
from jax.sharding import PartitionSpec as P

ITERS = 2
AXIAL = 64
NRAD = 32
ORDERS = 256
HALF = ORDERS // 2
EPS = 1e-06
SIN_COEFS = (1.5707963200919937, -0.6459637612912833, 0.07968992686556589, -0.0046741574942986315, 0.0001516785309118288)
BF16 = jnp.bfloat16
F32 = jnp.float32
VMEM = pl.BlockSpec(memory_space=pltpu.VMEM)
SMEM = pl.BlockSpec(memory_space=pltpu.SMEM)
HBM = pl.BlockSpec(memory_space=pltpu.HBM)


def cos_turns(turns):
    z = 1.0 - 4.0 * jnp.abs(turns - jnp.round(turns))
    square = z * z
    total = SIN_COEFS[-1] * square + SIN_COEFS[-2]
    for coef in SIN_COEFS[-3::-1]:
        total = total * square + coef
    return total * z


def sin_turns(turns):
    return cos_turns(turns - 0.25)


def turn_by(re, im, step_re, step_im):
    return re * step_re - im * step_im, re * step_im + im * step_re


def iota(shape, axis):
    return lax.broadcasted_iota(jnp.int32, shape, axis)


def nt_dot(a, b):
    return lax.dot_general(a, b, (((1,), (1,)), ((), ())), preferred_element_type=F32)


def groups(x):
    return x.reshape(x.shape[0] // 8, 8, x.shape[1])


def periodic(x):
    x = x + pltpu.roll(x, 4, 0)
    return x + pltpu.roll(x, 2, 0)


def codes_kernel(azimuth_hbm, axial_hbm, out_hbm, azimuth_ref, axial_ref, out_ref, sems):
    loads = [
        pltpu.make_async_copy(azimuth_hbm, azimuth_ref, sems.at[0]),
        pltpu.make_async_copy(axial_hbm, axial_ref, sems.at[1]),
    ]
    for load in loads:
        load.start()
    for load in loads:
        load.wait()
    code = azimuth_ref[...] * AXIAL + axial_ref[...]
    for copy in range(out_ref.shape[0]):
        out_ref[copy] = code
    store = pltpu.make_async_copy(out_ref, out_hbm, sems.at[2])
    store.start()
    store.wait()


def codes_call(azimuth, axial, copies):
    mics = azimuth.shape[0]
    return pl.pallas_call(
        codes_kernel,
        in_specs=[HBM] * 2,
        out_specs=HBM,
        out_shape=jax.ShapeDtypeStruct((copies, 1, mics), jnp.int32),
        scratch_shapes=[
            pltpu.VMEM((1, mics), jnp.int32),
            pltpu.VMEM((1, mics), jnp.int32),
            pltpu.VMEM((copies, 1, mics), jnp.int32),
            pltpu.SemaphoreType.DMA((3,)),
        ],
        name="codes",
        cost_estimate=pl.CostEstimate(flops=1 << 10, bytes_accessed=1 << 14, transcendentals=0),
    )(azimuth.reshape(1, -1), axial.reshape(1, -1))


def spectra_kernel(
    freq_hbm, m_hbm, n_hbm, signal_hbm, out_ref, freq_ref, m_ref, n_ref, analysis_ref, signal_ref, small_sems, sems
):
    loads = [
        pltpu.make_async_copy(freq_hbm, freq_ref, small_sems.at[0]),
        pltpu.make_async_copy(m_hbm, m_ref, small_sems.at[1]),
        pltpu.make_async_copy(n_hbm, n_ref, small_sems.at[2]),
    ]
    for load in loads:
        load.start()
    pieces, mics, span = signal_ref.shape
    copies = []
    for k in range(pieces):
        copies.append(pltpu.make_async_copy(signal_hbm.at[:, pl.ds(k * span, span)], signal_ref.at[k], sems.at[k]))
        copies[-1].start()
    for load in loads:
        load.wait()
    rows, seglen = analysis_ref.shape
    dests = out_ref.shape[0]
    freqs = rows // 2
    own = freqs // dests
    row = iota((freqs, 128), 0)
    freq = jnp.zeros((freqs, 128), jnp.int32)
    for f in range(freqs):
        freq = jnp.where(row == f, freq_ref[f], freq)
    freq = freq.astype(F32)
    lane = iota((freqs, 128), 1).astype(F32)
    start = freq * lane * (1.0 / seglen)
    step = freq * (128.0 / seglen)
    re, im = cos_turns(start), -sin_turns(start)
    step_re, step_im = cos_turns(step), -sin_turns(step)
    scale = (3.0 * seglen / 8.0) ** (-0.5)
    for block in range(seglen // 128):
        sample = iota((8, 128), 1).astype(F32) + block * 128.0
        window = (0.5 - 0.5 * cos_turns(sample * (1.0 / seglen)))[None] * scale
        at = slice(block * 128, (block + 1) * 128)
        analysis_ref[0:freqs, at] = (groups(re) * window).reshape(freqs, 128).astype(BF16)
        analysis_ref[freqs:, at] = (groups(im) * window).reshape(freqs, 128).astype(BF16)
        re, im = turn_by(re, im, step_re, step_im)

    m = m_ref[...]
    code = (jnp.where(m >= 0, m, HALF - 1 - m) * NRAD + n_ref[...]).astype(F32)
    tail = jnp.concatenate([code[:, :mics], code[:, mics:], jnp.zeros((2, mics), F32)], axis=0)
    for d in range(dests):
        out_ref[d, 2 * own :, :] = tail
    spectra = jnp.zeros((rows, mics), F32)
    for k in range(pieces):
        copies[k].wait()
        spectra = spectra + nt_dot(analysis_ref[:, k * span : (k + 1) * span], signal_ref[k])
    for d in range(dests):
        for k in range(2 * own):
            out_ref[d, k : k + 1, :] = spectra[k * dests + d : k * dests + d + 1]


def spectra_call(freq_bins, mode_m, mode_n, signal, dests):
    mics, seglen = signal.shape
    modes = mode_m.shape[0]
    rows = 2 * freq_bins.shape[0]
    return pl.pallas_call(
        spectra_kernel,
        in_specs=[HBM] * 4,
        out_specs=VMEM,
        out_shape=jax.ShapeDtypeStruct((dests, 8, mics), F32),
        scratch_shapes=[
            pltpu.SMEM(freq_bins.shape, jnp.int32),
            pltpu.VMEM((1, modes), jnp.int32),
            pltpu.VMEM((1, modes), jnp.int32),
            pltpu.VMEM((rows, seglen), BF16),
            pltpu.VMEM((8, mics, seglen // 8), BF16),
            pltpu.SemaphoreType.DMA((3,)),
            pltpu.SemaphoreType.DMA((8,)),
        ],
        name="spectra",
        cost_estimate=pl.CostEstimate(flops=2 * rows * mics * seglen, bytes_accessed=mics * seglen * 2, transcendentals=0),
    )(freq_bins, mode_m.reshape(1, -1), mode_n.reshape(1, -1), signal)


def basis_kernel(freq_ref, code_ref, azim_ref, early_ref, seed_ref):
    blocks, _, width = code_ref.shape
    chunks, _, per = azim_ref.shape
    base = lax.axis_index("mode")
    odd = (iota((8, width), 0) & 1) == 1
    freq = jnp.where(odd, freq_ref[base + chunks], freq_ref[base]).astype(F32)
    row = iota((8, width), 0).astype(F32)
    radial = (iota((8, width), 0) >> 1).astype(F32)

    early = early_ref.shape[0]

    def make(ch, whole):
        for piece in range(per // width):
            at = slice(piece * width, (piece + 1) * width)
            code = jnp.broadcast_to(code_ref[ch * (per // width) + piece], (8, width))
            azimuth = (code >> 6).astype(F32)
            axial = (code & (AXIAL - 1)).astype(F32)
            turns = azimuth * (row + 0.5) * (1.0 / 512)
            re, im = cos_turns(turns), sin_turns(turns)
            turns = azimuth * (8.0 / 512)
            step_re, step_im = cos_turns(turns), sin_turns(turns)
            next_re, next_im = turn_by(re, im, step_re, step_im)
            step_re, step_im = turn_by(step_re, step_im, step_re, step_im)
            re = jnp.stack([re, next_re])
            im = jnp.stack([im, next_im])
            for a in range(HALF // 16):
                azim_ref[ch, 16 * a : 16 * a + 16, at] = re.reshape(16, width).astype(BF16)
                azim_ref[ch, HALF + 16 * a : HALF + 16 * a + 16, at] = im.reshape(16, width).astype(BF16)
                if a + 1 < HALF // 16:
                    re, im = turn_by(re, im, step_re[None], step_im[None])
            turns = (axial * freq * (2.0 * NRAD - radial) - azimuth * 32.0) * (1.0 / 32768)
            re, im = cos_turns(turns), sin_turns(turns)
            turns = axial * freq * (-4.0 / 32768)
            step_re, step_im = cos_turns(turns), sin_turns(turns)
            if whole:
                for a in range(2 * NRAD // 8):
                    early_ref[ch, 0, 8 * a : 8 * a + 8, at] = re
                    early_ref[ch, 1, 8 * a : 8 * a + 8, at] = im
                    if a + 1 < 2 * NRAD // 8:
                        re, im = turn_by(re, im, step_re, step_im)
            else:
                for k, value in enumerate((re, im, step_re, step_im)):
                    seed_ref[ch - early, k, :, at] = value

    @pl.loop(0, early)
    def _(ch):
        make(ch, True)

    @pl.loop(early, chunks)
    def _(ch):
        make(ch, False)


def basis_call(freq_bins, codes, chunks):
    blocks, _, width = codes.shape
    per = blocks * width // chunks
    return pl.pallas_call(
        basis_kernel,
        in_specs=[SMEM, VMEM],
        out_specs=[VMEM] * 3,
        out_shape=[
            jax.ShapeDtypeStruct((chunks, ORDERS, per), BF16),
            jax.ShapeDtypeStruct((3 * chunks // 8, 2, 2 * NRAD, per), F32),
            jax.ShapeDtypeStruct((chunks - 3 * chunks // 8, 4, 8, per), F32),
        ],
        compiler_params=pltpu.CompilerParams(vmem_limit_bytes=12 << 20),
        name="basis",
        cost_estimate=pl.CostEstimate(flops=40 * ORDERS * per * chunks, bytes_accessed=3 << 20, transcendentals=0),
    )(freq_bins, codes)


def solve_kernel(
    recv_ref, azim_ref, early_ref, seed_ref, out_ref, late_ref, res_ref, image_ref, field_ref, onehot_ref, dir_ref, grown_ref, rows_ref, pick_ref
):
    chunks, _, per = recv_ref.shape
    mics = chunks * per
    stack = 2 * NRAD
    odd = (iota((8, per), 0) & 1) == 1
    early = early_ref.shape[0]

    def rad(ch, c):
        return early_ref[ch, c] if ch < early else late_ref[ch - early, c]

    for ch in range(chunks):
        for c in range(2):
            res_ref[ch, c] = jnp.where(odd, recv_ref[ch, 2 * c + 1 : 2 * c + 2, :], recv_ref[ch, 2 * c : 2 * c + 1, :])

        if ch < early:
            continue
        re, im, step_re, step_im = (seed_ref[ch - early, k] for k in range(4))
        for a in range(stack // 8):
            late_ref[ch - early, 0, 8 * a : 8 * a + 8] = re
            late_ref[ch - early, 1, 8 * a : 8 * a + 8] = im
            if a + 1 < stack // 8:
                re, im = turn_by(re, im, step_re, step_im)

    low_rows = iota((HALF, 128), 0).astype(F32).astype(BF16)
    high_rows = (iota((2 * stack, 128), 0) >> 1).astype(F32).astype(BF16)
    one, zero = jnp.ones((), BF16), jnp.zeros((), BF16)
    counts = jnp.zeros((2 * stack, HALF), F32)

    def split_code(ch, part):
        code = recv_ref[ch, 4 + part : 5 + part, :]
        order = jnp.floor(code * (1.0 / NRAD))
        upper = order >= HALF
        return code - order * NRAD, jnp.where(upper, order - HALF, order), upper

    def modes_of(k):
        return jnp.concatenate([onehot_ref[k, q] for q in range(per // 128)], axis=1)

    for ch in range(chunks):
        for part in range(2):
            radius, low, upper = split_code(ch, part)
            high = jnp.where(upper, radius + NRAD, radius).astype(BF16)
            low = low.astype(BF16)
            picks = []
            for q in range(per // 128):
                at = slice(q * 128, (q + 1) * 128)
                onehot_ref[2 * ch + part, q] = jnp.where(low_rows == low[:, at], one, zero)
                picks.append(jnp.where(high_rows == high[:, at], one, zero))
            counts = counts + nt_dot(jnp.concatenate(picks, axis=1), modes_of(2 * ch + part))
    counts = jnp.concatenate([counts[:stack], counts[stack:]], axis=1)

    weight = (mics ** (-0.5)) * lax.rsqrt(1.0 + (iota((stack, ORDERS), 0) >> 1).astype(F32))
    counts_weight = counts * weight

    def scaled(column, x):
        return (column[None] * groups(x)).reshape(x.shape)

    def row_sums(x):
        return periodic(jnp.sum(jnp.sum(groups(x), axis=0), axis=1, keepdims=True))

    def adjoint(advance):
        out = jnp.zeros((2 * stack, ORDERS), F32)
        for ch in range(chunks):
            re, im = advance(ch, 0)[None], advance(ch, 1)[None]
            ec, es = groups(rad(ch, 0)), groups(rad(ch, 1))
            field_ref[ch, 0:stack] = (re * ec + im * es).reshape(stack, per).astype(BF16)
            field_ref[ch, stack:] = (im * ec - re * es).reshape(stack, per).astype(BF16)
            out = out + nt_dot(field_ref[ch], azim_ref[ch])
        re, im = out[:stack], out[stack:]
        rc, rs, ic, ics = re[:, :HALF], re[:, HALF:], im[:, :HALF], im[:, HALF:]
        g_re = jnp.concatenate([rc + ics, rc - ics], axis=1) * weight
        g_im = jnp.concatenate([ic - rs, ic + rs], axis=1) * weight
        return g_re, g_im, row_sums(counts * (g_re * g_re + g_im * g_im))

    def forward():
        x_re, x_im = dir_ref[0] * counts_weight, dir_ref[1] * counts_weight
        p_re, m_re, p_im, m_im = x_re[:, :HALF], x_re[:, HALF:], x_im[:, :HALF], x_im[:, HALF:]
        rows_ref[0:stack] = jnp.concatenate([p_re + m_re, m_im - p_im], axis=1).astype(BF16)
        rows_ref[stack:] = jnp.concatenate([p_im + m_im, p_re - m_re], axis=1).astype(BF16)
        norm = jnp.zeros((8, per), F32)
        for ch in range(chunks):
            out = jnp.dot(rows_ref[...], azim_ref[ch], preferred_element_type=F32)
            t_re, t_im = out[:stack], out[stack:]
            ec, es = rad(ch, 0), rad(ch, 1)
            i_re = periodic(jnp.sum(groups(ec * t_re - es * t_im), axis=0))
            i_im = periodic(jnp.sum(groups(ec * t_im + es * t_re), axis=0))
            image_ref[ch, 0] = i_re
            image_ref[ch, 1] = i_im
            norm = norm + (i_re * i_re + i_im * i_im)
        return jnp.sum(norm, axis=1, keepdims=True)

    g_re, g_im, norm = adjoint(lambda ch, c: res_ref[ch, c])
    dir_ref[0] = g_re
    dir_ref[1] = g_im
    for sweep in range(ITERS):
        step = norm / (forward() + EPS)

        def advance(ch, c, step=step):
            value = res_ref[ch, c] - step * image_ref[ch, c]
            res_ref[ch, c] = value
            return value

        for c in range(2):
            grown = scaled(step, dir_ref[c])
            grown_ref[c] = grown if sweep == 0 else grown_ref[c] + grown
        if sweep + 1 < ITERS:
            g_re, g_im, next_norm = adjoint(advance)
            momentum = next_norm / (norm + EPS)
            dir_ref[0] = g_re + scaled(momentum, dir_ref[0])
            dir_ref[1] = g_im + scaled(momentum, dir_ref[1])
            norm = next_norm

    copies, _, lines, _, _ = out_ref.shape
    width = mics // copies
    even = (iota((8, per), 0) & 1) == 0
    upper = (iota((8, per), 0) & 2) == 0
    first = iota((8, 128), 0) < 2
    for ch in range(chunks):
        re, im = advance(ch, 0), advance(ch, 1)
        sides = [jnp.where(even, re, pltpu.roll(im, 1, 0)), jnp.where(even, pltpu.roll(re, 7, 0), im)]
        for piece in range(per // width):
            for fl in range(2):
                left = sides[fl][:, piece * width : piece * width + 128]
                right = sides[fl][:, piece * width + 128 : (piece + 1) * width]
                packed = jnp.where(first, left, right)[0:4].astype(BF16)
                for owner in range(fl * chunks // 2, (fl + 1) * chunks // 2):
                    out_ref[ch * (per // width) + piece, owner, lines - 1] = packed

    for c in range(2):
        for half in range(2):
            begin = (2 * c + half) * stack
            pick_ref[begin : begin + stack] = grown_ref[c, :, half * HALF : (half + 1) * HALF].astype(BF16)
    radial_rows = (iota((stack, per), 0) >> 1).astype(F32)
    first = iota((8, 128), 0) < 4
    for ch in range(chunks):
        tiles = []
        for part in range(2):
            radius, _, minus = split_code(ch, part)
            picked = jnp.dot(pick_ref[...], modes_of(2 * ch + part), preferred_element_type=F32)
            mask = radial_rows == radius
            sides = []
            for c in range(2):
                plus_rows = picked[2 * c * stack : (2 * c + 1) * stack]
                minus_rows = picked[(2 * c + 1) * stack : (2 * c + 2) * stack]
                side = jnp.where(mask, jnp.where(minus, minus_rows, plus_rows), 0.0)
                sides.append(periodic(jnp.sum(groups(side), axis=0)))
            re, im = sides
            value = jnp.where(upper, re, im)
            for q in range(0, per // 128, 2):
                tiles.append(jnp.where(first, value[:, q * 128 : (q + 1) * 128], value[:, (q + 1) * 128 : (q + 2) * 128]))
        for k, tile in enumerate(tiles):
            for half in range(2):
                packed = tile[4 * half : 4 * half + 4].astype(BF16)
                for copy in range(copies):
                    out_ref[copy, ch, 2 * k + half] = packed


def solve_call(recv, azim, early, seeds, copies):
    chunks, _, per = recv.shape
    modes, stack = 2 * chunks * per, 2 * NRAD
    return pl.pallas_call(
        solve_kernel,
        in_specs=[VMEM] * 4,
        out_specs=VMEM,
        out_shape=jax.ShapeDtypeStruct((copies, chunks, modes // chunks // 128 + 1, 4, 128), BF16),
        scratch_shapes=[
            pltpu.VMEM((chunks - 3 * chunks // 8, 2, stack, per), F32),
            pltpu.VMEM((chunks, 2, 8, per), F32),
            pltpu.VMEM((chunks, 2, 8, per), F32),
            pltpu.VMEM((chunks, 2 * stack, per), BF16),
            pltpu.VMEM((2 * chunks, per // 128, HALF, 128), BF16),
            pltpu.VMEM((2, stack, ORDERS), F32),
            pltpu.VMEM((2, stack, ORDERS), F32),
            pltpu.VMEM((2 * stack, ORDERS), BF16),
            pltpu.VMEM((4 * stack, HALF), BF16),
        ],
        compiler_params=pltpu.CompilerParams(vmem_limit_bytes=14 << 20),
        name="solve",
        cost_estimate=pl.CostEstimate(flops=10 * 256 * 4096 * 128, bytes_accessed=8 << 20, transcendentals=0),
    )(recv, azim, early, seeds)


def expand_kernel(in_ref, amp_hbm, pow_hbm, res_hbm, wide_ref, ready_ref, pow_ref, res_ref, sems):
    segs, dests, lines, rows, _ = in_ref.shape
    lines = lines - 1
    owner = lax.rem(2 * lax.axis_index("mode"), dests)
    for f in range(2):
        for s in range(segs):
            wide_ref[1, f, 8 * s : 8 * s + rows, :] = in_ref[s, owner + f, lines].astype(F32)
        for half in range(2):
            for c in range(2):
                value = wide_ref[1, f, pl.ds(2 * half + c, segs, stride=8), :]
                res_ref[2 * f + c, :, half * 128 : (half + 1) * 128] = value
    copies = [pltpu.make_async_copy(res_ref, res_hbm, sems.at[2 * dests])]
    copies[-1].start()
    for d in range(dests):
        for s in range(segs):
            for kc in range(lines):
                begin = 8 * s + rows * (kc % 2)
                wide_ref[d % 2, kc // 2, begin : begin + rows, :] = in_ref[s, d, kc].astype(F32)
        for kc in range(lines):
            at = slice(kc * 128, (kc + 1) * 128)
            for fl in range(rows // 2):
                power = jnp.zeros((segs, 128), F32)
                for c in range(2):
                    value = wide_ref[d % 2, kc // 2, pl.ds(rows * (kc % 2) + 2 * c + fl, segs, stride=8), :]
                    ready_ref[d, fl, c, :, at] = value
                    power = power + value * value
                f = d + fl * dests
                pow_ref[f : f + 1, at] = jnp.sum(power, axis=0, keepdims=True) * (1.0 / segs)
        for fl in range(rows // 2):
            f = d + fl * dests
            copies.append(pltpu.make_async_copy(ready_ref.at[d, fl], amp_hbm.at[pl.ds(2 * f, 2)], sems.at[2 * d + fl]))
            copies[-1].start()
    copies.append(pltpu.make_async_copy(pow_ref, pow_hbm, sems.at[2 * dests + 1]))
    copies[-1].start()
    for copy in copies:
        copy.wait()


def expand_call(recv):
    segs, dests, lines, rows, _ = recv.shape
    modes = (lines - 1) * 128
    return pl.pallas_call(
        expand_kernel,
        in_specs=[VMEM],
        out_specs=[HBM] * 3,
        out_shape=[
            jax.ShapeDtypeStruct((dests * rows, segs, modes), F32),
            jax.ShapeDtypeStruct((dests * rows // 2, modes), F32),
            jax.ShapeDtypeStruct((rows, segs, 256), F32),
        ],
        scratch_shapes=[
            pltpu.VMEM((2, (lines - 1) // 2, 8 * segs, 128), F32),
            pltpu.VMEM((dests, rows // 2, 2, segs, modes), F32),
            pltpu.VMEM((dests * rows // 2, modes), F32),
            pltpu.VMEM((rows, segs, 256), F32),
            pltpu.SemaphoreType.DMA((2 * dests + 2,)),
        ],
        compiler_params=pltpu.CompilerParams(vmem_limit_bytes=12 << 20),
        name="expand",
        cost_estimate=pl.CostEstimate(flops=1 << 21, bytes_accessed=3 << 20, transcendentals=0),
    )(recv)


def on_device(signal, mic_axial, mic_azimuth, mode_m, mode_n, freq_bins):
    segs = lax.axis_size("mic")
    owners = lax.axis_size("mode")
    freqs = freq_bins.shape[0]
    own = freqs // owners
    codes = lax.all_to_all(codes_call(mic_azimuth, mic_axial, segs), "mic", 0, 0, tiled=True)
    spectra = spectra_call(freq_bins, mode_m, mode_n, signal[0], owners)
    recv = lax.all_to_all(spectra, "mode", 0, 0, tiled=True)
    azim, early, seeds = basis_call(freq_bins, codes, owners)
    slots = solve_call(recv, azim, early, seeds, segs)
    shape = slots.shape
    slots = lax.all_to_all(slots.reshape(segs * owners, *shape[2:]), ("mic", "mode"), 0, 0, tiled=True)
    amplitude, power, residual = expand_call(slots.reshape(shape))
    modes = mode_m.shape[0]
    return (
        amplitude.reshape(freqs, 2, segs, modes),
        power,
        residual.reshape(own, 2, segs, residual.shape[2]),
    )


def solution(mesh):
    in_specs = (P("mic", "mode", None), P("mic"), P("mic"), P("mode"), P("mode"), P())
    out_specs = (P(None, None, None, "mode"), P(None, "mode"), P("mode", None, None, "mic"))
    return jax.shard_map(
        on_device, mesh=mesh, in_specs=in_specs, out_specs=out_specs, check_vma=False
    )
```

```python
import jax
import jax.numpy as jnp
from jax import lax
from jax.experimental import pallas as pl
from jax.experimental.pallas import tpu as pltpu
from jax.sharding import PartitionSpec as P

ITERS = 2
AXIAL = 64
NRAD = 32
ORDERS = 256
HALF = ORDERS // 2
EPS = 1e-06
SIN_COEFS = (1.5707963200919937, -0.6459637612912833, 0.07968992686556589, -0.0046741574942986315, 0.0001516785309118288)
BF16 = jnp.bfloat16
F32 = jnp.float32
VMEM = pl.BlockSpec(memory_space=pltpu.VMEM)
SMEM = pl.BlockSpec(memory_space=pltpu.SMEM)
HBM = pl.BlockSpec(memory_space=pltpu.HBM)


def cos_turns(turns):
    z = 1.0 - 4.0 * jnp.abs(turns - jnp.round(turns))
    square = z * z
    total = SIN_COEFS[-1] * square + SIN_COEFS[-2]
    for coef in SIN_COEFS[-3::-1]:
        total = total * square + coef
    return total * z


def sin_turns(turns):
    return cos_turns(turns - 0.25)


def turn_by(re, im, step_re, step_im):
    return re * step_re - im * step_im, re * step_im + im * step_re


def iota(shape, axis):
    return lax.broadcasted_iota(jnp.int32, shape, axis)


def nt_dot(a, b):
    return lax.dot_general(a, b, (((1,), (1,)), ((), ())), preferred_element_type=F32)


def groups(x):
    return x.reshape(x.shape[0] // 8, 8, x.shape[1])


def periodic(x):
    x = x + pltpu.roll(x, 4, 0)
    return x + pltpu.roll(x, 2, 0)


def codes_kernel(azimuth_hbm, axial_hbm, out_hbm, azimuth_ref, axial_ref, out_ref, sems):
    loads = [
        pltpu.make_async_copy(azimuth_hbm, azimuth_ref, sems.at[0]),
        pltpu.make_async_copy(axial_hbm, axial_ref, sems.at[1]),
    ]
    for load in loads:
        load.start()
    for load in loads:
        load.wait()
    code = azimuth_ref[...] * AXIAL + axial_ref[...]
    for copy in range(out_ref.shape[0]):
        out_ref[copy] = code
    store = pltpu.make_async_copy(out_ref, out_hbm, sems.at[2])
    store.start()
    store.wait()


def codes_call(azimuth, axial, copies):
    mics = azimuth.shape[0]
    return pl.pallas_call(
        codes_kernel,
        in_specs=[HBM] * 2,
        out_specs=HBM,
        out_shape=jax.ShapeDtypeStruct((copies, 1, mics), jnp.int32),
        scratch_shapes=[
            pltpu.VMEM((1, mics), jnp.int32),
            pltpu.VMEM((1, mics), jnp.int32),
            pltpu.VMEM((copies, 1, mics), jnp.int32),
            pltpu.SemaphoreType.DMA((3,)),
        ],
        name="codes",
        cost_estimate=pl.CostEstimate(flops=1 << 10, bytes_accessed=1 << 14, transcendentals=0),
    )(azimuth.reshape(1, -1), axial.reshape(1, -1))


def spectra_kernel(
    freq_hbm, m_hbm, n_hbm, signal_hbm, out_ref, freq_ref, m_ref, n_ref, analysis_ref, signal_ref, small_sems, sems
):
    loads = [
        pltpu.make_async_copy(freq_hbm, freq_ref, small_sems.at[0]),
        pltpu.make_async_copy(m_hbm, m_ref, small_sems.at[1]),
        pltpu.make_async_copy(n_hbm, n_ref, small_sems.at[2]),
    ]
    for load in loads:
        load.start()
    pieces, mics, span = signal_ref.shape
    copies = []
    for k in range(pieces):
        copies.append(pltpu.make_async_copy(signal_hbm.at[:, pl.ds(k * span, span)], signal_ref.at[k], sems.at[k]))
        copies[-1].start()
    for load in loads:
        load.wait()
    rows, seglen = analysis_ref.shape
    dests = out_ref.shape[0]
    freqs = rows // 2
    own = freqs // dests
    row = iota((freqs, 128), 0)
    freq = jnp.zeros((freqs, 128), jnp.int32)
    for f in range(freqs):
        freq = jnp.where(row == f, freq_ref[f], freq)
    freq = freq.astype(F32)
    lane = iota((freqs, 128), 1).astype(F32)
    start = freq * lane * (1.0 / seglen)
    step = freq * (128.0 / seglen)
    re, im = cos_turns(start), -sin_turns(start)
    step_re, step_im = cos_turns(step), -sin_turns(step)
    scale = (3.0 * seglen / 8.0) ** (-0.5)
    for block in range(seglen // 128):
        sample = iota((8, 128), 1).astype(F32) + block * 128.0
        window = (0.5 - 0.5 * cos_turns(sample * (1.0 / seglen)))[None] * scale
        at = slice(block * 128, (block + 1) * 128)
        analysis_ref[0:freqs, at] = (groups(re) * window).reshape(freqs, 128).astype(BF16)
        analysis_ref[freqs:, at] = (groups(im) * window).reshape(freqs, 128).astype(BF16)
        re, im = turn_by(re, im, step_re, step_im)

    m = m_ref[...]
    code = (jnp.where(m >= 0, m, HALF - 1 - m) * NRAD + n_ref[...]).astype(F32)
    tail = jnp.concatenate([code[:, :mics], code[:, mics:], jnp.zeros((2, mics), F32)], axis=0)
    for d in range(dests):
        out_ref[d, 2 * own :, :] = tail
    spectra = jnp.zeros((rows, mics), F32)
    for k in range(pieces):
        copies[k].wait()
        spectra = spectra + nt_dot(analysis_ref[:, k * span : (k + 1) * span], signal_ref[k])
    for d in range(dests):
        for k in range(2 * own):
            out_ref[d, k : k + 1, :] = spectra[k * dests + d : k * dests + d + 1]


def spectra_call(freq_bins, mode_m, mode_n, signal, dests):
    mics, seglen = signal.shape
    modes = mode_m.shape[0]
    rows = 2 * freq_bins.shape[0]
    return pl.pallas_call(
        spectra_kernel,
        in_specs=[HBM] * 4,
        out_specs=VMEM,
        out_shape=jax.ShapeDtypeStruct((dests, 8, mics), F32),
        scratch_shapes=[
            pltpu.SMEM(freq_bins.shape, jnp.int32),
            pltpu.VMEM((1, modes), jnp.int32),
            pltpu.VMEM((1, modes), jnp.int32),
            pltpu.VMEM((rows, seglen), BF16),
            pltpu.VMEM((8, mics, seglen // 8), BF16),
            pltpu.SemaphoreType.DMA((3,)),
            pltpu.SemaphoreType.DMA((8,)),
        ],
        name="spectra",
        cost_estimate=pl.CostEstimate(flops=2 * rows * mics * seglen, bytes_accessed=mics * seglen * 2, transcendentals=0),
    )(freq_bins, mode_m.reshape(1, -1), mode_n.reshape(1, -1), signal)


def basis_kernel(freq_ref, code_ref, azim_ref, early_ref, seed_ref):
    blocks, _, width = code_ref.shape
    chunks, _, per = azim_ref.shape
    base = lax.axis_index("mode")
    odd = (iota((8, width), 0) & 1) == 1
    freq = jnp.where(odd, freq_ref[base + chunks], freq_ref[base]).astype(F32)
    row = iota((8, width), 0).astype(F32)
    radial = (iota((8, width), 0) >> 1).astype(F32)

    early = early_ref.shape[0]

    def make(ch, whole):
        for piece in range(per // width):
            at = slice(piece * width, (piece + 1) * width)
            code = jnp.broadcast_to(code_ref[ch * (per // width) + piece], (8, width))
            azimuth = (code >> 6).astype(F32)
            axial = (code & (AXIAL - 1)).astype(F32)
            turns = azimuth * (row + 0.5) * (1.0 / 512)
            re, im = cos_turns(turns), sin_turns(turns)
            turns = azimuth * (8.0 / 512)
            step_re, step_im = cos_turns(turns), sin_turns(turns)
            next_re, next_im = turn_by(re, im, step_re, step_im)
            step_re, step_im = turn_by(step_re, step_im, step_re, step_im)
            re = jnp.stack([re, next_re])
            im = jnp.stack([im, next_im])
            for a in range(HALF // 16):
                azim_ref[ch, 16 * a : 16 * a + 16, at] = re.reshape(16, width).astype(BF16)
                azim_ref[ch, HALF + 16 * a : HALF + 16 * a + 16, at] = im.reshape(16, width).astype(BF16)
                if a + 1 < HALF // 16:
                    re, im = turn_by(re, im, step_re[None], step_im[None])
            turns = (axial * freq * (2.0 * NRAD - radial) - azimuth * 32.0) * (1.0 / 32768)
            re, im = cos_turns(turns), sin_turns(turns)
            turns = axial * freq * (-4.0 / 32768)
            step_re, step_im = cos_turns(turns), sin_turns(turns)
            if whole:
                for a in range(2 * NRAD // 8):
                    early_ref[ch, 0, 8 * a : 8 * a + 8, at] = re
                    early_ref[ch, 1, 8 * a : 8 * a + 8, at] = im
                    if a + 1 < 2 * NRAD // 8:
                        re, im = turn_by(re, im, step_re, step_im)
            else:
                for k, value in enumerate((re, im, step_re, step_im)):
                    seed_ref[ch - early, k, :, at] = value

    @pl.loop(0, early)
    def _(ch):
        make(ch, True)

    @pl.loop(early, chunks)
    def _(ch):
        make(ch, False)


def basis_call(freq_bins, codes, chunks):
    blocks, _, width = codes.shape
    per = blocks * width // chunks
    return pl.pallas_call(
        basis_kernel,
        in_specs=[SMEM, VMEM],
        out_specs=[VMEM] * 3,
        out_shape=[
            jax.ShapeDtypeStruct((chunks, ORDERS, per), BF16),
            jax.ShapeDtypeStruct((3 * chunks // 8, 2, 2 * NRAD, per), F32),
            jax.ShapeDtypeStruct((chunks - 3 * chunks // 8, 4, 8, per), F32),
        ],
        compiler_params=pltpu.CompilerParams(vmem_limit_bytes=12 << 20),
        name="basis",
        cost_estimate=pl.CostEstimate(flops=40 * ORDERS * per * chunks, bytes_accessed=3 << 20, transcendentals=0),
    )(freq_bins, codes)


def solve_kernel(
    recv_ref, azim_ref, early_ref, seed_ref, out_ref, late_ref, res_ref, image_ref, field_ref, onehot_ref, dir_ref, grown_ref, rows_ref, pick_ref
):
    chunks, _, per = recv_ref.shape
    mics = chunks * per
    stack = 2 * NRAD
    odd = (iota((8, per), 0) & 1) == 1
    early = early_ref.shape[0]

    def rad(ch, c):
        return early_ref[ch, c] if ch < early else late_ref[ch - early, c]

    for ch in range(chunks):
        for c in range(2):
            res_ref[ch, c] = jnp.where(odd, recv_ref[ch, 2 * c + 1 : 2 * c + 2, :], recv_ref[ch, 2 * c : 2 * c + 1, :])

        if ch < early:
            continue
        re, im, step_re, step_im = (seed_ref[ch - early, k] for k in range(4))
        for a in range(stack // 8):
            late_ref[ch - early, 0, 8 * a : 8 * a + 8] = re
            late_ref[ch - early, 1, 8 * a : 8 * a + 8] = im
            if a + 1 < stack // 8:
                re, im = turn_by(re, im, step_re, step_im)

    low_rows = iota((HALF, 128), 0).astype(F32).astype(BF16)
    high_rows = (iota((2 * stack, 128), 0) >> 1).astype(F32).astype(BF16)
    one, zero = jnp.ones((), BF16), jnp.zeros((), BF16)
    counts = jnp.zeros((2 * stack, HALF), F32)

    def split_code(ch, part):
        code = recv_ref[ch, 4 + part : 5 + part, :]
        order = jnp.floor(code * (1.0 / NRAD))
        upper = order >= HALF
        return code - order * NRAD, jnp.where(upper, order - HALF, order), upper

    def modes_of(k):
        return jnp.concatenate([onehot_ref[k, q] for q in range(per // 128)], axis=1)

    for ch in range(chunks):
        for part in range(2):
            radius, low, upper = split_code(ch, part)
            high = jnp.where(upper, radius + NRAD, radius).astype(BF16)
            low = low.astype(BF16)
            picks = []
            for q in range(per // 128):
                at = slice(q * 128, (q + 1) * 128)
                onehot_ref[2 * ch + part, q] = jnp.where(low_rows == low[:, at], one, zero)
                picks.append(jnp.where(high_rows == high[:, at], one, zero))
            counts = counts + nt_dot(jnp.concatenate(picks, axis=1), modes_of(2 * ch + part))
    counts = jnp.concatenate([counts[:stack], counts[stack:]], axis=1)

    weight = (mics ** (-0.5)) * lax.rsqrt(1.0 + (iota((stack, ORDERS), 0) >> 1).astype(F32))
    counts_weight = counts * weight

    def scaled(column, x):
        return (column[None] * groups(x)).reshape(x.shape)

    def row_sums(x):
        return periodic(jnp.sum(jnp.sum(groups(x), axis=0), axis=1, keepdims=True))

    def adjoint(advance):
        out = jnp.zeros((2 * stack, ORDERS), F32)
        for ch in range(chunks):
            re, im = advance(ch, 0)[None], advance(ch, 1)[None]
            ec, es = groups(rad(ch, 0)), groups(rad(ch, 1))
            field_ref[ch, 0:stack] = (re * ec + im * es).reshape(stack, per).astype(BF16)
            field_ref[ch, stack:] = (im * ec - re * es).reshape(stack, per).astype(BF16)
            out = out + nt_dot(field_ref[ch], azim_ref[ch])
        re, im = out[:stack], out[stack:]
        rc, rs, ic, ics = re[:, :HALF], re[:, HALF:], im[:, :HALF], im[:, HALF:]
        g_re = jnp.concatenate([rc + ics, rc - ics], axis=1) * weight
        g_im = jnp.concatenate([ic - rs, ic + rs], axis=1) * weight
        return g_re, g_im, row_sums(counts * (g_re * g_re + g_im * g_im))

    def forward():
        x_re, x_im = dir_ref[0] * counts_weight, dir_ref[1] * counts_weight
        p_re, m_re, p_im, m_im = x_re[:, :HALF], x_re[:, HALF:], x_im[:, :HALF], x_im[:, HALF:]
        rows_ref[0:stack] = jnp.concatenate([p_re + m_re, m_im - p_im], axis=1).astype(BF16)
        rows_ref[stack:] = jnp.concatenate([p_im + m_im, p_re - m_re], axis=1).astype(BF16)
        norm = jnp.zeros((8, per), F32)
        for ch in range(chunks):
            out = jnp.dot(rows_ref[...], azim_ref[ch], preferred_element_type=F32)
            t_re, t_im = out[:stack], out[stack:]
            ec, es = rad(ch, 0), rad(ch, 1)
            i_re = periodic(jnp.sum(groups(ec * t_re - es * t_im), axis=0))
            i_im = periodic(jnp.sum(groups(ec * t_im + es * t_re), axis=0))
            image_ref[ch, 0] = i_re
            image_ref[ch, 1] = i_im
            norm = norm + (i_re * i_re + i_im * i_im)
        return jnp.sum(norm, axis=1, keepdims=True)

    g_re, g_im, norm = adjoint(lambda ch, c: res_ref[ch, c])
    dir_ref[0] = g_re
    dir_ref[1] = g_im
    for sweep in range(ITERS):
        step = norm / (forward() + EPS)

        def advance(ch, c, step=step):
            value = res_ref[ch, c] - step * image_ref[ch, c]
            res_ref[ch, c] = value
            return value

        for c in range(2):
            grown = scaled(step, dir_ref[c])
            grown_ref[c] = grown if sweep == 0 else grown_ref[c] + grown
        if sweep + 1 < ITERS:
            g_re, g_im, next_norm = adjoint(advance)
            momentum = next_norm / (norm + EPS)
            dir_ref[0] = g_re + scaled(momentum, dir_ref[0])
            dir_ref[1] = g_im + scaled(momentum, dir_ref[1])
            norm = next_norm

    copies, _, lines, _, _ = out_ref.shape
    width = mics // copies
    even = (iota((8, per), 0) & 1) == 0
    upper = (iota((8, per), 0) & 2) == 0
    first = iota((8, 128), 0) < 2
    for ch in range(chunks):
        re, im = advance(ch, 0), advance(ch, 1)
        sides = [jnp.where(even, re, pltpu.roll(im, 1, 0)), jnp.where(even, pltpu.roll(re, 7, 0), im)]
        for piece in range(per // width):
            for fl in range(2):
                left = sides[fl][:, piece * width : piece * width + 128]
                right = sides[fl][:, piece * width + 128 : (piece + 1) * width]
                packed = jnp.where(first, left, right)[0:4].astype(BF16)
                for owner in range(fl * chunks // 2, (fl + 1) * chunks // 2):
                    out_ref[ch * (per // width) + piece, owner, lines - 1] = packed

    for c in range(2):
        for half in range(2):
            begin = (2 * c + half) * stack
            pick_ref[begin : begin + stack] = grown_ref[c, :, half * HALF : (half + 1) * HALF].astype(BF16)
    radial_rows = (iota((stack, per), 0) >> 1).astype(F32)
    first = iota((8, 128), 0) < 4
    for ch in range(chunks):
        tiles = []
        for part in range(2):
            radius, _, minus = split_code(ch, part)
            picked = jnp.dot(pick_ref[...], modes_of(2 * ch + part), preferred_element_type=F32)
            mask = radial_rows == radius
            sides = []
            for c in range(2):
                plus_rows = picked[2 * c * stack : (2 * c + 1) * stack]
                minus_rows = picked[(2 * c + 1) * stack : (2 * c + 2) * stack]
                side = jnp.where(mask, jnp.where(minus, minus_rows, plus_rows), 0.0)
                sides.append(periodic(jnp.sum(groups(side), axis=0)))
            re, im = sides
            value = jnp.where(upper, re, im)
            for q in range(0, per // 128, 2):
                tiles.append(jnp.where(first, value[:, q * 128 : (q + 1) * 128], value[:, (q + 1) * 128 : (q + 2) * 128]))
        for k, tile in enumerate(tiles):
            for half in range(2):
                packed = tile[4 * half : 4 * half + 4].astype(BF16)
                for copy in range(copies):
                    out_ref[copy, ch, 2 * k + half] = packed


def solve_call(recv, azim, early, seeds, copies):
    chunks, _, per = recv.shape
    modes, stack = 2 * chunks * per, 2 * NRAD
    return pl.pallas_call(
        solve_kernel,
        in_specs=[VMEM] * 4,
        out_specs=VMEM,
        out_shape=jax.ShapeDtypeStruct((copies, chunks, modes // chunks // 128 + 1, 4, 128), BF16),
        scratch_shapes=[
            pltpu.VMEM((chunks - 3 * chunks // 8, 2, stack, per), F32),
            pltpu.VMEM((chunks, 2, 8, per), F32),
            pltpu.VMEM((chunks, 2, 8, per), F32),
            pltpu.VMEM((chunks, 2 * stack, per), BF16),
            pltpu.VMEM((2 * chunks, per // 128, HALF, 128), BF16),
            pltpu.VMEM((2, stack, ORDERS), F32),
            pltpu.VMEM((2, stack, ORDERS), F32),
            pltpu.VMEM((2 * stack, ORDERS), BF16),
            pltpu.VMEM((4 * stack, HALF), BF16),
        ],
        compiler_params=pltpu.CompilerParams(vmem_limit_bytes=14 << 20),
        name="solve",
        cost_estimate=pl.CostEstimate(flops=10 * 256 * 4096 * 128, bytes_accessed=8 << 20, transcendentals=0),
    )(recv, azim, early, seeds)


def expand_kernel(in_ref, amp_hbm, pow_hbm, res_hbm, wide_ref, ready_ref, pow_ref, res_ref, sems):
    segs, dests, lines, rows, _ = in_ref.shape
    lines = lines - 1
    owner = lax.rem(2 * lax.axis_index("mode"), dests)
    for f in range(2):
        for s in range(segs):
            wide_ref[3, f, 8 * s : 8 * s + rows, :] = in_ref[s, owner + f, lines].astype(F32)
        for half in range(2):
            for c in range(2):
                value = wide_ref[3, f, pl.ds(2 * half + c, segs, stride=8), :]
                res_ref[2 * f + c, :, half * 128 : (half + 1) * 128] = value
    copies = [pltpu.make_async_copy(res_ref, res_hbm, sems.at[2 * dests])]
    copies[-1].start()
    for d in range(dests):
        for s in range(segs):
            for kc in range(lines):
                begin = 8 * s + rows * (kc % 2)
                wide_ref[d % 4, kc // 2, begin : begin + rows, :] = in_ref[s, d, kc].astype(F32)
        for kc in range(lines):
            at = slice(kc * 128, (kc + 1) * 128)
            for fl in range(rows // 2):
                power = jnp.zeros((segs, 128), F32)
                for c in range(2):
                    value = wide_ref[d % 4, kc // 2, pl.ds(rows * (kc % 2) + 2 * c + fl, segs, stride=8), :]
                    ready_ref[d, fl, c, :, at] = value
                    power = power + value * value
                f = d + fl * dests
                pow_ref[f : f + 1, at] = jnp.sum(power, axis=0, keepdims=True) * (1.0 / segs)
        for fl in range(rows // 2):
            f = d + fl * dests
            copies.append(pltpu.make_async_copy(ready_ref.at[d, fl], amp_hbm.at[pl.ds(2 * f, 2)], sems.at[2 * d + fl]))
            copies[-1].start()
    copies.append(pltpu.make_async_copy(pow_ref, pow_hbm, sems.at[2 * dests + 1]))
    copies[-1].start()
    for copy in copies:
        copy.wait()


def expand_call(recv):
    segs, dests, lines, rows, _ = recv.shape
    modes = (lines - 1) * 128
    return pl.pallas_call(
        expand_kernel,
        in_specs=[VMEM],
        out_specs=[HBM] * 3,
        out_shape=[
            jax.ShapeDtypeStruct((dests * rows, segs, modes), F32),
            jax.ShapeDtypeStruct((dests * rows // 2, modes), F32),
            jax.ShapeDtypeStruct((rows, segs, 256), F32),
        ],
        scratch_shapes=[
            pltpu.VMEM((4, (lines - 1) // 2, 8 * segs, 128), F32),
            pltpu.VMEM((dests, rows // 2, 2, segs, modes), F32),
            pltpu.VMEM((dests * rows // 2, modes), F32),
            pltpu.VMEM((rows, segs, 256), F32),
            pltpu.SemaphoreType.DMA((2 * dests + 2,)),
        ],
        compiler_params=pltpu.CompilerParams(vmem_limit_bytes=12 << 20),
        name="expand",
        cost_estimate=pl.CostEstimate(flops=1 << 21, bytes_accessed=3 << 20, transcendentals=0),
    )(recv)


def on_device(signal, mic_axial, mic_azimuth, mode_m, mode_n, freq_bins):
    segs = lax.axis_size("mic")
    owners = lax.axis_size("mode")
    freqs = freq_bins.shape[0]
    own = freqs // owners
    codes = lax.all_to_all(codes_call(mic_azimuth, mic_axial, segs), "mic", 0, 0, tiled=True)
    spectra = spectra_call(freq_bins, mode_m, mode_n, signal[0], owners)
    recv = lax.all_to_all(spectra, "mode", 0, 0, tiled=True)
    azim, early, seeds = basis_call(freq_bins, codes, owners)
    slots = solve_call(recv, azim, early, seeds, segs)
    shape = slots.shape
    slots = lax.all_to_all(slots.reshape(segs * owners, *shape[2:]), ("mic", "mode"), 0, 0, tiled=True)
    amplitude, power, residual = expand_call(slots.reshape(shape))
    modes = mode_m.shape[0]
    return (
        amplitude.reshape(freqs, 2, segs, modes),
        power,
        residual.reshape(own, 2, segs, residual.shape[2]),
    )


def solution(mesh):
    in_specs = (P("mic", "mode", None), P("mic"), P("mic"), P("mode"), P("mode"), P())
    out_specs = (P(None, None, None, "mode"), P(None, "mode"), P("mode", None, None, "mic"))
    return jax.shard_map(
        on_device, mesh=mesh, in_specs=in_specs, out_specs=out_specs, check_vma=False
    )
```
